32 devices in a mesh: lon: 8 (over y, x, core), lat: 2 (over z_hi), lev: 2 (over z_lo).
Axes of the slice: x: 2, y: 2, z: 4 (z_hi: 2, z_lo: 2; z = z_hi * 2 + z_lo), core: 2. Of those that a mesh axis runs over, the one named last changes fastest.
Arguments:
- tokens: bfloat16 [4, 12, 96, 768], P('lev', 'lat', 'lon'), may hold values from -6 to 6
- packed_weight: bfloat16 [768, 2304], replicated, may hold values from -0.21875 to 0.21875
- output_weight: bfloat16 [768, 768], replicated, may hold values from -0.21875 to 0.21875
- norm_gain: float32 [768], replicated, may hold values from 0.25 to 1.75
- merge_gain: float32 [3072], replicated, may hold values from 0.25 to 1.75
- bias_table: float32 [2, 2, 24, 3312], P('lev', 'lat'), may hold values from -4 to 304
- bias_index: int32 [144, 144], replicated, may hold values from 0 to 3311
- row_labels: int32 [12], P('lat'), may hold values from 0 to 9, as said below
- column_valid: int32 [96], replicated, may hold values 0 or 1
- merged_grad: bfloat16 [4, 6, 48, 3072], P(None, 'lat', ('lon', 'lev')), may hold values from -6 to 6
Outputs:
- merged: bfloat16 [4, 6, 48, 3072], P(None, 'lat', ('lon', 'lev'))
- grad_tokens: bfloat16 [4, 12, 96, 768], P('lev', 'lat', 'lon')
The draws below stay inside these ranges and needn't reach their ends.
Inputs may be any that keep to these rules, and one draw needn't show every extreme that they name: `row_labels`: labels never fall from one row to the next; the last 3 rows share a label that no other row has.
All inputs are finite; a program needn't handle non-finite values.
Results may differ from the reference program's by a relative error of at most 0.012.
Values may be sent and summed in bfloat16 or wider, within the bound.
No kernel may reach another device: no remote copies, remote signals or barrier semaphores. Data moves between devices by JAX's collectives and lax.ppermute only.
A program may use at most 64 MiB of HBM per device.

```python
import jax
import jax.numpy as jnp
from jax import lax

D = 768
HEADS = 24
HEAD = 32
WLAT = 6
WLON = 12
LEV_DEV = 2
NLEV = 4
NLAT = 12
NLON = 96
NWLEV = 2
NWLAT = 2
WIN = 144
BIAS_ROWS = 3312
CLAT = 6
CLON = 48


def draw_bias_table(key, part):
    shape = (NWLEV, NWLAT, HEADS, BIAS_ROWS)
    first_key = jax.random.fold_in(key, 0)
    return jnp.clip(jax.random.normal(first_key, shape, jnp.float32), -4.0, 4.0)


def draw_row_labels(key, part):
    positions = jnp.arange(NLAT, dtype=jnp.int32)
    marks = jax.random.randint(key, (NLAT,), 0, 4) == 0
    tail = positions >= NLAT - WLAT
    forced = (positions == NLAT - WLAT) | (positions == NLAT - WLAT // 2)
    marks = jnp.where(tail, forced, marks) | (positions == 0)
    starts = jnp.where(marks, positions, 0)
    return lax.cummax(starts).astype(jnp.int32)


def plant(array, rng, smallest, high):
    shape = array.shape
    spot = [jax.random.randint(jax.random.fold_in(rng, axis), (), 0, shape[axis]) for axis in range(len(shape))]
    array = array.at[tuple(spot)].set(smallest)
    longest = shape.index(max(shape))
    spot[longest] = (spot[longest] + 1) % shape[longest]
    return array.at[tuple(spot)].set(high)


def block_scale(stream_key, shape, pieces, least, largest):
    loudness = 1.0
    for dim, shards_of in pieces:
        steps = jax.random.uniform(jax.random.fold_in(jax.random.fold_in(stream_key, 6), dim), (shards_of,), jnp.float32, least / len(pieces), largest / len(pieces))
        loudness = loudness * jnp.repeat(jnp.exp(steps), shape[dim] // shards_of).reshape((-1,) + (1,) * (len(shape) - 1 - dim))
    return loudness


def scatter_about(stream_key, extent, deviation, most, shards=(), held_as=jnp.bfloat16):
    loudness = block_scale(stream_key, extent, shards, -0.22, 0.18) if shards else 1.0
    entries = jax.random.normal(stream_key, extent, jnp.float32) * deviation * loudness
    return jnp.minimum(jnp.maximum(entries, -most), most).astype(held_as)


def setup_inputs(seed: int = 0) -> dict:
    key_of = jax.random.split(jax.random.key(seed), 11)
    return {
        "tokens": scatter_about(key_of[0], (NLEV, NLAT, NLON, D), 1.0, 6.0, ((0, 2), (1, 2), (2, 8))),
        "packed_weight": scatter_about(key_of[1], (D, 3 * D), D ** -0.5, 0.21875),
        "output_weight": scatter_about(key_of[2], (D, D), D ** -0.5, 0.21875),
        "norm_gain": jnp.clip(1.0 + 0.15 * jax.random.normal(key_of[3], (D,), jnp.float32), 0.25, 1.75),
        "merge_gain": jnp.clip(1.0 + 0.15 * jax.random.normal(key_of[4], (4 * D,), jnp.float32), 0.25, 1.75),
        "bias_table": draw_bias_table(jax.random.fold_in(key_of[10], 71), 0),
        "bias_index": plant(jax.random.randint(key_of[6], (WIN, WIN), 0, BIAS_ROWS), jax.random.fold_in(key_of[6], 1), 0, BIAS_ROWS - 1).astype(jnp.int32),
        "row_labels": draw_row_labels(jax.random.fold_in(key_of[10], 71), 0),
        "column_valid": plant((jax.random.randint(key_of[8], (NLON,), 0, 8) < 7).astype(jnp.int32), jax.random.fold_in(key_of[8], 1), 0, 1),
        "merged_grad": scatter_about(key_of[9], (NLEV, CLAT, CLON, 4 * D), 1.0, 6.0, ((1, 2), (2, 16))),
    }


epsilon = 1e-05

def norm_rows(values, gain):
    data = values.astype(jnp.float32)
    center = data - lax.optimization_barrier(jnp.mean(data, axis=-1, keepdims=True))
    scale = lax.rsqrt(lax.optimization_barrier(jnp.mean(center * center, axis=-1, keepdims=True)) + epsilon)
    unit = center * scale
    return ((unit * gain).astype(jnp.bfloat16), unit, scale)

def norm_back(grad, gain, unit, scale):
    scaled = grad.astype(jnp.float32) * gain
    return scale * (scaled - lax.optimization_barrier(jnp.mean(scaled, axis=-1, keepdims=True)) - unit * lax.optimization_barrier(jnp.mean(scaled * unit, axis=-1, keepdims=True)))

def project(values, weight):
    flat = values.reshape(-1, values.shape[-1])
    product = jnp.dot(flat, weight, preferred_element_type=jnp.float32)
    return product.astype(jnp.bfloat16).reshape(values.shape[:-1] + (weight.shape[1],))

def project_back(values, weight):
    flat = values.reshape(-1, values.shape[-1])
    product = lax.dot_general(flat, weight, (((1,), (1,)), ((), ())), preferred_element_type=jnp.float32)
    return product.astype(jnp.bfloat16).reshape(values.shape[:-1] + (weight.shape[0],))

def to_windows(grid):
    levels, lines, columns, width = grid.shape
    parts = grid.reshape(levels, lines // WLAT, WLAT, columns // WLON, WLON, width)
    parts = parts.transpose(1, 3, 0, 2, 4, 5)
    return parts.reshape(-1, levels * WLAT * WLON, width)

def from_windows(blocks, levels, lines, columns):
    width = blocks.shape[-1]
    parts = blocks.reshape(lines // WLAT, columns // WLON, levels, WLAT, WLON, width)
    return parts.transpose(2, 0, 3, 1, 4, 5).reshape(levels, lines, columns, width)

def window_masks(labels, valid, levels):
    lines, columns = (labels.shape[0], valid.shape[0])
    window = levels * WLAT * WLON
    label_grid = jnp.broadcast_to(labels.reshape(lines // WLAT, 1, WLAT, 1), (lines // WLAT, levels, WLAT, WLON)).reshape(lines // WLAT, 1, window)
    valid_grid = jnp.broadcast_to(valid.reshape(columns // WLON, 1, 1, WLON), (columns // WLON, levels, WLAT, WLON)).reshape(1, columns // WLON, window)
    same = label_grid[:, :, :, None] == label_grid[:, :, None, :]
    keep = (valid_grid[:, :, None, :] > 0) | jnp.eye(window, dtype=bool)
    return (same & keep).reshape(-1, window, window)

def merge_cells(grid):
    levels, lines, columns, width = grid.shape
    parts = grid.reshape(levels, lines // 2, 2, columns // 2, 2, width).transpose(0, 1, 3, 4, 2, 5)
    return parts.reshape(levels, lines // 2, columns // 2, 4 * width)

def split_cells(cells):
    levels, lines, columns, width = cells.shape
    parts = cells.reshape(levels, lines, columns, 2, 2, width // 4).transpose(0, 1, 4, 2, 3, 5)
    return parts.reshape(levels, lines * 2, columns * 2, width // 4)

def attend(triple, typed, allowed):
    count, window = (triple.shape[0], triple.shape[1])
    parts = triple.reshape(count, window, 3, HEADS, HEAD)
    query, key, value = (parts[:, :, 0], parts[:, :, 1], parts[:, :, 2])
    scores = jnp.einsum('wqhd,wkhd->whqk', query.astype(jnp.float32), key.astype(jnp.float32)) * HEAD ** (-0.5)
    scores = (scores.reshape((typed.shape[0], -1) + scores.shape[1:]) + typed[:, None]).reshape(scores.shape)
    scores = jnp.where(allowed[:, None], scores, -jnp.inf)
    peak = lax.optimization_barrier(jnp.max(scores, axis=-1, keepdims=True))
    raised = jnp.exp(scores - peak)
    weights = raised / lax.optimization_barrier(jnp.sum(raised, axis=-1, keepdims=True))
    rounded = weights.astype(jnp.bfloat16)
    heads = jnp.einsum('whqk,wkhd->wqhd', rounded.astype(jnp.float32), value.astype(jnp.float32))
    heads = heads.astype(jnp.bfloat16).reshape(count, window, HEADS * HEAD)
    return (heads, (query, key, value, weights, rounded))

def attend_back(grad_heads, saved):
    query, key, value, weights, rounded = saved
    count, window = (query.shape[0], query.shape[1])
    grad_split = grad_heads.reshape(count, window, HEADS, HEAD).astype(jnp.float32)
    grad_weights = jnp.einsum('wqhd,wkhd->whqk', grad_split, value.astype(jnp.float32))
    grad_values = jnp.einsum('whqk,wqhd->wkhd', rounded.astype(jnp.float32), grad_split).astype(jnp.bfloat16)
    grad_scores = weights * (grad_weights - lax.optimization_barrier(jnp.sum(weights * grad_weights, axis=-1, keepdims=True)))
    grad_scores = (grad_scores * HEAD ** (-0.5)).astype(jnp.bfloat16).astype(jnp.float32)
    grad_queries = jnp.einsum('whqk,wkhd->wqhd', grad_scores, key.astype(jnp.float32)).astype(jnp.bfloat16)
    grad_keys = jnp.einsum('whqk,wqhd->wkhd', grad_scores, query.astype(jnp.float32)).astype(jnp.bfloat16)
    stacked = jnp.stack((grad_queries, grad_keys, grad_values), axis=2)
    return stacked.reshape(count, window, 3 * HEADS * HEAD)

def reference(tokens, packed_weight, output_weight, norm_gain, merge_gain, bias_table, bias_index, row_labels, column_valid, merged_grad):
    half_lines, half_columns = (WLAT // 2, WLON // 2)
    normed, unit_one, scale_one = norm_rows(tokens, norm_gain)
    rolled = jnp.roll(normed, (-half_lines, -half_columns), axis=(1, 2))
    valid = jnp.roll(column_valid, -half_columns)
    groups = NWLEV * NWLAT
    tables = bias_table.reshape(groups, 1, HEADS, BIAS_ROWS)
    labels = jnp.tile(row_labels.reshape(NWLAT, WLAT), (NWLEV, 1))

    def to_groups(grid):
        width = grid.shape[-1]
        parts = grid.reshape(NWLEV, LEV_DEV, NWLAT, WLAT, NLON, width).transpose(0, 2, 1, 3, 4, 5)
        return parts.reshape(groups, LEV_DEV, WLAT, NLON, width)

    def from_groups(stack):
        width = stack.shape[-1]
        parts = stack.reshape(NWLEV, NWLAT, LEV_DEV, WLAT, NLON, width).transpose(0, 2, 1, 3, 4, 5)
        return parts.reshape(NLEV, NLAT, NLON, width)

    def run_group(grid, table, label):
        allowed = window_masks(label, valid, LEV_DEV)
        typed = jnp.take(table, bias_index, axis=2)
        return attend(project(to_windows(grid), packed_weight), typed, allowed)

    def forward_group(item):
        grid, table, label = item
        heads, saved = run_group(grid, table, label)
        return from_windows(project(heads, output_weight), LEV_DEV, WLAT, NLON)
    attended = from_groups(lax.map(forward_group, (to_groups(rolled), tables, labels)))
    attended = jnp.roll(attended, (half_lines, half_columns), axis=(1, 2))
    residual = (tokens.astype(jnp.float32) + attended.astype(jnp.float32)).astype(jnp.bfloat16)
    merged, unit_two, scale_two = norm_rows(merge_cells(residual), merge_gain)
    grad_cells = norm_back(merged_grad, merge_gain, unit_two, scale_two).astype(jnp.bfloat16)
    grad_residual = split_cells(grad_cells)
    grad_rolled = jnp.roll(grad_residual, (-half_lines, -half_columns), axis=(1, 2))

    def backward_group(item):
        grid, table, label, grad_grid = item
        heads, saved = run_group(grid, table, label)
        grad_heads = project_back(to_windows(grad_grid), output_weight)
        grad_triple = attend_back(grad_heads, saved)
        return from_windows(project_back(grad_triple, packed_weight), LEV_DEV, WLAT, NLON)
    grad_inputs = from_groups(lax.map(backward_group, (to_groups(rolled), tables, labels, to_groups(grad_rolled))))
    grad_normed = jnp.roll(grad_inputs, (half_lines, half_columns), axis=(1, 2))
    grad_tokens = grad_residual.astype(jnp.float32) + norm_back(grad_normed, norm_gain, unit_one, scale_one)
    return (merged, grad_tokens.astype(jnp.bfloat16))
```

```python
import functools

import jax
import jax.numpy as jnp
import numpy as np
from jax import lax
from jax.experimental import pallas as pl
from jax.experimental.pallas import tpu as pltpu
from jax.sharding import PartitionSpec as P

HEADS = 24
HEAD = 32
WLAT = 6
WLON = 12
HALF_LAT = WLAT // 2
HALF_LON = WLON // 2
LEVELS = 2
WIN = LEVELS * WLAT * WLON
QUAD = WIN // 4
CELLS = LEVELS * HALF_LON // 2
GROUP = 128 // HEAD
TAIL = WIN - 128
TAIL_GROUPS = WIN // 8
PAD = 16
BLOCKED = -1e30

epsilon = 1e-05
f32 = jnp.float32
bf16 = jnp.bfloat16

NN = (((1,), (0,)), ((), ()))
NT = (((1,), (1,)), ((), ()))


def token_table():
    rows = []
    for quad in range(4):
        for r in range(HALF_LAT):
            for s in range(2):
                for l in range(LEVELS):
                    for j in range(HALF_LON // 2):
                        rows.append((quad, r, s, l, j))
    return np.array(rows)


TOKENS = token_table()
QUADS, ROW3, SIDE, LEVEL, PAIR = TOKENS.T
ROW = (QUADS & 1) * HALF_LAT + ROW3
COL = (QUADS >> 1) * HALF_LON + 2 * PAIR + SIDE
NATURAL = LEVEL * WLAT * WLON + ROW * WLON + COL
LINE = ROW3 + np.where(QUADS & 1, 0, HALF_LAT)
COLUMN = 2 * PAIR + SIDE + np.where(QUADS >> 1, 0, HALF_LON)
PLACE = (LEVEL * WLAT + LINE) * PAD + COLUMN
HALVES = (ROW == 0) | (ROW == WLAT - 1)


def one_hot(index, width):
    return (index[:, None] == np.arange(width)[None, :]).astype(np.float32)


def constants():
    order = one_hot(NATURAL, WIN)
    pack = one_hot(PLACE, LEVELS * WLAT * PAD)
    cell_row = np.where(ROW == 0, 0, (ROW + 1) // 2)
    cell = ((cell_row * 2 + (QUADS >> 1)) * LEVELS + LEVEL) * (HALF_LON // 2) + PAIR
    same = (cell[:, None] == cell[None, :]).astype(np.float32)
    first = [t for t in range(WIN) if ROW[t] == 0 and SIDE[t] == 0]
    last = [t for t in range(WIN) if ROW[t] == WLAT - 1 and SIDE[t] == 0]
    pick = one_hot(np.array(first + last), WIN)
    spread = same @ pick.T
    rows = np.stack((ROW, COL)).astype(np.int32)
    return order, pack, same, pick, spread, rows


ORDER, PACK, SAME, PICK, SPREAD, COORDS = constants()


def mxu(a, b, dims=NN):
    return lax.dot_general(a, b, dims, preferred_element_type=f32)


def exact(a, b):
    return lax.dot_general(a, b, NN, precision=lax.Precision.HIGHEST, preferred_element_type=f32)


def params(megabytes=48):
    return pltpu.CompilerParams(vmem_limit_bytes=megabytes << 20)


def shape(dims, dtype):
    return jax.ShapeDtypeStruct(dims, dtype)


def cost(flops, nbytes):
    return pl.CostEstimate(flops=flops, bytes_accessed=nbytes, transcendentals=0)


def lev_index():
    return lax.axis_index("lev")


def pack_kernel(tokens, grad, pack, own, lat, lon, both, same_here, other_here, same_next, other_next, padded, rows):
    width = tokens.shape[-1]
    for l in range(LEVELS):
        for r in range(WLAT):
            at = (l * WLAT + r) * PAD
            line = tokens[l, r].astype(f32)
            padded[at : at + PAD, :] = jnp.concatenate(
                (line, jnp.zeros((PAD - WLON, width), f32)), axis=0
            ).astype(bf16)
    for quad, out in enumerate((own, lat, lon, both)):
        out[...] = mxu(pack[quad], padded[...]).astype(bf16)
    me = lev_index()
    pairs = HALF_LON // 2
    for out, level, full, half, odd in (
        (same_here, me, 2, 1, 1),
        (other_here, 1 - me, 2, 1, 1),
        (same_next, me, 0, 1, 0),
        (other_next, 1 - me, 0, 1, 0),
    ):
        for l in range(LEVELS):
            at = slice(l * pairs, (l + 1) * pairs)
            halved = grad[level * LEVELS + l, half].astype(f32)
            for s in range(2):
                block = s * 2 + odd
                rows[at, s * width : (s + 1) * width] = halved[:, block * width : (block + 1) * width]
            rows[at, 2 * width :] = grad[level * LEVELS + l, full].astype(f32)
        out[...] = rows[...].astype(bf16)


def pack_pieces(tokens, grad):
    width = tokens.shape[-1]
    token_piece = shape((QUAD, width), bf16)
    cell_piece = shape((CELLS, 6 * width), bf16)
    return pl.pallas_call(
        pack_kernel,
        out_shape=[token_piece] * 4 + [cell_piece] * 4,
        scratch_shapes=[
            pltpu.VMEM((LEVELS * WLAT * PAD, width), bf16),
            pltpu.VMEM((CELLS, 6 * width), f32),
        ],
        compiler_params=params(),
        name="pack",
    )(tokens, grad, jnp.asarray(PACK.reshape(4, QUAD, -1), bf16))


def bias_kernel(table, index, order, coords, coords_t, labels, valid, main, tail, padded, high, low, mask, mask_t):
    heads, entries = table.shape[-2:]
    chunks = (entries + 127) // 128
    whole = entries // 128 * 128
    padded[:, :whole] = table[0, 0, :, :whole]
    if whole < entries:
        padded[:, whole:] = jnp.concatenate(
            (table[0, 0, :, whole:], jnp.zeros((heads, chunks * 128 - entries), f32)), axis=1
        )

    row_q, row_k = coords[0:1, :], coords_t[:, 0:1]
    col_k = coords_t[:, 1:2]
    label_q, label_k = jnp.zeros_like(row_q), jnp.zeros_like(row_k)
    for r in range(WLAT):
        label_q = jnp.where(row_q == r, labels[r], label_q)
        label_k = jnp.where(row_k == r, labels[r], label_k)
    valid_k = jnp.zeros_like(col_k)
    start = lax.axis_index("lon") * WLON + HALF_LON
    total = valid.shape[0]
    for c in range(WLON):
        at = start + c
        at = jnp.where(at >= total, at - total, at)
        valid_k = jnp.where(col_k == c, valid[at], valid_k)
    rows = lax.broadcasted_iota(jnp.int32, (WIN, WIN), 0)
    columns = lax.broadcasted_iota(jnp.int32, (WIN, WIN), 1)
    seen = (label_k == label_q) & ((valid_k > 0) | (rows == columns))
    added = jnp.where(seen, 0.0, BLOCKED).astype(f32)
    mask[...] = added[:, :128]
    mask_t[...] = jnp.concatenate((added[:, 128:], jnp.zeros((WIN, 128 - TAIL), f32)), axis=1)

    entry = index[...]
    permute = order[...]

    def place(values, out):
        moved = mxu(mxu(permute, values.astype(f32).astype(bf16), NT).astype(bf16), permute, NT)
        moved = moved.astype(jnp.int32)
        out[0:WIN, :] = moved[:, :128]
        rest = jnp.concatenate((moved[:, 128:], jnp.zeros((WIN, 128 - TAIL), jnp.int32)), axis=1)
        for first in range(0, TAIL_GROUPS, 8):
            total = None
            for g in range(first, min(first + 8, TAIL_GROUPS)):
                piece = rest[g * 8 : g * 8 + 8]
                if g > first:
                    piece = pltpu.roll(piece, TAIL * (g - first), 1)
                total = piece if total is None else total + piece
            out[WIN + first : WIN + first + 8, :] = total

    place(lax.shift_right_logical(entry, 7), high)
    place(entry & 127, low)

    def lookup(row):
        chunk = jnp.broadcast_to(high[pl.ds(row, 1), :], (8, 128))
        lane = jnp.broadcast_to(low[pl.ds(row, 1), :], (8, 128))
        found = [None] * (heads // 8)
        for c in range(chunks):
            here = chunk == c
            for block in range(heads // 8):
                source = padded[block * 8 : block * 8 + 8, c * 128 : (c + 1) * 128]
                value = jnp.take_along_axis(source, lane, axis=1, mode="promise_in_bounds")
                found[block] = value if c == 0 else jnp.where(here, value, found[block])
        return found

    def main_row(key, _):
        extra = jnp.broadcast_to(mask[pl.ds(key, 1), :], (8, 128))
        for block, value in enumerate(lookup(key)):
            main[pl.ds(block * 8 * WIN + key, 8, stride=WIN), :] = value + extra
        return 0

    lax.fori_loop(0, WIN, main_row, 0, unroll=2)
    for first in range(0, TAIL_GROUPS, 8):
        for s in range(8):
            for block, value in enumerate(lookup(WIN + first + s)):
                for g in range(first, min(first + 8, TAIL_GROUPS)):
                    key = g * 8 + s
                    moved = pltpu.roll(value, 128 - TAIL * (g - first), 1) if g > first else value
                    extra = jnp.broadcast_to(mask_t[key : key + 1, :], (8, 128))
                    tail[pl.ds(block * 8 * WIN + key, 8, stride=WIN), :] = moved + extra


def window_bias(table, index, labels, valid):
    heads, entries = table.shape[-2:]
    chunks = (entries + 127) // 128
    scalar = pl.BlockSpec(memory_space=pltpu.SMEM)
    vector = pl.BlockSpec(memory_space=pltpu.VMEM)
    index_rows = WIN + (TAIL_GROUPS + 7) // 8 * 8
    return pl.pallas_call(
        bias_kernel,
        out_shape=[shape((heads * WIN, 128), f32)] * 2,
        in_specs=[vector] * 5 + [scalar] * 2,
        scratch_shapes=[
            pltpu.VMEM((heads, chunks * 128), f32),
            pltpu.VMEM((index_rows, 128), jnp.int32),
            pltpu.VMEM((index_rows, 128), jnp.int32),
            pltpu.VMEM((WIN, 128), f32),
            pltpu.VMEM((WIN, 128), f32),
        ],
        compiler_params=params(),
        cost_estimate=cost(10**9, 2 * 10**7),
        name="bias",
    )(table, index, jnp.asarray(ORDER, bf16), jnp.asarray(COORDS), jnp.asarray(COORDS.T), labels, valid)


def row_mean(values):
    return jnp.mean(values, axis=-1, keepdims=True)


def unit_rows(data):
    center = data - row_mean(data)
    scale = lax.rsqrt(row_mean(center * center) + epsilon)
    return center * scale, scale


def stacked(block):
    lane = lax.broadcasted_iota(jnp.int32, (1, 128), 1) // HEAD
    return jnp.concatenate(
        [jnp.where(lane == h, block, jnp.zeros((), block.dtype)) for h in range(GROUP)], axis=0
    )


def lanes_of(parts):
    lane = lax.broadcasted_iota(jnp.int32, (1, 128), 1) // HEAD
    out = parts[0]
    for h in range(1, GROUP):
        out = jnp.where(lane == h, parts[h], out)
    return out


def forward_kernel(
    own, lat, lon, both, packed, output, gain, main, tail,
    weights, triple, keys_t, residual, tokens,
    gathered, values_t, heads_t,
):
    width = own.shape[-1]
    for quad, piece in enumerate((own, lat, lon, both)):
        gathered[quad * QUAD : (quad + 1) * QUAD, :] = piece[...].astype(f32)
    data = gathered[...]
    tokens[...] = data.astype(bf16)
    unit, _ = unit_rows(data)
    normed = (unit * gain[...]).astype(bf16)
    triple[...] = mxu(normed, packed[...]).astype(bf16)
    keys_t[...] = triple[:, width : 2 * width].astype(f32).T.astype(bf16)
    values_t[...] = triple[:, 2 * width :].astype(f32).T.astype(bf16)
    for g in range(width // 128):
        query = triple[:, g * 128 : (g + 1) * 128]
        key = triple[:, width + g * 128 : width + (g + 1) * 128]
        product = mxu(stacked(key), query, NT) * HEAD ** (-0.5)
        for h in range(GROUP):
            head = g * GROUP + h
            at = slice(head * WIN, (head + 1) * WIN)
            bias = jnp.concatenate((main[at, :], tail[at, :TAIL]), axis=1)
            scores = product[h * WIN : (h + 1) * WIN] + bias
            raised = jnp.exp(scores - jnp.max(scores, axis=0, keepdims=True))
            share = (raised * (1.0 / jnp.sum(raised, axis=0, keepdims=True))).astype(bf16)
            weights[at, :] = share
            here = slice(head * HEAD, (head + 1) * HEAD)
            heads_t[here, :] = mxu(values_t[here, :], share)
    heads = heads_t[...].T.astype(bf16)
    attended = mxu(heads, output[...]).astype(bf16)
    residual[...] = (data + attended.astype(f32)).astype(bf16)


def forward(pieces, packed, output, gain, main, tail):
    width = output.shape[0]
    return pl.pallas_call(
        forward_kernel,
        out_shape=[
            shape((HEADS * WIN, WIN), bf16),
            shape((WIN, 3 * width), bf16),
            shape((width, WIN), bf16),
            shape((WIN, width), bf16),
            shape((WIN, width), bf16),
        ],
        scratch_shapes=[
            pltpu.VMEM((WIN, width), f32),
            pltpu.VMEM((width, WIN), bf16),
            pltpu.VMEM((width, WIN), f32),
        ],
        compiler_params=params(),
        cost_estimate=cost(10**9, 2 * 10**7),
        name="forward",
    )(*pieces, packed, output, gain, main, tail)


def cell_blocks():
    out = []
    for quad in range(4):
        for r in range(HALF_LAT):
            odd = 1 - (r + (quad & 1) * HALF_LAT) % 2
            half = r == (HALF_LAT - 1 if quad & 1 else 0)
            for s in range(2):
                block = s * 2 + odd
                at = quad * QUAD + (r * 2 + s) * CELLS
                out.append((quad, at, block, s if half else 2 + block))
    return out


def columns_of(parts):
    lane = lax.broadcasted_iota(jnp.int32, (1, 128), 1)
    out = jnp.zeros((WIN, 128), f32)
    for i, part in enumerate(parts):
        out = jnp.where(lane == i, part, out)
    return out


def moments_kernel(
    residual, same_here, other_here, same_next, other_next, gain, same, pick, count,
    scaled, moments, sent,
):
    width = residual.shape[-1]
    second = lev_index() == 1
    sides = {}
    for kind, (near, far) in enumerate(((same_here, other_here), (same_next, other_next))):
        a, b = near[...].astype(f32), far[...].astype(f32)
        sides[kind] = jnp.where(second, a, b)
        sides[kind + 2] = jnp.where(second, b, a)
    for quad, at, block, lane in cell_blocks():
        part = sides[quad][:, lane * width : (lane + 1) * width]
        scaled[at : at + CELLS, :] = part * gain[:, block * width : (block + 1) * width]
    data = residual[...].astype(f32)
    grouping = same[...]
    inverse = count[...]
    total = jnp.sum(data, axis=-1, keepdims=True)
    middle = exact(grouping, jnp.broadcast_to(total, (WIN, 128)))[:, 0:1] * inverse
    center = data - middle
    grad = scaled[...]
    sums = columns_of((
        jnp.sum(center * center, axis=-1, keepdims=True),
        jnp.sum(grad, axis=-1, keepdims=True),
        jnp.sum(grad * center, axis=-1, keepdims=True),
    ))
    sums = exact(grouping, sums)
    lane = lax.broadcasted_iota(jnp.int32, (1, 128), 1)
    sums = jnp.where(lane == 3, middle, sums)
    moments[...] = sums
    sent[...] = exact(pick[...], sums)


def cell_moments(residual, cells, gain):
    width = residual.shape[-1]
    count = np.where(HALVES, 1 / (2 * width), 1 / (4 * width)).astype(np.float32)[:, None]
    return pl.pallas_call(
        moments_kernel,
        out_shape=[shape((WIN, width), f32), shape((WIN, 128), f32), shape((4 * CELLS, 128), f32)],
        compiler_params=params(),
        cost_estimate=cost(10**8, 10**6),
        name="moments",
    )(residual, *cells, gain, jnp.asarray(SAME), jnp.asarray(PICK), jnp.asarray(count))


def merge_kernel(
    residual, scaled, moments, before, after, gain, spread, halves,
    same_here, other_here, same_next, other_next, grad, unit,
):
    width = residual.shape[-1]
    second = lev_index() == 1
    there = jnp.concatenate((before[2 * CELLS :], after[: 2 * CELLS]), axis=0)
    theirs = exact(spread[...], there)
    mine = moments[...]
    shared = halves[...] > 0
    full = 4.0 * width
    middle = jnp.where(shared, 0.5 * (mine[:, 3:4] + theirs[:, 3:4]), mine[:, 3:4])
    gap = theirs[:, 3:4] - mine[:, 3:4]
    spread_sum = jnp.where(shared, mine[:, 0:1] + theirs[:, 0:1] + gap * gap * width, mine[:, 0:1])
    scale = lax.rsqrt(spread_sum / full + epsilon)
    grad_sum = jnp.where(shared, mine[:, 1:2] + theirs[:, 1:2], mine[:, 1:2])
    cross = jnp.where(
        shared,
        mine[:, 2:3] + (mine[:, 3:4] - middle) * mine[:, 1:2]
        + theirs[:, 2:3] + (theirs[:, 3:4] - middle) * theirs[:, 1:2],
        mine[:, 2:3],
    )
    normed = (residual[...].astype(f32) - middle) * scale
    unit[...] = normed
    grad[...] = (scale * (scaled[...] - grad_sum / full - normed * (cross * scale / full))).astype(bf16)
    for kind, (near, far) in enumerate(((same_here, other_here), (same_next, other_next))):
        for quad, at, block, lane in cell_blocks():
            if quad != kind:
                continue
            factor = gain[:, block * width : (block + 1) * width]
            left = unit[at : at + CELLS, :] * factor
            right = unit[at + 2 * QUAD : at + 2 * QUAD + CELLS, :] * factor
            here = slice(lane * width, (lane + 1) * width)
            near[:, here] = jnp.where(second, left, right).astype(bf16)
            far[:, here] = jnp.where(second, right, left).astype(bf16)


def merge_back(residual, scaled, moments, before, after, gain):
    width = residual.shape[-1]
    piece = shape((CELLS, 6 * width), bf16)
    return pl.pallas_call(
        merge_kernel,
        out_shape=[piece] * 4 + [shape((WIN, width), bf16)],
        scratch_shapes=[pltpu.VMEM((WIN, width), f32)],
        compiler_params=params(),
        cost_estimate=cost(10**8, 10**6),
        name="merge",
    )(
        residual, scaled, moments, before, after, gain, jnp.asarray(SPREAD),
        jnp.asarray(HALVES.astype(np.float32)[:, None]),
    )


def backward_kernel(
    grad, weights, triple, keys_t, tokens, packed, output, gain,
    own, lat, lon, both,
    joined, queries_t,
):
    width = grad.shape[-1]
    upstream = grad[...]
    grad_heads = mxu(upstream, output[...], NT).astype(bf16)
    for g in range(width // 128):
        here = slice(g * 128, (g + 1) * 128)
        query = triple[:, g * 128 : (g + 1) * 128]
        value = triple[:, 2 * width + g * 128 : 2 * width + (g + 1) * 128]
        arriving = grad_heads[:, here]
        product = mxu(stacked(value), arriving, NT)
        shares = weights[g * GROUP * WIN : (g + 1) * GROUP * WIN, :]
        grad_value = mxu(shares, arriving)
        slopes = []
        for h in range(GROUP):
            head = g * GROUP + h
            share = shares[h * WIN : (h + 1) * WIN].astype(f32)
            change = product[h * WIN : (h + 1) * WIN]
            level = jnp.sum(share * change, axis=0, keepdims=True)
            slope = (share * (change - level) * HEAD ** (-0.5)).astype(bf16)
            at = slice(head * HEAD, (head + 1) * HEAD)
            queries_t[at, :] = mxu(keys_t[at, :], slope)
            slopes.append(slope)
        grad_key = mxu(jnp.concatenate(slopes, axis=0), query)
        split = [slice(h * WIN, (h + 1) * WIN) for h in range(GROUP)]
        joined[:, width + g * 128 : width + (g + 1) * 128] = lanes_of([grad_key[s] for s in split]).astype(bf16)
        joined[:, 2 * width + g * 128 : 2 * width + (g + 1) * 128] = lanes_of(
            [grad_value[s] for s in split]
        ).astype(bf16)
    joined[:, :width] = queries_t[...].T.astype(bf16)
    grad_inputs = mxu(joined[...], packed[...], NT).astype(bf16)
    unit, scale = unit_rows(tokens[...].astype(f32))
    scaled = grad_inputs.astype(f32) * gain[...]
    out = upstream.astype(f32) + scale * (scaled - row_mean(scaled) - unit * row_mean(scaled * unit))
    for quad, piece in enumerate((own, lat, lon, both)):
        piece[...] = out[quad * QUAD : (quad + 1) * QUAD].astype(bf16)


def backward(grad, weights, triple, keys_t, tokens, packed, output, gain):
    width = grad.shape[-1]
    return pl.pallas_call(
        backward_kernel,
        out_shape=[shape((QUAD, width), bf16)] * 4,
        scratch_shapes=[pltpu.VMEM((WIN, 3 * width), bf16), pltpu.VMEM((width, WIN), f32)],
        compiler_params=params(),
        cost_estimate=cost(2 * 10**9, 2 * 10**7),
        name="backward",
    )(grad, weights, triple, keys_t, tokens, packed, output, gain)


def unpack_kernel(own, lat, lon, both, place, same_here, other_here, same_next, other_next, merged, tokens):
    width = own.shape[-1]
    total = None
    for quad, piece in enumerate((own, lat, lon, both)):
        part = mxu(place[quad], piece[...])
        total = part if total is None else total + part
    for l in range(LEVELS):
        for r in range(WLAT):
            at = (l * WLAT + r) * PAD
            tokens[l, r] = total[at : at + WLON].astype(bf16)
    me = lev_index()
    pairs = HALF_LON // 2
    for level, full, odd, piece in (
        (me, 2, 1, same_here),
        (1 - me, 2, 1, other_here),
        (me, 0, 0, same_next),
        (1 - me, 0, 0, other_next),
    ):
        cells = piece[...].astype(f32)
        for l in range(LEVELS):
            part = cells[l * pairs : (l + 1) * pairs].astype(bf16)
            for s in range(2):
                block = s * 2 + odd
                merged[level * LEVELS + l, 1, :, block * width : (block + 1) * width] = part[
                    :, s * width : (s + 1) * width
                ]
            merged[level * LEVELS + l, full] = part[:, 2 * width :]


def unpack_pieces(token_pieces, cell_pieces):
    width = token_pieces[0].shape[-1]
    place = np.transpose(PACK.reshape(4, QUAD, -1), (0, 2, 1))
    return pl.pallas_call(
        unpack_kernel,
        out_shape=[
            shape((2 * LEVELS, HALF_LAT, HALF_LON // 2, 4 * width), bf16),
            shape((LEVELS, WLAT, WLON, width), bf16),
        ],
        compiler_params=params(),
        name="unpack",
    )(*token_pieces, jnp.asarray(place, bf16), *cell_pieces)


def routes(sizes, target):
    lons, lats, levs = sizes

    def number(i, a, k):
        return ((i % lons) * lats + a % lats) * levs + k % levs

    return [
        (number(i, a, k), number(*target(i, a, k)))
        for i in range(lons)
        for a in range(lats)
        for k in range(levs)
    ]


def send(block, sizes, target, back=False):
    pairs = routes(sizes, target)
    if back:
        pairs = [(b, a) for a, b in pairs]
    return lax.ppermute(block, ("lon", "lat", "lev"), pairs)


TOKEN_TARGETS = (
    lambda i, a, k: (i, a - 1, k),
    lambda i, a, k: (i - 1, a, k),
    lambda i, a, k: (i - 1, a - 1, k),
)
CELL_TARGETS = (
    lambda i, a, k: (i - (1 - k), a, k),
    lambda i, a, k: (i - (1 - k), a, 1 - k),
    lambda i, a, k: (i - (1 - k), a - 1, k),
    lambda i, a, k: (i - (1 - k), a - 1, 1 - k),
)


def per_device(
    sizes,
    tokens,
    packed_weight,
    output_weight,
    norm_gain,
    merge_gain,
    bias_table,
    bias_index,
    row_labels,
    column_valid,
    merged_grad,
):
    own, *rest = pack_pieces(tokens, merged_grad)
    pieces = [own] + [send(x, sizes, t) for x, t in zip(rest[:3], TOKEN_TARGETS)]
    cells = [send(x, sizes, t) for x, t in zip(rest[3:], CELL_TARGETS)]
    main, tail = window_bias(bias_table, bias_index, row_labels, column_valid)
    gain = norm_gain.reshape(1, -1)
    cell_gain = merge_gain.reshape(1, -1)
    weights, triple, keys_t, residual, data = forward(pieces, packed_weight, output_weight, gain, main, tail)
    scaled, moments, sent = cell_moments(residual, cells, cell_gain)
    before = send(sent, sizes, lambda i, a, k: (i, a + 1, k))
    after = before if sizes[1] == 2 else send(sent, sizes, lambda i, a, k: (i, a - 1, k))
    *merged, grad = merge_back(residual, scaled, moments, before, after, cell_gain)
    merged = [send(x, sizes, t, True) for x, t in zip(merged, CELL_TARGETS)]
    own, *rest = backward(grad, weights, triple, keys_t, data, packed_weight, output_weight, gain)
    grads = [own] + [send(x, sizes, t, True) for x, t in zip(rest, TOKEN_TARGETS)]
    return unpack_pieces(grads, merged)


def solution(mesh):
    sizes = tuple(mesh.shape[name] for name in ("lon", "lat", "lev"))
    placed = (
        P("lev", "lat", "lon", None),
        P(),
        P(),
        P(),
        P(),
        P("lev", "lat", None, None),
        P(),
        P("lat"),
        P(),
        P(None, "lat", ("lon", "lev"), None),
    )
    return jax.shard_map(
        functools.partial(per_device, sizes),
        mesh=mesh,
        in_specs=placed,
        out_specs=(P(None, "lat", ("lon", "lev"), None), P("lev", "lat", "lon", None)),
        check_vma=False,
    )
```

```python
import functools

import jax
import jax.numpy as jnp
from jax import lax
from jax.experimental import pallas as pl
from jax.experimental.pallas import tpu as pltpu
from jax.sharding import PartitionSpec as P

HEADS = 24
HEAD = 32
WLAT = 6
WLON = 12
HALF_LAT = WLAT // 2
HALF_LON = WLON // 2
LEVELS = 2
WIN = LEVELS * WLAT * WLON
QUAD = WIN // 4
PAIRS = HALF_LON // 2
CELLS = LEVELS * PAIRS
GROUP = 128 // HEAD
TAIL = WIN - 128
TAIL_GROUPS = WIN // 8
BLOCKED = -1e30

epsilon = 1e-05
f32 = jnp.float32
bf16 = jnp.bfloat16

NN = (((1,), (0,)), ((), ()))
NT = (((1,), (1,)), ((), ()))


def token_row(quad, row, side, pair):
    return quad * QUAD + ((row * 2 + side) * PAIRS + pair) * LEVELS


def split_tokens(t):
    def digit(rest, size, count):
        found = jnp.zeros_like(rest)
        for i in range(1, count):
            found = found + (rest >= i * size).astype(jnp.int32)
        return found, rest - found * size

    quad, rest = digit(t, QUAD, 4)
    row, rest = digit(rest, 2 * CELLS, HALF_LAT)
    side, rest = digit(rest, CELLS, 2)
    pair, level = digit(rest, LEVELS, PAIRS)
    right, below = digit(quad, 2, 2)
    row = row + HALF_LAT * below
    column = right * HALF_LON + 2 * pair + side
    return row, column, level, right


def token_places(dims, axis):
    return split_tokens(lax.broadcasted_iota(jnp.int32, dims, axis))


def mxu(a, b, dims=NN):
    return lax.dot_general(a, b, dims, preferred_element_type=f32)


def exact(a, b):
    return lax.dot_general(a, b, NN, precision=lax.Precision.HIGHEST, preferred_element_type=f32)


def params(megabytes=12):
    return pltpu.CompilerParams(vmem_limit_bytes=megabytes << 20)


def shape(dims, dtype):
    return jax.ShapeDtypeStruct(dims, dtype)


def cost(flops, nbytes):
    return pl.CostEstimate(flops=flops, bytes_accessed=nbytes, transcendentals=0)


def lev_index():
    return lax.axis_index("lev")


def quadrant(values, quad):
    return values[quad * QUAD : (quad + 1) * QUAD]


def cell_places():
    return [(0, 0, True, 0), (0, 1, True, 1), (1, 0, True, 2), (1, 1, False, 0), (2, 0, False, 1), (2, 1, False, 2)]


def pack_kernel(tokens, grad, own, first, second, third, kept, fourth, fifth, rows, cells):
    width = tokens.shape[-1]
    for line in range(WLAT):
        for column in range(WLON):
            quad = (0 if line >= HALF_LAT else 1) + (0 if column >= HALF_LON else 2)
            inner = column % HALF_LON
            at = token_row(quad, line % HALF_LAT, inner % 2, inner // 2)
            rows[at : at + LEVELS, :] = tokens[line, column].astype(f32)
    upper = lax.axis_index("lev") == 1
    for row, odd, below, inner in cell_places():
        for pair in range(PAIRS):
            for side in range(2):
                block = side * 2 + odd
                part = grad[row, pair, :, block * width : (block + 1) * width].astype(f32)
                low, high = part[:LEVELS], part[LEVELS:]
                at = token_row(int(below), inner, side, pair)
                cells[at : at + LEVELS, :] = jnp.where(upper, high, low)
                at = at + 2 * QUAD
                cells[at : at + LEVELS, :] = jnp.where(upper, low, high)
    data, grads = rows[...], cells[...]
    lat, lon, both = quadrant(data, 1), quadrant(data, 2), quadrant(data, 3)
    here, below = quadrant(grads, 0), quadrant(grads, 1)
    own[...] = quadrant(data, 0).astype(bf16)
    first[...] = jnp.concatenate((jnp.where(upper, lat, both), below), axis=0).astype(bf16)
    second[...] = jnp.where(upper, both, lat).astype(bf16)
    third[...] = jnp.concatenate((lon, here), axis=0).astype(bf16)
    kept[...] = here.astype(bf16)
    fourth[...] = quadrant(grads, 2).astype(bf16)
    fifth[...] = quadrant(grads, 3).astype(bf16)


def pack_pieces(tokens, grad):
    width = tokens.shape[-1]
    piece, double = shape((QUAD, width), bf16), shape((2 * QUAD, width), bf16)
    return pl.pallas_call(
        pack_kernel,
        out_shape=[piece, double, piece, double, piece, piece, piece],
        scratch_shapes=[pltpu.VMEM((WIN, width), f32)] * 2,
        compiler_params=params(),
        name="pack",
    )(tokens, grad)


def bias_kernel(
    table_at, index_at, labels_at, valid_at, main, tail,
    table, index, labels, valid, split, fine, high, low, fine_high, fine_low, rest_rows, mask, mask_tail, done,
):
    copies = [
        pltpu.make_async_copy(source, target, done.at[i])
        for i, (source, target) in enumerate(
            ((table_at.at[0, 0], table), (index_at, index), (labels_at, labels), (valid_at, valid))
        )
    ]
    for copy in copies:
        copy.start()
    row_k, column_k, level_k, _ = token_places((WIN, 1), 0)
    row_q, _, _, _ = token_places((1, WIN), 1)
    natural = (level_k * WLAT + row_k) * WLON + column_k
    columns = lax.broadcasted_iota(jnp.int32, (WIN, WIN), 1)
    rows = lax.broadcasted_iota(jnp.int32, (WIN, WIN), 0)
    permute = jnp.where(natural == columns, 1.0, 0.0).astype(bf16)
    for copy in copies:
        copy.wait()

    label_q, label_k = jnp.zeros_like(row_q), jnp.zeros_like(row_k)
    for r in range(WLAT):
        label_q = jnp.where(row_q == r, labels[r], label_q)
        label_k = jnp.where(row_k == r, labels[r], label_k)
    valid_k = jnp.zeros_like(column_k)
    start = lax.axis_index("lon") * WLON + HALF_LON
    total = valid.shape[0]
    for c in range(WLON):
        at = start + c
        at = jnp.where(at >= total, at - total, at)
        valid_k = jnp.where(column_k == c, valid[at], valid_k)
    seen = (label_k == label_q) & ((valid_k > 0) | (rows == columns))
    added = jnp.where(seen, 0.0, BLOCKED).astype(f32)
    mask[...] = added[:, :128]
    mask_tail[...] = jnp.concatenate((added[:, 128:], jnp.zeros((WIN, 128 - TAIL), f32)), axis=1)

    heads, entries = table.shape
    gathered = 8
    wide = heads - gathered
    chunks = (entries + 255) // 256
    small_chunks = (entries + 127) // 128
    for c in range(small_chunks):
        size = min(128, entries - c * 128)
        part = table[wide:, c * 128 : c * 128 + size]
        if size < 128:
            part = jnp.concatenate((part, jnp.zeros((gathered, 128 - size), f32)), axis=1)
        fine[:, c * 128 : (c + 1) * 128] = part
    for c in range(chunks):
        size = min(256, entries - c * 256)
        part = table[:wide, c * 256 : c * 256 + size]
        if size < 256:
            part = jnp.concatenate((part, jnp.zeros((wide, 256 - size), f32)), axis=1)
        coarse = part.astype(bf16).astype(f32)
        split[c * wide : (c + 1) * wide, :] = coarse
        split[(chunks + c) * wide : (chunks + c + 1) * wide, :] = part - coarse
    source = split[...].astype(bf16)
    part_rows = chunks * wide

    def place(values, out):
        moved = mxu(mxu(permute, values.astype(f32).astype(bf16), NT).astype(bf16), permute, NT)
        out[0:WIN, :] = moved[:, :128]
        rest_rows[...] = jnp.concatenate((moved[:, 128:], jnp.zeros((WIN, 128 - TAIL), f32)), axis=1)
        total = None
        for g in range(8):
            piece = rest_rows[pl.ds(g, TAIL_GROUPS, stride=8), :]
            if g:
                piece = pltpu.roll(piece, TAIL * g, 1)
            total = piece if total is None else total + piece
        out[WIN : WIN + TAIL_GROUPS, :] = total

    entry = index[...]
    place(lax.shift_right_logical(entry, 8), high)
    place(entry & 255, low)
    upper, lower = high[...], low[...]
    far = lower >= 128.0
    fine_high[...] = (2.0 * upper + jnp.where(far, 1.0, 0.0)).astype(jnp.int32)
    fine_low[...] = jnp.where(far, lower - 128.0, lower).astype(jnp.int32)
    depth = lax.broadcasted_iota(jnp.int32, (256, 128), 0).astype(f32).astype(bf16)
    one, zero = jnp.ones((), bf16), jnp.zeros((), bf16)

    def lookup(row):
        hot = []
        for j in range(2):
            lane = jnp.broadcast_to(low[pl.ds(row + j, 1), :], (16, 128)).astype(bf16)
            hot.append(jnp.where(depth == jnp.concatenate([lane] * 16, axis=0), one, zero))
        product = mxu(source, jnp.concatenate(hot, axis=1))
        out = []
        for j in range(2):
            here = slice(j * 128, (j + 1) * 128)
            chunk = jnp.broadcast_to(high[pl.ds(row + j, 1), :], (8, 128))
            coarse, rest = [None] * (wide // 8), [None] * (wide // 8)
            for c in range(chunks):
                hit = chunk == c
                for block in range(wide // 8):
                    at = c * wide + block * 8
                    a = product[at : at + 8, here]
                    b = product[part_rows + at : part_rows + at + 8, here]
                    coarse[block] = a if c == 0 else jnp.where(hit, a, coarse[block])
                    rest[block] = b if c == 0 else jnp.where(hit, b, rest[block])
            found = [a + b for a, b in zip(coarse, rest)]
            chunk = jnp.broadcast_to(fine_high[pl.ds(row + j, 1), :], (8, 128))
            lane = jnp.broadcast_to(fine_low[pl.ds(row + j, 1), :], (8, 128))
            value = None
            for c in range(small_chunks):
                a = jnp.take_along_axis(fine[:, c * 128 : (c + 1) * 128], lane, axis=1, mode="promise_in_bounds")
                value = a if c == 0 else jnp.where(chunk == c, a, value)
            found.append(value)
            out.append(found)
        return out

    for key in range(0, WIN, 2):
        for j, found in enumerate(lookup(key)):
            extra = jnp.broadcast_to(mask[key + j : key + j + 1, :], (8, 128))
            for block, value in enumerate(found):
                main[pl.ds(block * 8 * WIN + key + j, 8, stride=WIN), :] = value + extra
    for row in range(0, TAIL_GROUPS, 2):
        for j, found in enumerate(lookup(WIN + row)):
            for block, value in enumerate(found):
                for g in range(8):
                    key = (row + j) * 8 + g
                    moved = pltpu.roll(value, 128 - TAIL * g, 1) if g else value
                    extra = jnp.broadcast_to(mask_tail[key : key + 1, :], (8, 128))
                    tail[pl.ds(block * 8 * WIN + key, 8, stride=WIN), :] = moved + extra


def window_bias(table, index, labels, valid):
    heads, entries = table.shape[-2:]
    whole = (entries + 255) // 256
    index_rows = WIN + TAIL_GROUPS
    return pl.pallas_call(
        bias_kernel,
        out_shape=[shape((heads * WIN, 128), f32)] * 2,
        in_specs=[pl.BlockSpec(memory_space=pltpu.MemorySpace.HBM)] * 4,
        scratch_shapes=[
            pltpu.VMEM((heads, entries), f32),
            pltpu.VMEM(index.shape, jnp.int32),
            pltpu.SMEM(labels.shape, jnp.int32),
            pltpu.SMEM(valid.shape, jnp.int32),
            pltpu.VMEM((2 * whole * (heads - 8), 256), f32),
            pltpu.VMEM((8, (entries + 127) // 128 * 128), f32),
            pltpu.VMEM((index_rows, 128), f32),
            pltpu.VMEM((index_rows, 128), f32),
            pltpu.VMEM((index_rows, 128), jnp.int32),
            pltpu.VMEM((index_rows, 128), jnp.int32),
            pltpu.VMEM((WIN, 128), f32),
            pltpu.VMEM((WIN, 128), f32),
            pltpu.VMEM((WIN, 128), f32),
            pltpu.SemaphoreType.DMA((4,)),
        ],
        compiler_params=params(),
        cost_estimate=cost(10**10, 2 * 10**7),
        name="bias",
    )(table, index, labels, valid)


def row_mean(values):
    return jnp.mean(values, axis=-1, keepdims=True)


def unit_rows(data):
    center = data - row_mean(data)
    scale = lax.rsqrt(row_mean(center * center) + epsilon)
    return center * scale, scale


def stacked(block):
    lane = lax.broadcasted_iota(jnp.int32, (1, 128), 1) // HEAD
    return jnp.concatenate(
        [jnp.where(lane == h, block, jnp.zeros((), block.dtype)) for h in range(GROUP)], axis=0
    )


def lanes_of(parts):
    lane = lax.broadcasted_iota(jnp.int32, (1, 128), 1) // HEAD
    out = parts[0]
    for h in range(1, GROUP):
        out = jnp.where(lane == h, parts[h], out)
    return out


def forward_kernel(
    own, first, second, third, packed, output, gain, main, tail,
    weights, triple, keys_t, residual, tokens,
    gathered, values_t, heads_t,
):
    width = own.shape[-1]
    upper = lax.axis_index("lev") == 1
    a, b = first[...].astype(f32)[:QUAD], second[...].astype(f32)
    lon = third[...].astype(f32)[:QUAD]
    for quad, piece in enumerate((own[...].astype(f32), jnp.where(upper, a, b), lon, jnp.where(upper, b, a))):
        gathered[quad * QUAD : (quad + 1) * QUAD, :] = piece
    data = gathered[...]
    tokens[...] = data.astype(bf16)
    unit, _ = unit_rows(data)
    normed = (unit * gain[...].reshape(1, -1)).astype(bf16)
    triple[...] = mxu(normed, packed[...]).astype(bf16)
    keys_t[...] = triple[:, width : 2 * width].astype(f32).T.astype(bf16)
    values_t[...] = triple[:, 2 * width :].astype(f32).T.astype(bf16)
    for g in range(width // 128):
        query = triple[:, g * 128 : (g + 1) * 128]
        key = triple[:, width + g * 128 : width + (g + 1) * 128]
        product = mxu(stacked(key), query, NT) * HEAD ** (-0.5)
        for h in range(GROUP):
            head = g * GROUP + h
            at = slice(head * WIN, (head + 1) * WIN)
            bias = jnp.concatenate((main[at, :], tail[at, :TAIL]), axis=1)
            scores = product[h * WIN : (h + 1) * WIN] + bias
            raised = jnp.exp(scores - jnp.max(scores, axis=0, keepdims=True))
            share = (raised * (1.0 / jnp.sum(raised, axis=0, keepdims=True))).astype(bf16)
            weights[at, :] = share
            here = slice(head * HEAD, (head + 1) * HEAD)
            heads_t[here, :] = mxu(values_t[here, :], share)
    heads = heads_t[...].T.astype(bf16)
    attended = mxu(heads, output[...]).astype(bf16)
    residual[...] = (data + attended.astype(f32)).astype(bf16)


def forward(pieces, packed, output, gain, main, tail):
    width = output.shape[0]
    return pl.pallas_call(
        forward_kernel,
        out_shape=[
            shape((HEADS * WIN, WIN), bf16),
            shape((WIN, 3 * width), bf16),
            shape((width, WIN), bf16),
            shape((WIN, width), bf16),
            shape((WIN, width), bf16),
        ],
        scratch_shapes=[
            pltpu.VMEM((WIN, width), f32),
            pltpu.VMEM((width, WIN), bf16),
            pltpu.VMEM((width, WIN), f32),
        ],
        compiler_params=params(),
        cost_estimate=cost(10**9, 2 * 10**7),
        name="forward",
    )(*pieces, packed, output, gain, main, tail)


def gain_rows(gain, out):
    width = out.shape[-1]
    for quad in range(4):
        for row in range(HALF_LAT):
            odd = 1 - (row + (quad & 1) * HALF_LAT) % 2
            for side in range(2):
                block = side * 2 + odd
                at = token_row(quad, row, side, 0)
                factor = gain[:, block * width : (block + 1) * width]
                out[at : at + CELLS, :] = jnp.broadcast_to(factor, (CELLS, width))


def cell_number(places):
    row, column, level, right = places
    band = lax.shift_right_logical(row + 1, 1)
    return (band * HALF_LON + lax.shift_right_logical(column, 1)) * LEVELS + level


def split_row(places):
    return (places[0] == 0) | (places[0] == WLAT - 1)


def sent_tokens(dims, axis):
    i = lax.broadcasted_iota(jnp.int32, dims, axis)
    last = (i >= 2 * CELLS).astype(jnp.int32)
    i = i - last * 2 * CELLS
    right = (i >= CELLS).astype(jnp.int32)
    cell = i - right * CELLS
    return (2 * right + last) * QUAD + last * (HALF_LAT - 1) * 2 * CELLS + cell


def columns_of(parts):
    lane = lax.broadcasted_iota(jnp.int32, (1, 128), 1)
    out = jnp.zeros((WIN, 128), f32)
    for i, part in enumerate(parts):
        out = jnp.where(lane == i, part, out)
    return out


def moments_kernel(residual, kept, first, third, fourth, fifth, gain, scaled, moments, sent, factors):
    width = residual.shape[-1]
    upper = lax.axis_index("lev") == 1
    own, a, b = kept[...].astype(f32), fourth[...].astype(f32), fifth[...].astype(f32)
    below, right = first[...].astype(f32)[QUAD:], third[...].astype(f32)[QUAD:]
    gain_rows(gain, factors)
    for quad, part in enumerate((
        jnp.where(upper, own, a),
        jnp.where(upper, below, b),
        jnp.where(upper, a, right),
        jnp.where(upper, b, below),
    )):
        scaled[quad * QUAD : (quad + 1) * QUAD, :] = part
    grad = scaled[...] * factors[...]
    scaled[...] = grad
    data = residual[...].astype(f32)
    down = token_places((WIN, 1), 0)
    grouping = jnp.where(cell_number(down) == cell_number(token_places((1, WIN), 1)), 1.0, 0.0).astype(f32)
    inverse = jnp.where(split_row(down), 1 / (2 * width), 1 / (4 * width)).astype(f32)
    total = jnp.sum(data, axis=-1, keepdims=True)
    middle = exact(grouping, jnp.broadcast_to(total, (WIN, 128)))[:, 0:1] * inverse
    center = data - middle
    sums = columns_of((
        jnp.sum(center * center, axis=-1, keepdims=True),
        jnp.sum(grad, axis=-1, keepdims=True),
        jnp.sum(grad * center, axis=-1, keepdims=True),
    ))
    sums = exact(grouping, sums)
    lane = lax.broadcasted_iota(jnp.int32, (1, 128), 1)
    sums = jnp.where(lane == 3, middle, sums)
    moments[...] = sums
    pick = sent_tokens((4 * CELLS, 1), 0) == lax.broadcasted_iota(jnp.int32, (4 * CELLS, WIN), 1)
    sent[...] = exact(jnp.where(pick, 1.0, 0.0).astype(f32), sums)


def cell_moments(residual, pieces, gain):
    width = residual.shape[-1]
    return pl.pallas_call(
        moments_kernel,
        out_shape=[shape((WIN, width), f32), shape((WIN, 128), f32), shape((4 * CELLS, 128), f32)],
        scratch_shapes=[pltpu.VMEM((WIN, width), f32)],
        compiler_params=params(),
        cost_estimate=cost(10**8, 10**6),
        name="moments",
    )(residual, *pieces, gain)


def merge_kernel(residual, scaled, moments, before, after, gain, kept, below, right, far, grad, factors):
    width = residual.shape[-1]
    upper = lax.axis_index("lev") == 1
    gain_rows(gain, factors)
    down = token_places((WIN, 1), 0)
    shared = split_row(down)
    row = down[0]
    sender = split_tokens(sent_tokens((1, 4 * CELLS), 1))
    match = (cell_number(down) == cell_number(sender)) & shared
    there = jnp.concatenate((before[2 * CELLS :], after[: 2 * CELLS]), axis=0)
    theirs = exact(jnp.where(match, 1.0, 0.0).astype(f32), there)
    mine = moments[...]
    full = 4.0 * width
    middle = jnp.where(shared, 0.5 * (mine[:, 3:4] + theirs[:, 3:4]), mine[:, 3:4])
    gap = theirs[:, 3:4] - mine[:, 3:4]
    square = jnp.where(shared, mine[:, 0:1] + theirs[:, 0:1] + gap * gap * width, mine[:, 0:1])
    scale = lax.rsqrt(square / full + epsilon)
    grad_sum = jnp.where(shared, mine[:, 1:2] + theirs[:, 1:2], mine[:, 1:2])
    cross = jnp.where(
        shared,
        mine[:, 2:3] + (mine[:, 3:4] - middle) * mine[:, 1:2]
        + theirs[:, 2:3] + (theirs[:, 3:4] - middle) * theirs[:, 1:2],
        mine[:, 2:3],
    )
    unit = (residual[...].astype(f32) - middle) * scale
    grad[...] = (scale * (scaled[...] - grad_sum / full - unit * (cross * scale / full))).astype(bf16)
    out = unit * factors[...]
    parts = [quadrant(out, quad) for quad in range(4)]
    kept[...] = jnp.where(upper, parts[0], parts[2]).astype(bf16)
    below[...] = jnp.where(upper, parts[1], parts[3]).astype(bf16)
    right[...] = jnp.where(upper, parts[2], parts[0]).astype(bf16)
    far[...] = jnp.where(upper, parts[3], parts[1]).astype(bf16)


def merge_back(residual, scaled, moments, before, after, gain):
    width = residual.shape[-1]
    piece = shape((QUAD, width), bf16)
    return pl.pallas_call(
        merge_kernel,
        out_shape=[piece] * 4 + [shape((WIN, width), bf16)],
        scratch_shapes=[pltpu.VMEM((WIN, width), f32)],
        compiler_params=params(),
        cost_estimate=cost(10**8, 10**6),
        name="merge",
    )(residual, scaled, moments, before, after, gain)


def backward_kernel(grad, weights, triple, keys_t, output, joined, queries_t):
    width = grad.shape[-1]
    upstream = grad[...]
    grad_heads = mxu(upstream, output[...], NT).astype(bf16)
    for g in range(width // 128):
        here = slice(g * 128, (g + 1) * 128)
        query = triple[:, g * 128 : (g + 1) * 128]
        value = triple[:, 2 * width + g * 128 : 2 * width + (g + 1) * 128]
        arriving = grad_heads[:, here]
        product = mxu(stacked(value), arriving, NT)
        shares = weights[g * GROUP * WIN : (g + 1) * GROUP * WIN, :]
        grad_value = mxu(shares, arriving)
        slopes = []
        for h in range(GROUP):
            head = g * GROUP + h
            share = shares[h * WIN : (h + 1) * WIN].astype(f32)
            change = product[h * WIN : (h + 1) * WIN]
            level = jnp.sum(share * change, axis=0, keepdims=True)
            slope = (share * (change - level) * HEAD ** (-0.5)).astype(bf16)
            at = slice(head * HEAD, (head + 1) * HEAD)
            queries_t[at, :] = mxu(keys_t[at, :], slope)
            slopes.append(slope)
        grad_key = mxu(jnp.concatenate(slopes, axis=0), query)
        split = [slice(h * WIN, (h + 1) * WIN) for h in range(GROUP)]
        joined[:, width + g * 128 : width + (g + 1) * 128] = lanes_of([grad_key[s] for s in split]).astype(bf16)
        joined[:, 2 * width + g * 128 : 2 * width + (g + 1) * 128] = lanes_of(
            [grad_value[s] for s in split]
        ).astype(bf16)
    joined[:, :width] = queries_t[...].T.astype(bf16)


def backward(grad, weights, triple, keys_t, output):
    width = grad.shape[-1]
    return pl.pallas_call(
        backward_kernel,
        out_shape=shape((WIN, 3 * width), bf16),
        scratch_shapes=[pltpu.VMEM((width, WIN), f32)],
        compiler_params=params(),
        cost_estimate=cost(10**10, 2 * 10**7),
        name="backward",
    )(grad, weights, triple, keys_t, output)


def finish_kernel(grad, joined, tokens, packed, gain, own, lat, lon, both):
    grad_inputs = mxu(joined[...], packed[...], NT).astype(bf16)
    unit, scale = unit_rows(tokens[...].astype(f32))
    scaled = grad_inputs.astype(f32) * gain[...].reshape(1, -1)
    out = grad[...].astype(f32) + scale * (scaled - row_mean(scaled) - unit * row_mean(scaled * unit))
    for quad, piece in enumerate((own, lat, lon, both)):
        piece[...] = quadrant(out, quad).astype(bf16)


def finish(grad, joined, tokens, packed, gain):
    width = grad.shape[-1]
    return pl.pallas_call(
        finish_kernel,
        out_shape=[shape((QUAD, width), bf16)] * 4,
        compiler_params=params(),
        cost_estimate=cost(10**9, 2 * 10**6),
        name="finish",
    )(grad, joined, tokens, packed, gain)


def unpack_kernel(own, lat, lon, both, same_here, other_here, same_next, other_next, merged, tokens):
    width = own.shape[-1]
    quads = [piece[...].astype(f32) for piece in (own, lat, lon, both)]
    for line in range(WLAT):
        for column in range(WLON):
            quad = (0 if line >= HALF_LAT else 1) + (0 if column >= HALF_LON else 2)
            inner = column % HALF_LON
            at = token_row(0, line % HALF_LAT, inner % 2, inner // 2)
            tokens[line, column] = quads[quad][at : at + LEVELS].astype(bf16)
    upper = lax.axis_index("lev") == 1
    same = (same_here[...].astype(f32), same_next[...].astype(f32))
    other = (other_here[...].astype(f32), other_next[...].astype(f32))
    low = [jnp.where(upper, b, a) for a, b in zip(same, other)]
    high = [jnp.where(upper, a, b) for a, b in zip(same, other)]
    for row, odd, below, inner in cell_places():
        for pair in range(PAIRS):
            for side in range(2):
                block = side * 2 + odd
                at = token_row(0, inner, side, pair)
                here = slice(at, at + LEVELS)
                merged[row, pair, :, block * width : (block + 1) * width] = jnp.concatenate(
                    (low[below][here], high[below][here]), axis=0
                ).astype(bf16)


def unpack_pieces(token_pieces, cell_pieces):
    width = token_pieces[0].shape[-1]
    return pl.pallas_call(
        unpack_kernel,
        out_shape=[
            shape((HALF_LAT, PAIRS, 2 * LEVELS, 4 * width), bf16),
            shape((WLAT, WLON, LEVELS, width), bf16),
        ],
        compiler_params=params(),
        name="unpack",
    )(*token_pieces, *cell_pieces)


def routes(sizes, target):
    lons, lats, levs = sizes

    def number(i, a, k):
        return ((i % lons) * lats + a % lats) * levs + k % levs

    return [
        (number(i, a, k), number(*target(i, a, k)))
        for i in range(lons)
        for a in range(lats)
        for k in range(levs)
    ]


def send(block, sizes, target, back=False):
    pairs = routes(sizes, target)
    if back:
        pairs = [(b, a) for a, b in pairs]
    return lax.ppermute(block, ("lon", "lat", "lev"), pairs)


FIRST = lambda i, a, k: (i - (1 - k), a - 1, k)
SECOND = lambda i, a, k: (i - k, a - 1, k)
THIRD = lambda i, a, k: (i - 1, a, k)
FOURTH = lambda i, a, k: (i - (1 - k), a, 1 - k)
FIFTH = lambda i, a, k: (i - (1 - k), a - 1, 1 - k)
LAT = lambda i, a, k: (i, a - 1, k)
LON = lambda i, a, k: (i - 1, a, k)
BOTH = lambda i, a, k: (i - 1, a - 1, k)
HERE = lambda i, a, k: (i - (1 - k), a, k)


def per_device(
    sizes,
    tokens,
    packed_weight,
    output_weight,
    norm_gain,
    merge_gain,
    bias_table,
    bias_index,
    row_labels,
    column_valid,
    merged_grad,
):
    own, first, second, third, kept, fourth, fifth = pack_pieces(
        tokens.transpose(1, 2, 0, 3), merged_grad.transpose(1, 2, 0, 3)
    )
    first = send(first, sizes, FIRST)
    second = send(second, sizes, SECOND)
    third = send(third, sizes, THIRD)
    fourth = send(fourth, sizes, FOURTH)
    fifth = send(fifth, sizes, FIFTH)
    main, tail = window_bias(bias_table, bias_index, row_labels, column_valid)
    cell_gain = merge_gain.reshape(1, -1)
    weights, triple, keys_t, residual, data = forward(
        (own, first, second, third), packed_weight, output_weight, norm_gain, main, tail
    )
    scaled, moments, sent = cell_moments(residual, (kept, first, third, fourth, fifth), cell_gain)
    before = send(sent, sizes, lambda i, a, k: (i, a + 1, k))
    after = before if sizes[1] == 2 else send(sent, sizes, lambda i, a, k: (i, a - 1, k))
    kept, below, right, far, grad = merge_back(residual, scaled, moments, before, after, cell_gain)
    below = send(below, sizes, FIRST, True)
    far = send(far, sizes, FIFTH, True)
    right = send(right, sizes, FOURTH, True)
    kept = send(kept, sizes, HERE, True)
    joined = backward(grad, weights, triple, keys_t, output_weight)
    joined, kept, below, right, far = lax.optimization_barrier((joined, kept, below, right, far))
    own, lat, lon, both = finish(grad, joined, data, packed_weight, norm_gain)
    lat = send(lat, sizes, LAT, True)
    both = send(both, sizes, BOTH, True)
    lon = send(lon, sizes, LON, True)
    merged, grads = unpack_pieces((own, lat, lon, both), (kept, right, below, far))
    return merged.transpose(2, 0, 1, 3), grads.transpose(2, 0, 1, 3)


def solution(mesh):
    sizes = tuple(mesh.shape[name] for name in ("lon", "lat", "lev"))
    placed = (
        P("lev", "lat", "lon", None),
        P(),
        P(),
        P(),
        P(),
        P("lev", "lat", None, None),
        P(),
        P("lat"),
        P(),
        P(None, "lat", ("lon", "lev"), None),
    )
    return jax.shard_map(
        functools.partial(per_device, sizes),
        mesh=mesh,
        in_specs=placed,
        out_specs=(P(None, "lat", ("lon", "lev"), None), P("lev", "lat", "lon", None)),
        check_vma=False,
    )
```

```python
import functools

import jax
import jax.numpy as jnp
from jax import lax
from jax.experimental import pallas as pl
from jax.experimental.pallas import tpu as pltpu
from jax.sharding import PartitionSpec as P

HEADS = 24
HEAD = 32
WLAT = 6
WLON = 12
HALF_LAT = WLAT // 2
HALF_LON = WLON // 2
LEVELS = 2
WIN = LEVELS * WLAT * WLON
QUAD = WIN // 4
PAIRS = HALF_LON // 2
CELLS = LEVELS * PAIRS
GROUP = 128 // HEAD
TAIL = WIN - 128
TAIL_GROUPS = WIN // 8
BLOCKED = -1e30

epsilon = 1e-05
f32 = jnp.float32
bf16 = jnp.bfloat16

NN = (((1,), (0,)), ((), ()))
NT = (((1,), (1,)), ((), ()))


def token_row(quad, row, side, pair):
    return quad * QUAD + ((row * 2 + side) * PAIRS + pair) * LEVELS


def split_tokens(t):
    def digit(rest, size, count):
        found = jnp.zeros_like(rest)
        for i in range(1, count):
            found = found + (rest >= i * size).astype(jnp.int32)
        return found, rest - found * size

    quad, rest = digit(t, QUAD, 4)
    row, rest = digit(rest, 2 * CELLS, HALF_LAT)
    side, rest = digit(rest, CELLS, 2)
    pair, level = digit(rest, LEVELS, PAIRS)
    right, below = digit(quad, 2, 2)
    row = row + HALF_LAT * below
    column = right * HALF_LON + 2 * pair + side
    return row, column, level, right


def token_places(dims, axis):
    return split_tokens(lax.broadcasted_iota(jnp.int32, dims, axis))


def mxu(a, b, dims=NN):
    return lax.dot_general(a, b, dims, preferred_element_type=f32)


def exact(a, b):
    return lax.dot_general(a, b, NN, precision=lax.Precision.HIGHEST, preferred_element_type=f32)


def params(megabytes=12):
    return pltpu.CompilerParams(vmem_limit_bytes=megabytes << 20)


def shape(dims, dtype):
    return jax.ShapeDtypeStruct(dims, dtype)


def cost(flops, nbytes):
    return pl.CostEstimate(flops=flops, bytes_accessed=nbytes, transcendentals=0)


def in_hbm(*arrays):
    return [pltpu.with_memory_space_constraint(x, pltpu.MemorySpace.HBM) for x in arrays]


def start_copies(done, *pairs):
    copies = [pltpu.make_async_copy(source, target, done.at[i]) for i, (source, target) in enumerate(pairs)]
    for copy in copies:
        copy.start()
    return copies


def quadrant(values, quad):
    return values[quad * QUAD : (quad + 1) * QUAD]


def cell_places():
    return [(0, 0, True, 0), (0, 1, True, 1), (1, 0, True, 2), (1, 1, False, 0), (2, 0, False, 1), (2, 1, False, 2)]


def pack_kernel(
    tokens_at, grad_at, own, first, second, third, kept, fourth, fifth, tokens, grad, rows, cells, done
):
    width = tokens.shape[-1]
    copies = start_copies(done, (tokens_at, tokens), (grad_at, grad))
    copies[0].wait()
    for line in range(WLAT):
        for column in range(WLON):
            quad = (0 if line >= HALF_LAT else 1) + (0 if column >= HALF_LON else 2)
            inner = column % HALF_LON
            at = token_row(quad, line % HALF_LAT, inner % 2, inner // 2)
            rows[at : at + LEVELS, :] = tokens[line, column].astype(f32)
    copies[1].wait()
    upper = lax.axis_index("lev") == 1
    for row, odd, below, inner in cell_places():
        for pair in range(PAIRS):
            for side in range(2):
                block = side * 2 + odd
                part = grad[row, pair, :, block * width : (block + 1) * width].astype(f32)
                low, high = part[:LEVELS], part[LEVELS:]
                at = token_row(int(below), inner, side, pair)
                cells[at : at + LEVELS, :] = jnp.where(upper, high, low)
                at = at + 2 * QUAD
                cells[at : at + LEVELS, :] = jnp.where(upper, low, high)
    data, grads = rows[...], cells[...]
    lat, lon, both = quadrant(data, 1), quadrant(data, 2), quadrant(data, 3)
    here, below = quadrant(grads, 0), quadrant(grads, 1)
    own[...] = quadrant(data, 0).astype(bf16)
    first[...] = jnp.concatenate((jnp.where(upper, lat, both), below), axis=0).astype(bf16)
    second[...] = jnp.where(upper, both, lat).astype(bf16)
    third[...] = jnp.concatenate((lon, here), axis=0).astype(bf16)
    kept[...] = here.astype(bf16)
    fourth[...] = quadrant(grads, 2).astype(bf16)
    fifth[...] = quadrant(grads, 3).astype(bf16)


def pack_pieces(tokens, grad):
    width = tokens.shape[-1]
    piece, double = shape((QUAD, width), bf16), shape((2 * QUAD, width), bf16)
    return pl.pallas_call(
        pack_kernel,
        out_shape=[piece, double, piece, double, piece, piece, piece],
        in_specs=[pl.BlockSpec(memory_space=pltpu.MemorySpace.HBM)] * 2,
        scratch_shapes=[
            pltpu.VMEM(tokens.shape, bf16),
            pltpu.VMEM(grad.shape, bf16),
            pltpu.VMEM((WIN, width), f32),
            pltpu.VMEM((WIN, width), f32),
            pltpu.SemaphoreType.DMA((2,)),
        ],
        compiler_params=params(),
        name="pack",
    )(*in_hbm(tokens, grad))


def bias_kernel(
    table_at, index_at, labels_at, valid_at, main, tail,
    table, index, labels, valid, split, fine, high, low, fine_high, fine_low, rest_rows, mask, mask_tail, done,
):
    copies = start_copies(
        done, (table_at.at[0, 0], table), (index_at, index), (labels_at, labels), (valid_at, valid)
    )
    row_k, column_k, level_k, _ = token_places((WIN, 1), 0)
    row_q, _, _, _ = token_places((1, WIN), 1)
    natural = (level_k * WLAT + row_k) * WLON + column_k
    columns = lax.broadcasted_iota(jnp.int32, (WIN, WIN), 1)
    rows = lax.broadcasted_iota(jnp.int32, (WIN, WIN), 0)
    permute = jnp.where(natural == columns, 1.0, 0.0).astype(bf16)
    for copy in copies:
        copy.wait()

    label_q, label_k = jnp.zeros_like(row_q), jnp.zeros_like(row_k)
    for r in range(WLAT):
        label_q = jnp.where(row_q == r, labels[r], label_q)
        label_k = jnp.where(row_k == r, labels[r], label_k)
    valid_k = jnp.zeros_like(column_k)
    start = lax.axis_index("lon") * WLON + HALF_LON
    total = valid.shape[0]
    for c in range(WLON):
        at = start + c
        at = jnp.where(at >= total, at - total, at)
        valid_k = jnp.where(column_k == c, valid[at], valid_k)
    seen = (label_k == label_q) & ((valid_k > 0) | (rows == columns))
    added = jnp.where(seen, 0.0, BLOCKED).astype(f32)
    mask[...] = added[:, :128]
    mask_tail[...] = jnp.concatenate((added[:, 128:], jnp.zeros((WIN, 128 - TAIL), f32)), axis=1)

    heads, entries = table.shape
    gathered = 8
    wide = heads - gathered
    chunks = (entries + 255) // 256
    small_chunks = (entries + 127) // 128
    for c in range(small_chunks):
        size = min(128, entries - c * 128)
        part = table[wide:, c * 128 : c * 128 + size]
        if size < 128:
            part = jnp.concatenate((part, jnp.zeros((gathered, 128 - size), f32)), axis=1)
        fine[:, c * 128 : (c + 1) * 128] = part
    for c in range(chunks):
        size = min(256, entries - c * 256)
        part = table[:wide, c * 256 : c * 256 + size]
        if size < 256:
            part = jnp.concatenate((part, jnp.zeros((wide, 256 - size), f32)), axis=1)
        coarse = part.astype(bf16).astype(f32)
        split[c * wide : (c + 1) * wide, :] = coarse
        split[(chunks + c) * wide : (chunks + c + 1) * wide, :] = part - coarse
    source = split[...].astype(bf16)
    part_rows = chunks * wide

    def place(values, out):
        moved = mxu(mxu(permute, values.astype(f32).astype(bf16), NT).astype(bf16), permute, NT)
        out[0:WIN, :] = moved[:, :128]
        rest_rows[...] = jnp.concatenate((moved[:, 128:], jnp.zeros((WIN, 128 - TAIL), f32)), axis=1)
        total = None
        for g in range(8):
            piece = rest_rows[pl.ds(g, TAIL_GROUPS, stride=8), :]
            if g:
                piece = pltpu.roll(piece, TAIL * g, 1)
            total = piece if total is None else total + piece
        out[WIN : WIN + TAIL_GROUPS, :] = total

    entry = index[...]
    place(lax.shift_right_logical(entry, 8), high)
    place(entry & 255, low)
    upper, lower = high[...], low[...]
    far = lower >= 128.0
    fine_high[...] = (2.0 * upper + jnp.where(far, 1.0, 0.0)).astype(jnp.int32)
    fine_low[...] = jnp.where(far, lower - 128.0, lower).astype(jnp.int32)
    depth = lax.broadcasted_iota(jnp.int32, (256, 128), 0).astype(f32).astype(bf16)
    one, zero = jnp.ones((), bf16), jnp.zeros((), bf16)

    def lookup(row):
        hot = []
        for j in range(2):
            lane = jnp.broadcast_to(low[pl.ds(row + j, 1), :], (16, 128)).astype(bf16)
            hot.append(jnp.where(depth == jnp.concatenate([lane] * 16, axis=0), one, zero))
        product = mxu(source, jnp.concatenate(hot, axis=1))
        out = []
        for j in range(2):
            here = slice(j * 128, (j + 1) * 128)
            chunk = jnp.broadcast_to(high[pl.ds(row + j, 1), :], (8, 128))
            coarse, rest = [None] * (wide // 8), [None] * (wide // 8)
            for c in range(chunks):
                hit = chunk == c
                for block in range(wide // 8):
                    at = c * wide + block * 8
                    a = product[at : at + 8, here]
                    b = product[part_rows + at : part_rows + at + 8, here]
                    coarse[block] = a if c == 0 else jnp.where(hit, a, coarse[block])
                    rest[block] = b if c == 0 else jnp.where(hit, b, rest[block])
            found = [a + b for a, b in zip(coarse, rest)]
            chunk = jnp.broadcast_to(fine_high[pl.ds(row + j, 1), :], (8, 128))
            lane = jnp.broadcast_to(fine_low[pl.ds(row + j, 1), :], (8, 128))
            value = None
            for c in range(small_chunks):
                a = jnp.take_along_axis(fine[:, c * 128 : (c + 1) * 128], lane, axis=1, mode="promise_in_bounds")
                value = a if c == 0 else jnp.where(chunk == c, a, value)
            found.append(value)
            out.append(found)
        return out

    for key in range(0, WIN, 2):
        for j, found in enumerate(lookup(key)):
            extra = jnp.broadcast_to(mask[key + j : key + j + 1, :], (8, 128))
            for block, value in enumerate(found):
                main[pl.ds(block * 8 * WIN + key + j, 8, stride=WIN), :] = value + extra
    for row in range(0, TAIL_GROUPS, 2):
        for j, found in enumerate(lookup(WIN + row)):
            for block, value in enumerate(found):
                for g in range(8):
                    key = (row + j) * 8 + g
                    moved = pltpu.roll(value, 128 - TAIL * g, 1) if g else value
                    extra = jnp.broadcast_to(mask_tail[key : key + 1, :], (8, 128))
                    tail[pl.ds(block * 8 * WIN + key, 8, stride=WIN), :] = moved + extra


def window_bias(table, index, labels, valid):
    heads, entries = table.shape[-2:]
    whole = (entries + 255) // 256
    index_rows = WIN + TAIL_GROUPS
    return pl.pallas_call(
        bias_kernel,
        out_shape=[shape((heads * WIN, 128), f32)] * 2,
        in_specs=[pl.BlockSpec(memory_space=pltpu.MemorySpace.HBM)] * 4,
        scratch_shapes=[
            pltpu.VMEM((heads, entries), f32),
            pltpu.VMEM(index.shape, jnp.int32),
            pltpu.SMEM(labels.shape, jnp.int32),
            pltpu.SMEM(valid.shape, jnp.int32),
            pltpu.VMEM((2 * whole * (heads - 8), 256), f32),
            pltpu.VMEM((8, (entries + 127) // 128 * 128), f32),
            pltpu.VMEM((index_rows, 128), f32),
            pltpu.VMEM((index_rows, 128), f32),
            pltpu.VMEM((index_rows, 128), jnp.int32),
            pltpu.VMEM((index_rows, 128), jnp.int32),
            pltpu.VMEM((WIN, 128), f32),
            pltpu.VMEM((WIN, 128), f32),
            pltpu.VMEM((WIN, 128), f32),
            pltpu.SemaphoreType.DMA((4,)),
        ],
        compiler_params=params(),
        cost_estimate=cost(10**10, 2 * 10**7),
        name="bias",
    )(*in_hbm(table, index, labels, valid))


def row_mean(values):
    return jnp.mean(values, axis=-1, keepdims=True)


def unit_rows(data):
    center = data - row_mean(data)
    scale = lax.rsqrt(row_mean(center * center) + epsilon)
    return center * scale, scale


def stacked(block):
    lane = lax.broadcasted_iota(jnp.int32, (1, 128), 1) // HEAD
    return jnp.concatenate(
        [jnp.where(lane == h, block, jnp.zeros((), block.dtype)) for h in range(GROUP)], axis=0
    )


def lanes_of(parts):
    lane = lax.broadcasted_iota(jnp.int32, (1, 128), 1) // HEAD
    out = parts[0]
    for h in range(1, GROUP):
        out = jnp.where(lane == h, parts[h], out)
    return out


def forward_kernel(
    own, first, second, third, packed, output, gain, main, tail,
    weights, triple, keys_t, residual, tokens,
    gathered, values_t, heads_t,
):
    width = own.shape[-1]
    upper = lax.axis_index("lev") == 1
    a, b = first[...].astype(f32)[:QUAD], second[...].astype(f32)
    lon = third[...].astype(f32)[:QUAD]
    for quad, piece in enumerate((own[...].astype(f32), jnp.where(upper, a, b), lon, jnp.where(upper, b, a))):
        gathered[quad * QUAD : (quad + 1) * QUAD, :] = piece
    data = gathered[...]
    tokens[...] = data.astype(bf16)
    unit, _ = unit_rows(data)
    normed = (unit * gain[...].reshape(1, -1)).astype(bf16)
    triple[...] = mxu(normed, packed[...]).astype(bf16)
    keys_t[...] = triple[:, width : 2 * width].astype(f32).T.astype(bf16)
    values_t[...] = triple[:, 2 * width :].astype(f32).T.astype(bf16)
    for g in range(width // 128):
        query = triple[:, g * 128 : (g + 1) * 128]
        key = triple[:, width + g * 128 : width + (g + 1) * 128]
        product = mxu(stacked(key), query, NT) * HEAD ** (-0.5)
        for h in range(GROUP):
            head = g * GROUP + h
            at = slice(head * WIN, (head + 1) * WIN)
            bias = jnp.concatenate((main[at, :], tail[at, :TAIL]), axis=1)
            scores = product[h * WIN : (h + 1) * WIN] + bias
            raised = jnp.exp(scores - jnp.max(scores, axis=0, keepdims=True))
            share = (raised * (1.0 / jnp.sum(raised, axis=0, keepdims=True))).astype(bf16)
            weights[at, :] = share
            here = slice(head * HEAD, (head + 1) * HEAD)
            heads_t[here, :] = mxu(values_t[here, :], share)
    heads = heads_t[...].T.astype(bf16)
    attended = mxu(heads, output[...]).astype(bf16)
    residual[...] = (data + attended.astype(f32)).astype(bf16)


def forward(pieces, packed, output, gain, main, tail):
    width = output.shape[0]
    return pl.pallas_call(
        forward_kernel,
        out_shape=[
            shape((HEADS * WIN, WIN), bf16),
            shape((WIN, 3 * width), bf16),
            shape((width, WIN), bf16),
            shape((WIN, width), bf16),
            shape((WIN, width), bf16),
        ],
        scratch_shapes=[
            pltpu.VMEM((WIN, width), f32),
            pltpu.VMEM((width, WIN), bf16),
            pltpu.VMEM((width, WIN), f32),
        ],
        compiler_params=params(),
        cost_estimate=cost(10**9, 2 * 10**7),
        name="forward",
    )(*pieces, packed, output, gain, main, tail)


def gain_rows(gain, out):
    width = out.shape[-1]
    for quad in range(4):
        for row in range(HALF_LAT):
            odd = 1 - (row + (quad & 1) * HALF_LAT) % 2
            for side in range(2):
                block = side * 2 + odd
                at = token_row(quad, row, side, 0)
                factor = gain[:, block * width : (block + 1) * width]
                out[at : at + CELLS, :] = jnp.broadcast_to(factor, (CELLS, width))


def cell_number(places):
    row, column, level, right = places
    band = lax.shift_right_logical(row + 1, 1)
    return (band * HALF_LON + lax.shift_right_logical(column, 1)) * LEVELS + level


def split_row(places):
    return (places[0] == 0) | (places[0] == WLAT - 1)


def sent_tokens(dims, axis):
    i = lax.broadcasted_iota(jnp.int32, dims, axis)
    last = (i >= 2 * CELLS).astype(jnp.int32)
    i = i - last * 2 * CELLS
    right = (i >= CELLS).astype(jnp.int32)
    cell = i - right * CELLS
    return (2 * right + last) * QUAD + last * (HALF_LAT - 1) * 2 * CELLS + cell


def columns_of(parts):
    lane = lax.broadcasted_iota(jnp.int32, (1, 128), 1)
    out = jnp.zeros((WIN, 128), f32)
    for i, part in enumerate(parts):
        out = jnp.where(lane == i, part, out)
    return out


def moments_kernel(residual, kept, first, third, fourth, fifth, gain, scaled, moments, sent, factors):
    width = residual.shape[-1]
    upper = lax.axis_index("lev") == 1
    own, a, b = kept[...].astype(f32), fourth[...].astype(f32), fifth[...].astype(f32)
    below, right = first[...].astype(f32)[QUAD:], third[...].astype(f32)[QUAD:]
    gain_rows(gain, factors)
    for quad, part in enumerate((
        jnp.where(upper, own, a),
        jnp.where(upper, below, b),
        jnp.where(upper, a, right),
        jnp.where(upper, b, below),
    )):
        scaled[quad * QUAD : (quad + 1) * QUAD, :] = part
    grad = scaled[...] * factors[...]
    scaled[...] = grad
    data = residual[...].astype(f32)
    down = token_places((WIN, 1), 0)
    grouping = jnp.where(cell_number(down) == cell_number(token_places((1, WIN), 1)), 1.0, 0.0).astype(f32)
    inverse = jnp.where(split_row(down), 1 / (2 * width), 1 / (4 * width)).astype(f32)
    total = jnp.sum(data, axis=-1, keepdims=True)
    middle = exact(grouping, jnp.broadcast_to(total, (WIN, 128)))[:, 0:1] * inverse
    center = data - middle
    sums = columns_of((
        jnp.sum(center * center, axis=-1, keepdims=True),
        jnp.sum(grad, axis=-1, keepdims=True),
        jnp.sum(grad * center, axis=-1, keepdims=True),
    ))
    sums = exact(grouping, sums)
    lane = lax.broadcasted_iota(jnp.int32, (1, 128), 1)
    sums = jnp.where(lane == 3, middle, sums)
    moments[...] = sums
    pick = sent_tokens((4 * CELLS, 1), 0) == lax.broadcasted_iota(jnp.int32, (4 * CELLS, WIN), 1)
    sent[...] = exact(jnp.where(pick, 1.0, 0.0).astype(f32), sums)


def cell_moments(residual, pieces, gain):
    width = residual.shape[-1]
    return pl.pallas_call(
        moments_kernel,
        out_shape=[shape((WIN, width), f32), shape((WIN, 128), f32), shape((4 * CELLS, 128), f32)],
        scratch_shapes=[pltpu.VMEM((WIN, width), f32)],
        compiler_params=params(),
        cost_estimate=cost(10**8, 10**6),
        name="moments",
    )(residual, *pieces, gain)


def merge_kernel(residual, scaled, moments, before, after, gain, kept, below, right, far, grad, factors):
    width = residual.shape[-1]
    upper = lax.axis_index("lev") == 1
    gain_rows(gain, factors)
    down = token_places((WIN, 1), 0)
    shared = split_row(down)
    row = down[0]
    sender = split_tokens(sent_tokens((1, 4 * CELLS), 1))
    match = (cell_number(down) == cell_number(sender)) & shared
    there = jnp.concatenate((before[2 * CELLS :], after[: 2 * CELLS]), axis=0)
    theirs = exact(jnp.where(match, 1.0, 0.0).astype(f32), there)
    mine = moments[...]
    full = 4.0 * width
    middle = jnp.where(shared, 0.5 * (mine[:, 3:4] + theirs[:, 3:4]), mine[:, 3:4])
    gap = theirs[:, 3:4] - mine[:, 3:4]
    square = jnp.where(shared, mine[:, 0:1] + theirs[:, 0:1] + gap * gap * width, mine[:, 0:1])
    scale = lax.rsqrt(square / full + epsilon)
    grad_sum = jnp.where(shared, mine[:, 1:2] + theirs[:, 1:2], mine[:, 1:2])
    cross = jnp.where(
        shared,
        mine[:, 2:3] + (mine[:, 3:4] - middle) * mine[:, 1:2]
        + theirs[:, 2:3] + (theirs[:, 3:4] - middle) * theirs[:, 1:2],
        mine[:, 2:3],
    )
    unit = (residual[...].astype(f32) - middle) * scale
    grad[...] = (scale * (scaled[...] - grad_sum / full - unit * (cross * scale / full))).astype(bf16)
    out = unit * factors[...]
    parts = [quadrant(out, quad) for quad in range(4)]
    kept[...] = jnp.where(upper, parts[0], parts[2]).astype(bf16)
    below[...] = jnp.where(upper, parts[1], parts[3]).astype(bf16)
    right[...] = jnp.where(upper, parts[2], parts[0]).astype(bf16)
    far[...] = jnp.where(upper, parts[3], parts[1]).astype(bf16)


def merge_back(residual, scaled, moments, before, after, gain):
    width = residual.shape[-1]
    piece = shape((QUAD, width), bf16)
    return pl.pallas_call(
        merge_kernel,
        out_shape=[piece] * 4 + [shape((WIN, width), bf16)],
        scratch_shapes=[pltpu.VMEM((WIN, width), f32)],
        compiler_params=params(),
        cost_estimate=cost(10**8, 10**6),
        name="merge",
    )(residual, scaled, moments, before, after, gain)


def backward_kernel(grad, weights, triple, keys_t, output, joined, queries_t):
    width = grad.shape[-1]
    upstream = grad[...]
    grad_heads = mxu(upstream, output[...], NT).astype(bf16)
    for g in range(width // 128):
        here = slice(g * 128, (g + 1) * 128)
        query = triple[:, g * 128 : (g + 1) * 128]
        value = triple[:, 2 * width + g * 128 : 2 * width + (g + 1) * 128]
        arriving = grad_heads[:, here]
        product = mxu(stacked(value), arriving, NT)
        shares = weights[g * GROUP * WIN : (g + 1) * GROUP * WIN, :]
        grad_value = mxu(shares, arriving)
        slopes = []
        for h in range(GROUP):
            head = g * GROUP + h
            share = shares[h * WIN : (h + 1) * WIN].astype(f32)
            change = product[h * WIN : (h + 1) * WIN]
            level = jnp.sum(share * change, axis=0, keepdims=True)
            slope = (share * (change - level) * HEAD ** (-0.5)).astype(bf16)
            at = slice(head * HEAD, (head + 1) * HEAD)
            queries_t[at, :] = mxu(keys_t[at, :], slope)
            slopes.append(slope)
        grad_key = mxu(jnp.concatenate(slopes, axis=0), query)
        split = [slice(h * WIN, (h + 1) * WIN) for h in range(GROUP)]
        joined[:, width + g * 128 : width + (g + 1) * 128] = lanes_of([grad_key[s] for s in split]).astype(bf16)
        joined[:, 2 * width + g * 128 : 2 * width + (g + 1) * 128] = lanes_of(
            [grad_value[s] for s in split]
        ).astype(bf16)
    joined[:, :width] = queries_t[...].T.astype(bf16)


def backward(grad, weights, triple, keys_t, output):
    width = grad.shape[-1]
    return pl.pallas_call(
        backward_kernel,
        out_shape=shape((WIN, 3 * width), bf16),
        scratch_shapes=[pltpu.VMEM((width, WIN), f32)],
        compiler_params=params(),
        cost_estimate=cost(10**10, 2 * 10**7),
        name="backward",
    )(grad, weights, triple, keys_t, output)


def finish_kernel(grad, joined, tokens, packed, gain, own, lat, lon, both):
    grad_inputs = mxu(joined[...], packed[...], NT).astype(bf16)
    unit, scale = unit_rows(tokens[...].astype(f32))
    scaled = grad_inputs.astype(f32) * gain[...].reshape(1, -1)
    out = grad[...].astype(f32) + scale * (scaled - row_mean(scaled) - unit * row_mean(scaled * unit))
    for quad, piece in enumerate((own, lat, lon, both)):
        piece[...] = quadrant(out, quad).astype(bf16)


def finish(grad, joined, tokens, packed, gain):
    width = grad.shape[-1]
    return pl.pallas_call(
        finish_kernel,
        out_shape=[shape((QUAD, width), bf16)] * 4,
        compiler_params=params(),
        cost_estimate=cost(10**9, 2 * 10**6),
        name="finish",
    )(grad, joined, tokens, packed, gain)


def unpack_kernel(own, lat, lon, both, same_here, other_here, same_next, other_next, merged, tokens):
    width = own.shape[-1]
    quads = [piece[...].astype(f32) for piece in (own, lat, lon, both)]
    for line in range(WLAT):
        for column in range(WLON):
            quad = (0 if line >= HALF_LAT else 1) + (0 if column >= HALF_LON else 2)
            inner = column % HALF_LON
            at = token_row(0, line % HALF_LAT, inner % 2, inner // 2)
            tokens[line, column] = quads[quad][at : at + LEVELS].astype(bf16)
    upper = lax.axis_index("lev") == 1
    same = (same_here[...].astype(f32), same_next[...].astype(f32))
    other = (other_here[...].astype(f32), other_next[...].astype(f32))
    low = [jnp.where(upper, b, a) for a, b in zip(same, other)]
    high = [jnp.where(upper, a, b) for a, b in zip(same, other)]
    for row, odd, below, inner in cell_places():
        for pair in range(PAIRS):
            for side in range(2):
                block = side * 2 + odd
                at = token_row(0, inner, side, pair)
                here = slice(at, at + LEVELS)
                merged[row, pair, :, block * width : (block + 1) * width] = jnp.concatenate(
                    (low[below][here], high[below][here]), axis=0
                ).astype(bf16)


def unpack_pieces(token_pieces, cell_pieces):
    width = token_pieces[0].shape[-1]
    return pl.pallas_call(
        unpack_kernel,
        out_shape=[
            shape((HALF_LAT, PAIRS, 2 * LEVELS, 4 * width), bf16),
            shape((WLAT, WLON, LEVELS, width), bf16),
        ],
        compiler_params=params(),
        name="unpack",
    )(*token_pieces, *cell_pieces)


def routes(sizes, target):
    lons, lats, levs = sizes

    def number(i, a, k):
        return ((i % lons) * lats + a % lats) * levs + k % levs

    return [
        (number(i, a, k), number(*target(i, a, k)))
        for i in range(lons)
        for a in range(lats)
        for k in range(levs)
    ]


def send(block, sizes, target, back=False):
    pairs = routes(sizes, target)
    if back:
        pairs = [(b, a) for a, b in pairs]
    return lax.ppermute(block, ("lon", "lat", "lev"), pairs)


FIRST = lambda i, a, k: (i - (1 - k), a - 1, k)
SECOND = lambda i, a, k: (i - k, a - 1, k)
THIRD = lambda i, a, k: (i - 1, a, k)
FOURTH = lambda i, a, k: (i - (1 - k), a, 1 - k)
FIFTH = lambda i, a, k: (i - (1 - k), a - 1, 1 - k)
LAT = lambda i, a, k: (i, a - 1, k)
LON = lambda i, a, k: (i - 1, a, k)
BOTH = lambda i, a, k: (i - 1, a - 1, k)
HERE = lambda i, a, k: (i - (1 - k), a, k)


def per_device(
    sizes,
    tokens,
    packed_weight,
    output_weight,
    norm_gain,
    merge_gain,
    bias_table,
    bias_index,
    row_labels,
    column_valid,
    merged_grad,
):
    own, first, second, third, kept, fourth, fifth = pack_pieces(
        tokens.transpose(1, 2, 0, 3), merged_grad.transpose(1, 2, 0, 3)
    )
    first = send(first, sizes, FIRST)
    second = send(second, sizes, SECOND)
    third = send(third, sizes, THIRD)
    fourth = send(fourth, sizes, FOURTH)
    fifth = send(fifth, sizes, FIFTH)
    main, tail = window_bias(bias_table, bias_index, row_labels, column_valid)
    cell_gain = merge_gain.reshape(1, -1)
    weights, triple, keys_t, residual, data = forward(
        (own, first, second, third), packed_weight, output_weight, norm_gain, main, tail
    )
    scaled, moments, sent = cell_moments(residual, (kept, first, third, fourth, fifth), cell_gain)
    before = send(sent, sizes, lambda i, a, k: (i, a + 1, k))
    after = before if sizes[1] == 2 else send(sent, sizes, lambda i, a, k: (i, a - 1, k))
    kept, below, right, far, grad = merge_back(residual, scaled, moments, before, after, cell_gain)
    below = send(below, sizes, FIRST, True)
    far = send(far, sizes, FIFTH, True)
    right = send(right, sizes, FOURTH, True)
    kept = send(kept, sizes, HERE, True)
    joined = backward(grad, weights, triple, keys_t, output_weight)
    own, lat, lon, both = finish(grad, joined, data, packed_weight, norm_gain)
    lat, lon, both, kept, below, right, far = lax.optimization_barrier((lat, lon, both, kept, below, right, far))
    lat = send(lat, sizes, LAT, True)
    both = send(both, sizes, BOTH, True)
    lon = send(lon, sizes, LON, True)
    merged, grads = unpack_pieces((own, lat, lon, both), (kept, right, below, far))
    return merged.transpose(2, 0, 1, 3), grads.transpose(2, 0, 1, 3)


def solution(mesh):
    sizes = tuple(mesh.shape[name] for name in ("lon", "lat", "lev"))
    placed = (
        P("lev", "lat", "lon", None),
        P(),
        P(),
        P(),
        P(),
        P("lev", "lat", None, None),
        P(),
        P("lat"),
        P(),
        P(None, "lat", ("lon", "lev"), None),
    )
    return jax.shard_map(
        functools.partial(per_device, sizes),
        mesh=mesh,
        in_specs=placed,
        out_specs=(P(None, "lat", ("lon", "lev"), None), P("lev", "lat", "lon", None)),
        check_vma=False,
    )
```

```python
import functools

import jax
import jax.numpy as jnp
from jax import lax
from jax.experimental import pallas as pl
from jax.experimental.pallas import tpu as pltpu
from jax.sharding import PartitionSpec as P

HEADS = 24
HEAD = 32
WLAT = 6
WLON = 12
HALF_LAT = WLAT // 2
HALF_LON = WLON // 2
LEVELS = 2
WIN = LEVELS * WLAT * WLON
QUAD = WIN // 4
PAIRS = HALF_LON // 2
CELLS = LEVELS * PAIRS
GROUP = 128 // HEAD
TAIL = WIN - 128
TAIL_GROUPS = WIN // 8
BLOCKED = -1e30

epsilon = 1e-05
f32 = jnp.float32
bf16 = jnp.bfloat16

NN = (((1,), (0,)), ((), ()))
NT = (((1,), (1,)), ((), ()))


def token_row(quad, row, side, pair):
    return quad * QUAD + ((row * 2 + side) * PAIRS + pair) * LEVELS


def split_tokens(t):
    def digit(rest, size, count):
        found = jnp.zeros_like(rest)
        for i in range(1, count):
            found = found + (rest >= i * size).astype(jnp.int32)
        return found, rest - found * size

    quad, rest = digit(t, QUAD, 4)
    row, rest = digit(rest, 2 * CELLS, HALF_LAT)
    side, rest = digit(rest, CELLS, 2)
    pair, level = digit(rest, LEVELS, PAIRS)
    right, below = digit(quad, 2, 2)
    row = row + HALF_LAT * below
    column = right * HALF_LON + 2 * pair + side
    return row, column, level, right


def token_places(dims, axis):
    return split_tokens(lax.broadcasted_iota(jnp.int32, dims, axis))


def mxu(a, b, dims=NN):
    return lax.dot_general(a, b, dims, preferred_element_type=f32)


def exact(a, b):
    return lax.dot_general(a, b, NN, precision=lax.Precision.HIGHEST, preferred_element_type=f32)


def params(megabytes=12):
    return pltpu.CompilerParams(vmem_limit_bytes=megabytes << 20)


def shape(dims, dtype):
    return jax.ShapeDtypeStruct(dims, dtype)


def cost(flops, nbytes):
    return pl.CostEstimate(flops=flops, bytes_accessed=nbytes, transcendentals=0)


def in_hbm(*arrays):
    return [pltpu.with_memory_space_constraint(x, pltpu.MemorySpace.HBM) for x in arrays]


def start_copies(done, *pairs):
    copies = [pltpu.make_async_copy(source, target, done.at[i]) for i, (source, target) in enumerate(pairs)]
    for copy in copies:
        copy.start()
    return copies


def quadrant(values, quad):
    return values[quad * QUAD : (quad + 1) * QUAD]


def cell_places():
    return [(0, 0, True, 0), (0, 1, True, 1), (1, 0, True, 2), (1, 1, False, 0), (2, 0, False, 1), (2, 1, False, 2)]


def pack_kernel(
    tokens_at, grad_at, own, first, second, third, kept, fourth, fifth, tokens, grad, rows, cells, done
):
    width = tokens.shape[-1]
    copies = start_copies(done, (tokens_at, tokens), (grad_at, grad))
    copies[0].wait()
    for line in range(WLAT):
        for column in range(WLON):
            quad = (0 if line >= HALF_LAT else 1) + (0 if column >= HALF_LON else 2)
            inner = column % HALF_LON
            at = token_row(quad, line % HALF_LAT, inner % 2, inner // 2)
            rows[at : at + LEVELS, :] = tokens[line, column].astype(f32)
    copies[1].wait()
    upper = lax.axis_index("lev") == 1
    for row, odd, below, inner in cell_places():
        for pair in range(PAIRS):
            for side in range(2):
                block = side * 2 + odd
                part = grad[row, pair, :, block * width : (block + 1) * width].astype(f32)
                low, high = part[:LEVELS], part[LEVELS:]
                at = token_row(int(below), inner, side, pair)
                cells[at : at + LEVELS, :] = jnp.where(upper, high, low)
                at = at + 2 * QUAD
                cells[at : at + LEVELS, :] = jnp.where(upper, low, high)
    data, grads = rows[...], cells[...]
    lat, lon, both = quadrant(data, 1), quadrant(data, 2), quadrant(data, 3)
    here, below = quadrant(grads, 0), quadrant(grads, 1)
    own[...] = quadrant(data, 0).astype(bf16)
    first[...] = jnp.concatenate((jnp.where(upper, lat, both), below), axis=0).astype(bf16)
    second[...] = jnp.where(upper, both, lat).astype(bf16)
    third[...] = jnp.concatenate((lon, here), axis=0).astype(bf16)
    kept[...] = here.astype(bf16)
    fourth[...] = quadrant(grads, 2).astype(bf16)
    fifth[...] = quadrant(grads, 3).astype(bf16)


def pack_pieces(tokens, grad):
    width = tokens.shape[-1]
    piece, double = shape((QUAD, width), bf16), shape((2 * QUAD, width), bf16)
    return pl.pallas_call(
        pack_kernel,
        out_shape=[piece, double, piece, double, piece, piece, piece],
        in_specs=[pl.BlockSpec(memory_space=pltpu.MemorySpace.HBM)] * 2,
        scratch_shapes=[
            pltpu.VMEM(tokens.shape, bf16),
            pltpu.VMEM(grad.shape, bf16),
            pltpu.VMEM((WIN, width), f32),
            pltpu.VMEM((WIN, width), f32),
            pltpu.SemaphoreType.DMA((2,)),
        ],
        compiler_params=params(),
        name="pack",
    )(*in_hbm(tokens, grad))


def bias_kernel(
    table_at, index_at, labels_at, valid_at, main, tail,
    table, index, labels, valid, split, fine, high, low, fine_high, fine_low, rest_rows, mask, mask_tail, done,
):
    copies = start_copies(
        done, (table_at.at[0, 0], table), (index_at, index), (labels_at, labels), (valid_at, valid)
    )
    row_k, column_k, level_k, _ = token_places((WIN, 1), 0)
    row_q, _, _, _ = token_places((1, WIN), 1)
    natural = (level_k * WLAT + row_k) * WLON + column_k
    columns = lax.broadcasted_iota(jnp.int32, (WIN, WIN), 1)
    rows = lax.broadcasted_iota(jnp.int32, (WIN, WIN), 0)
    permute = jnp.where(natural == columns, 1.0, 0.0).astype(bf16)
    for copy in copies:
        copy.wait()

    label_q, label_k = jnp.zeros_like(row_q), jnp.zeros_like(row_k)
    for r in range(WLAT):
        label_q = jnp.where(row_q == r, labels[r], label_q)
        label_k = jnp.where(row_k == r, labels[r], label_k)
    valid_k = jnp.zeros_like(column_k)
    start = lax.axis_index("lon") * WLON + HALF_LON
    total = valid.shape[0]
    for c in range(WLON):
        at = start + c
        at = jnp.where(at >= total, at - total, at)
        valid_k = jnp.where(column_k == c, valid[at], valid_k)
    seen = (label_k == label_q) & ((valid_k > 0) | (rows == columns))
    added = jnp.where(seen, 0.0, BLOCKED).astype(f32)
    mask[...] = added[:, :128]
    mask_tail[...] = jnp.concatenate((added[:, 128:], jnp.zeros((WIN, 128 - TAIL), f32)), axis=1)

    heads, entries = table.shape
    gathered = 8
    wide = heads - gathered
    chunks = (entries + 255) // 256
    small_chunks = (entries + 127) // 128
    for c in range(small_chunks):
        size = min(128, entries - c * 128)
        part = table[wide:, c * 128 : c * 128 + size]
        if size < 128:
            part = jnp.concatenate((part, jnp.zeros((gathered, 128 - size), f32)), axis=1)
        fine[:, c * 128 : (c + 1) * 128] = part
    for c in range(chunks):
        size = min(256, entries - c * 256)
        part = table[:wide, c * 256 : c * 256 + size]
        if size < 256:
            part = jnp.concatenate((part, jnp.zeros((wide, 256 - size), f32)), axis=1)
        coarse = part.astype(bf16).astype(f32)
        split[c * wide : (c + 1) * wide, :] = coarse
        split[(chunks + c) * wide : (chunks + c + 1) * wide, :] = part - coarse
    source = split[...].astype(bf16)
    part_rows = chunks * wide

    def place(values, out):
        moved = mxu(mxu(permute, values.astype(f32).astype(bf16), NT).astype(bf16), permute, NT)
        out[0:WIN, :] = moved[:, :128]
        rest_rows[...] = jnp.concatenate((moved[:, 128:], jnp.zeros((WIN, 128 - TAIL), f32)), axis=1)
        total = None
        for g in range(8):
            piece = rest_rows[pl.ds(g, TAIL_GROUPS, stride=8), :]
            if g:
                piece = pltpu.roll(piece, TAIL * g, 1)
            total = piece if total is None else total + piece
        out[WIN : WIN + TAIL_GROUPS, :] = total

    entry = index[...]
    place(lax.shift_right_logical(entry, 8), high)
    place(entry & 255, low)
    upper, lower = high[...], low[...]
    far = lower >= 128.0
    fine_high[...] = (2.0 * upper + jnp.where(far, 1.0, 0.0)).astype(jnp.int32)
    fine_low[...] = jnp.where(far, lower - 128.0, lower).astype(jnp.int32)
    depth = lax.broadcasted_iota(jnp.int32, (256, 128), 0).astype(f32).astype(bf16)
    one, zero = jnp.ones((), bf16), jnp.zeros((), bf16)

    def lookup(row):
        hot = []
        for j in range(2):
            lane = jnp.broadcast_to(low[pl.ds(row + j, 1), :], (16, 128)).astype(bf16)
            hot.append(jnp.where(depth == jnp.concatenate([lane] * 16, axis=0), one, zero))
        product = mxu(source, jnp.concatenate(hot, axis=1))
        out = []
        for j in range(2):
            here = slice(j * 128, (j + 1) * 128)
            chunk = jnp.broadcast_to(high[pl.ds(row + j, 1), :], (8, 128))
            coarse, rest = [None] * (wide // 8), [None] * (wide // 8)
            for c in range(chunks):
                hit = chunk == c
                for block in range(wide // 8):
                    at = c * wide + block * 8
                    a = product[at : at + 8, here]
                    b = product[part_rows + at : part_rows + at + 8, here]
                    coarse[block] = a if c == 0 else jnp.where(hit, a, coarse[block])
                    rest[block] = b if c == 0 else jnp.where(hit, b, rest[block])
            found = [a + b for a, b in zip(coarse, rest)]
            chunk = jnp.broadcast_to(fine_high[pl.ds(row + j, 1), :], (8, 128))
            lane = jnp.broadcast_to(fine_low[pl.ds(row + j, 1), :], (8, 128))
            value = None
            for c in range(small_chunks):
                a = jnp.take_along_axis(fine[:, c * 128 : (c + 1) * 128], lane, axis=1, mode="promise_in_bounds")
                value = a if c == 0 else jnp.where(chunk == c, a, value)
            found.append(value)
            out.append(found)
        return out

    for key in range(0, WIN, 2):
        for j, found in enumerate(lookup(key)):
            extra = jnp.broadcast_to(mask[key + j : key + j + 1, :], (8, 128))
            for block, value in enumerate(found):
                main[pl.ds(block * 8 * WIN + key + j, 8, stride=WIN), :] = value + extra
    for row in range(0, TAIL_GROUPS, 2):
        for j, found in enumerate(lookup(WIN + row)):
            for block, value in enumerate(found):
                for g in range(8):
                    key = (row + j) * 8 + g
                    moved = pltpu.roll(value, 128 - TAIL * g, 1) if g else value
                    extra = jnp.broadcast_to(mask_tail[key : key + 1, :], (8, 128))
                    tail[pl.ds(block * 8 * WIN + key, 8, stride=WIN), :] = moved + extra


def window_bias(table, index, labels, valid):
    heads, entries = table.shape[-2:]
    whole = (entries + 255) // 256
    index_rows = WIN + TAIL_GROUPS
    return pl.pallas_call(
        bias_kernel,
        out_shape=[shape((heads * WIN, 128), f32)] * 2,
        in_specs=[pl.BlockSpec(memory_space=pltpu.MemorySpace.HBM)] * 4,
        scratch_shapes=[
            pltpu.VMEM((heads, entries), f32),
            pltpu.VMEM(index.shape, jnp.int32),
            pltpu.SMEM(labels.shape, jnp.int32),
            pltpu.SMEM(valid.shape, jnp.int32),
            pltpu.VMEM((2 * whole * (heads - 8), 256), f32),
            pltpu.VMEM((8, (entries + 127) // 128 * 128), f32),
            pltpu.VMEM((index_rows, 128), f32),
            pltpu.VMEM((index_rows, 128), f32),
            pltpu.VMEM((index_rows, 128), jnp.int32),
            pltpu.VMEM((index_rows, 128), jnp.int32),
            pltpu.VMEM((WIN, 128), f32),
            pltpu.VMEM((WIN, 128), f32),
            pltpu.VMEM((WIN, 128), f32),
            pltpu.SemaphoreType.DMA((4,)),
        ],
        compiler_params=params(),
        cost_estimate=cost(10**10, 2 * 10**7),
        name="bias",
    )(*in_hbm(table, index, labels, valid))


def row_mean(values):
    return jnp.mean(values, axis=-1, keepdims=True)


def unit_rows(data):
    center = data - row_mean(data)
    scale = lax.rsqrt(row_mean(center * center) + epsilon)
    return center * scale, scale


def stacked(block):
    lane = lax.broadcasted_iota(jnp.int32, (1, 128), 1) // HEAD
    return jnp.concatenate(
        [jnp.where(lane == h, block, jnp.zeros((), block.dtype)) for h in range(GROUP)], axis=0
    )


def lanes_of(parts):
    lane = lax.broadcasted_iota(jnp.int32, (1, 128), 1) // HEAD
    out = parts[0]
    for h in range(1, GROUP):
        out = jnp.where(lane == h, parts[h], out)
    return out


def forward_kernel(
    own, first, second, third, packed, output, gain, main, tail,
    weights, triple, keys_t, residual, tokens,
    gathered, values_t, heads_t,
):
    width = own.shape[-1]
    upper = lax.axis_index("lev") == 1
    a, b = first[...].astype(f32)[:QUAD], second[...].astype(f32)
    lon = third[...].astype(f32)[:QUAD]
    for quad, piece in enumerate((own[...].astype(f32), jnp.where(upper, a, b), lon, jnp.where(upper, b, a))):
        gathered[quad * QUAD : (quad + 1) * QUAD, :] = piece
    data = gathered[...]
    tokens[...] = data.astype(bf16)
    unit, _ = unit_rows(data)
    normed = (unit * gain[...].reshape(1, -1)).astype(bf16)
    triple[...] = mxu(normed, packed[...]).astype(bf16)
    keys_t[...] = triple[:, width : 2 * width].astype(f32).T.astype(bf16)
    values_t[...] = triple[:, 2 * width :].astype(f32).T.astype(bf16)
    for g in range(width // 128):
        query = triple[:, g * 128 : (g + 1) * 128]
        key = triple[:, width + g * 128 : width + (g + 1) * 128]
        product = mxu(stacked(key), query, NT) * HEAD ** (-0.5)
        for h in range(GROUP):
            head = g * GROUP + h
            at = slice(head * WIN, (head + 1) * WIN)
            bias = jnp.concatenate((main[at, :], tail[at, :TAIL]), axis=1)
            scores = product[h * WIN : (h + 1) * WIN] + bias
            raised = jnp.exp(scores - jnp.max(scores, axis=0, keepdims=True))
            share = (raised * (1.0 / jnp.sum(raised, axis=0, keepdims=True))).astype(bf16)
            weights[at, :] = share
            here = slice(head * HEAD, (head + 1) * HEAD)
            heads_t[here, :] = mxu(values_t[here, :], share)
    heads = heads_t[...].T.astype(bf16)
    attended = mxu(heads, output[...]).astype(bf16)
    residual[...] = (data + attended.astype(f32)).astype(bf16)


def forward(pieces, packed, output, gain, main, tail):
    width = output.shape[0]
    return pl.pallas_call(
        forward_kernel,
        out_shape=[
            shape((HEADS * WIN, WIN), bf16),
            shape((WIN, 3 * width), bf16),
            shape((width, WIN), bf16),
            shape((WIN, width), bf16),
            shape((WIN, width), bf16),
        ],
        scratch_shapes=[
            pltpu.VMEM((WIN, width), f32),
            pltpu.VMEM((width, WIN), bf16),
            pltpu.VMEM((width, WIN), f32),
        ],
        compiler_params=params(),
        cost_estimate=cost(10**9, 2 * 10**7),
        name="forward",
    )(*pieces, packed, output, gain, main, tail)


def gain_rows(gain, out):
    width = out.shape[-1]
    for quad in range(4):
        for row in range(HALF_LAT):
            odd = 1 - (row + (quad & 1) * HALF_LAT) % 2
            for side in range(2):
                block = side * 2 + odd
                at = token_row(quad, row, side, 0)
                factor = gain[:, block * width : (block + 1) * width]
                out[at : at + CELLS, :] = jnp.broadcast_to(factor, (CELLS, width))


def cell_number(places):
    row, column, level, right = places
    band = lax.shift_right_logical(row + 1, 1)
    return (band * HALF_LON + lax.shift_right_logical(column, 1)) * LEVELS + level


def split_row(places):
    return (places[0] == 0) | (places[0] == WLAT - 1)


def sent_tokens(dims, axis):
    i = lax.broadcasted_iota(jnp.int32, dims, axis)
    last = (i >= 2 * CELLS).astype(jnp.int32)
    i = i - last * 2 * CELLS
    right = (i >= CELLS).astype(jnp.int32)
    cell = i - right * CELLS
    return (2 * right + last) * QUAD + last * (HALF_LAT - 1) * 2 * CELLS + cell


def columns_of(parts):
    lane = lax.broadcasted_iota(jnp.int32, (1, 128), 1)
    out = jnp.zeros((WIN, 128), f32)
    for i, part in enumerate(parts):
        out = jnp.where(lane == i, part, out)
    return out


def moments_kernel(residual, kept, first, third, fourth, fifth, gain, scaled, moments, sent, factors):
    width = residual.shape[-1]
    upper = lax.axis_index("lev") == 1
    own, a, b = kept[...].astype(f32), fourth[...].astype(f32), fifth[...].astype(f32)
    below, right = first[...].astype(f32)[QUAD:], third[...].astype(f32)[QUAD:]
    gain_rows(gain, factors)
    for quad, part in enumerate((
        jnp.where(upper, own, a),
        jnp.where(upper, below, b),
        jnp.where(upper, a, right),
        jnp.where(upper, b, below),
    )):
        scaled[quad * QUAD : (quad + 1) * QUAD, :] = part
    grad = scaled[...] * factors[...]
    scaled[...] = grad
    data = residual[...].astype(f32)
    down = token_places((WIN, 1), 0)
    grouping = jnp.where(cell_number(down) == cell_number(token_places((1, WIN), 1)), 1.0, 0.0).astype(f32)
    inverse = jnp.where(split_row(down), 1 / (2 * width), 1 / (4 * width)).astype(f32)
    total = jnp.sum(data, axis=-1, keepdims=True)
    middle = exact(grouping, jnp.broadcast_to(total, (WIN, 128)))[:, 0:1] * inverse
    center = data - middle
    sums = columns_of((
        jnp.sum(center * center, axis=-1, keepdims=True),
        jnp.sum(grad, axis=-1, keepdims=True),
        jnp.sum(grad * center, axis=-1, keepdims=True),
    ))
    sums = exact(grouping, sums)
    lane = lax.broadcasted_iota(jnp.int32, (1, 128), 1)
    sums = jnp.where(lane == 3, middle, sums)
    moments[...] = sums
    pick = sent_tokens((4 * CELLS, 1), 0) == lax.broadcasted_iota(jnp.int32, (4 * CELLS, WIN), 1)
    sent[...] = exact(jnp.where(pick, 1.0, 0.0).astype(f32), sums)


def cell_moments(residual, pieces, gain):
    width = residual.shape[-1]
    return pl.pallas_call(
        moments_kernel,
        out_shape=[shape((WIN, width), f32), shape((WIN, 128), f32), shape((4 * CELLS, 128), f32)],
        scratch_shapes=[pltpu.VMEM((WIN, width), f32)],
        compiler_params=params(),
        cost_estimate=cost(10**8, 10**6),
        name="moments",
    )(residual, *pieces, gain)


def merge_kernel(residual, scaled, moments, before, after, gain, near, over, grad, factors):
    width = residual.shape[-1]
    upper = lax.axis_index("lev") == 1
    gain_rows(gain, factors)
    down = token_places((WIN, 1), 0)
    shared = split_row(down)
    row = down[0]
    sender = split_tokens(sent_tokens((1, 4 * CELLS), 1))
    match = (cell_number(down) == cell_number(sender)) & shared
    there = jnp.concatenate((before[2 * CELLS :], after[: 2 * CELLS]), axis=0)
    theirs = exact(jnp.where(match, 1.0, 0.0).astype(f32), there)
    mine = moments[...]
    full = 4.0 * width
    middle = jnp.where(shared, 0.5 * (mine[:, 3:4] + theirs[:, 3:4]), mine[:, 3:4])
    gap = theirs[:, 3:4] - mine[:, 3:4]
    square = jnp.where(shared, mine[:, 0:1] + theirs[:, 0:1] + gap * gap * width, mine[:, 0:1])
    scale = lax.rsqrt(square / full + epsilon)
    grad_sum = jnp.where(shared, mine[:, 1:2] + theirs[:, 1:2], mine[:, 1:2])
    cross = jnp.where(
        shared,
        mine[:, 2:3] + (mine[:, 3:4] - middle) * mine[:, 1:2]
        + theirs[:, 2:3] + (theirs[:, 3:4] - middle) * theirs[:, 1:2],
        mine[:, 2:3],
    )
    unit = (residual[...].astype(f32) - middle) * scale
    grad[...] = (scale * (scaled[...] - grad_sum / full - unit * (cross * scale / full))).astype(bf16)
    out = unit * factors[...]
    parts = [quadrant(out, quad) for quad in range(4)]
    left, right = jnp.concatenate(parts[:2], axis=0), jnp.concatenate(parts[2:], axis=0)
    near[...] = jnp.where(upper, left, right).astype(bf16)
    over[...] = jnp.where(upper, right, left).astype(bf16)


def merge_back(residual, scaled, moments, before, after, gain):
    width = residual.shape[-1]
    piece = shape((2 * QUAD, width), bf16)
    return pl.pallas_call(
        merge_kernel,
        out_shape=[piece] * 2 + [shape((WIN, width), bf16)],
        scratch_shapes=[pltpu.VMEM((WIN, width), f32)],
        compiler_params=params(),
        cost_estimate=cost(10**8, 10**6),
        name="merge",
    )(residual, scaled, moments, before, after, gain)


def backward_kernel(grad, weights, triple, keys_t, output, joined, queries_t):
    width = grad.shape[-1]
    upstream = grad[...]
    grad_heads = mxu(upstream, output[...], NT).astype(bf16)
    for g in range(width // 128):
        here = slice(g * 128, (g + 1) * 128)
        query = triple[:, g * 128 : (g + 1) * 128]
        value = triple[:, 2 * width + g * 128 : 2 * width + (g + 1) * 128]
        arriving = grad_heads[:, here]
        product = mxu(stacked(value), arriving, NT)
        shares = weights[g * GROUP * WIN : (g + 1) * GROUP * WIN, :]
        grad_value = mxu(shares, arriving)
        slopes = []
        for h in range(GROUP):
            head = g * GROUP + h
            share = shares[h * WIN : (h + 1) * WIN].astype(f32)
            change = product[h * WIN : (h + 1) * WIN]
            level = jnp.sum(share * change, axis=0, keepdims=True)
            slope = (share * (change - level) * HEAD ** (-0.5)).astype(bf16)
            at = slice(head * HEAD, (head + 1) * HEAD)
            queries_t[at, :] = mxu(keys_t[at, :], slope)
            slopes.append(slope)
        grad_key = mxu(jnp.concatenate(slopes, axis=0), query)
        split = [slice(h * WIN, (h + 1) * WIN) for h in range(GROUP)]
        joined[:, width + g * 128 : width + (g + 1) * 128] = lanes_of([grad_key[s] for s in split]).astype(bf16)
        joined[:, 2 * width + g * 128 : 2 * width + (g + 1) * 128] = lanes_of(
            [grad_value[s] for s in split]
        ).astype(bf16)
    joined[:, :width] = queries_t[...].T.astype(bf16)


def backward(grad, weights, triple, keys_t, output):
    width = grad.shape[-1]
    return pl.pallas_call(
        backward_kernel,
        out_shape=shape((WIN, 3 * width), bf16),
        scratch_shapes=[pltpu.VMEM((width, WIN), f32)],
        compiler_params=params(),
        cost_estimate=cost(10**10, 2 * 10**7),
        name="backward",
    )(grad, weights, triple, keys_t, output)


def finish_kernel(grad, joined, tokens, packed, gain, own, lat, lon, both):
    grad_inputs = mxu(joined[...], packed[...], NT).astype(bf16)
    unit, scale = unit_rows(tokens[...].astype(f32))
    scaled = grad_inputs.astype(f32) * gain[...].reshape(1, -1)
    out = grad[...].astype(f32) + scale * (scaled - row_mean(scaled) - unit * row_mean(scaled * unit))
    for quad, piece in enumerate((own, lat, lon, both)):
        piece[...] = quadrant(out, quad).astype(bf16)


def finish(grad, joined, tokens, packed, gain):
    width = grad.shape[-1]
    return pl.pallas_call(
        finish_kernel,
        out_shape=[shape((QUAD, width), bf16)] * 4,
        compiler_params=params(),
        cost_estimate=cost(10**10, 2 * 10**6),
        name="finish",
    )(grad, joined, tokens, packed, gain)


def relay_kernel(near, cross, out):
    out[...] = jnp.concatenate((near[...].astype(f32)[QUAD:], cross[...].astype(f32)[QUAD:]), axis=0).astype(bf16)


def relay(near, cross):
    return pl.pallas_call(
        relay_kernel,
        out_shape=shape(near.shape, bf16),
        compiler_params=params(),
        name="relay",
    )(near, cross)


def token_kernel(own, lat, lon, both, tokens):
    quads = [piece[...].astype(f32) for piece in (own, lat, lon, both)]
    for line in range(WLAT):
        for column in range(WLON):
            quad = (0 if line >= HALF_LAT else 1) + (0 if column >= HALF_LON else 2)
            inner = column % HALF_LON
            at = token_row(0, line % HALF_LAT, inner % 2, inner // 2)
            tokens[line, column] = quads[quad][at : at + LEVELS].astype(bf16)


def unpack_tokens(*pieces):
    width = pieces[0].shape[-1]
    return pl.pallas_call(
        token_kernel,
        out_shape=shape((WLAT, WLON, LEVELS, width), bf16),
        compiler_params=params(),
        name="unpack_tokens",
    )(*pieces)


def cell_kernel(near, cross, onward, merged):
    width = near.shape[-1]
    upper = lax.axis_index("lev") == 1
    arrived = onward[...].astype(f32)
    same = (near[...].astype(f32)[:QUAD], arrived[:QUAD])
    other = (cross[...].astype(f32)[:QUAD], arrived[QUAD:])
    low = [jnp.where(upper, b, a) for a, b in zip(same, other)]
    high = [jnp.where(upper, a, b) for a, b in zip(same, other)]
    for row, odd, below, inner in cell_places():
        for pair in range(PAIRS):
            for side in range(2):
                block = side * 2 + odd
                at = token_row(0, inner, side, pair)
                here = slice(at, at + LEVELS)
                merged[row, pair, :, block * width : (block + 1) * width] = jnp.concatenate(
                    (low[below][here], high[below][here]), axis=0
                ).astype(bf16)


def unpack_cells(near, cross, onward):
    width = near.shape[-1]
    return pl.pallas_call(
        cell_kernel,
        out_shape=shape((HALF_LAT, PAIRS, 2 * LEVELS, 4 * width), bf16),
        compiler_params=params(),
        cost_estimate=cost(10**9, 10**6),
        name="unpack_cells",
    )(near, cross, onward)


def routes(sizes, target):
    lons, lats, levs = sizes

    def number(i, a, k):
        return ((i % lons) * lats + a % lats) * levs + k % levs

    return [
        (number(i, a, k), number(*target(i, a, k)))
        for i in range(lons)
        for a in range(lats)
        for k in range(levs)
    ]


def send(block, sizes, target, back=False):
    pairs = routes(sizes, target)
    if back:
        pairs = [(b, a) for a, b in pairs]
    return lax.ppermute(block, ("lon", "lat", "lev"), pairs)


FIRST = lambda i, a, k: (i - (1 - k), a - 1, k)
SECOND = lambda i, a, k: (i - k, a - 1, k)
THIRD = lambda i, a, k: (i - 1, a, k)
FOURTH = lambda i, a, k: (i - (1 - k), a, 1 - k)
FIFTH = lambda i, a, k: (i - (1 - k), a - 1, 1 - k)
LAT = lambda i, a, k: (i, a - 1, k)
LON = lambda i, a, k: (i - 1, a, k)
BOTH = lambda i, a, k: (i - 1, a - 1, k)
HERE = lambda i, a, k: (i - (1 - k), a, k)


def per_device(
    sizes,
    tokens,
    packed_weight,
    output_weight,
    norm_gain,
    merge_gain,
    bias_table,
    bias_index,
    row_labels,
    column_valid,
    merged_grad,
):
    own, first, second, third, kept, fourth, fifth = pack_pieces(
        tokens.transpose(1, 2, 0, 3), merged_grad.transpose(1, 2, 0, 3)
    )
    first = send(first, sizes, FIRST)
    second = send(second, sizes, SECOND)
    third = send(third, sizes, THIRD)
    fourth = send(fourth, sizes, FOURTH)
    fifth = send(fifth, sizes, FIFTH)
    main, tail = window_bias(bias_table, bias_index, row_labels, column_valid)
    cell_gain = merge_gain.reshape(1, -1)
    weights, triple, keys_t, residual, data = forward(
        (own, first, second, third), packed_weight, output_weight, norm_gain, main, tail
    )
    scaled, moments, sent = cell_moments(residual, (kept, first, third, fourth, fifth), cell_gain)
    before = send(sent, sizes, lambda i, a, k: (i, a + 1, k))
    after = before if sizes[1] == 2 else send(sent, sizes, lambda i, a, k: (i, a - 1, k))
    near, cross, grad = merge_back(residual, scaled, moments, before, after, cell_gain)
    near = send(near, sizes, HERE, True)
    cross = send(cross, sizes, FOURTH, True)
    joined = backward(grad, weights, triple, keys_t, output_weight)
    joined, near, cross = lax.optimization_barrier((joined, near, cross))
    onward = send(relay(near, cross), sizes, LAT, True)
    own, lat, lon, both = finish(grad, joined, data, packed_weight, norm_gain)
    lat = send(lat, sizes, LAT, True)
    both = send(both, sizes, BOTH, True)
    lon = send(lon, sizes, LON, True)
    merged = unpack_cells(near, cross, onward)
    merged, lat, both, lon = lax.optimization_barrier((merged, lat, both, lon))
    grads = unpack_tokens(own, lat, lon, both)
    return merged.transpose(2, 0, 1, 3), grads.transpose(2, 0, 1, 3)


def solution(mesh):
    sizes = tuple(mesh.shape[name] for name in ("lon", "lat", "lev"))
    placed = (
        P("lev", "lat", "lon", None),
        P(),
        P(),
        P(),
        P(),
        P("lev", "lat", None, None),
        P(),
        P("lat"),
        P(),
        P(None, "lat", ("lon", "lev"), None),
    )
    return jax.shard_map(
        functools.partial(per_device, sizes),
        mesh=mesh,
        in_specs=placed,
        out_specs=(P(None, "lat", ("lon", "lev"), None), P("lev", "lat", "lon", None)),
        check_vma=False,
    )
```

```python
import functools

import jax
import jax.numpy as jnp
from jax import lax
from jax.experimental import pallas as pl
from jax.experimental.pallas import tpu as pltpu
from jax.sharding import PartitionSpec as P

HEADS = 24
HEAD = 32
WLAT = 6
WLON = 12
HALF_LAT = WLAT // 2
HALF_LON = WLON // 2
LEVELS = 2
WIN = LEVELS * WLAT * WLON
QUAD = WIN // 4
PAIRS = HALF_LON // 2
CELLS = LEVELS * PAIRS
GROUP = 128 // HEAD
TAIL = WIN - 128
TAIL_GROUPS = WIN // 8
BLOCKED = -1e30

epsilon = 1e-05
f32 = jnp.float32
bf16 = jnp.bfloat16

NN = (((1,), (0,)), ((), ()))
NT = (((1,), (1,)), ((), ()))


def token_row(quad, row, side, pair):
    return quad * QUAD + ((row * 2 + side) * PAIRS + pair) * LEVELS


def split_tokens(t):
    def digit(rest, size, count):
        found = jnp.zeros_like(rest)
        for i in range(1, count):
            found = found + (rest >= i * size).astype(jnp.int32)
        return found, rest - found * size

    quad, rest = digit(t, QUAD, 4)
    row, rest = digit(rest, 2 * CELLS, HALF_LAT)
    side, rest = digit(rest, CELLS, 2)
    pair, level = digit(rest, LEVELS, PAIRS)
    right, below = digit(quad, 2, 2)
    row = row + HALF_LAT * below
    column = right * HALF_LON + 2 * pair + side
    return row, column, level, right


def token_places(dims, axis):
    return split_tokens(lax.broadcasted_iota(jnp.int32, dims, axis))


def mxu(a, b, dims=NN):
    return lax.dot_general(a, b, dims, preferred_element_type=f32)


def exact(a, b):
    return lax.dot_general(a, b, NN, precision=lax.Precision.HIGHEST, preferred_element_type=f32)


def params(megabytes=12):
    return pltpu.CompilerParams(vmem_limit_bytes=megabytes << 20)


def shape(dims, dtype):
    return jax.ShapeDtypeStruct(dims, dtype)


def cost(flops, nbytes):
    return pl.CostEstimate(flops=flops, bytes_accessed=nbytes, transcendentals=0)


def in_hbm(*arrays):
    return [pltpu.with_memory_space_constraint(x, pltpu.MemorySpace.HBM) for x in arrays]


def start_copies(done, *pairs):
    copies = [pltpu.make_async_copy(source, target, done.at[i]) for i, (source, target) in enumerate(pairs)]
    for copy in copies:
        copy.start()
    return copies


def quadrant(values, quad):
    return values[quad * QUAD : (quad + 1) * QUAD]


def cell_places():
    return [(0, 0, True, 0), (0, 1, True, 1), (1, 0, True, 2), (1, 1, False, 0), (2, 0, False, 1), (2, 1, False, 2)]


def pack_kernel(
    tokens_at, grad_at, own, first, second, third, kept, fourth, fifth, tokens, grad, rows, cells, done
):
    width = tokens.shape[-1]
    copies = start_copies(done, (tokens_at, tokens), (grad_at, grad))
    copies[0].wait()
    for line in range(WLAT):
        for column in range(WLON):
            quad = (0 if line >= HALF_LAT else 1) + (0 if column >= HALF_LON else 2)
            inner = column % HALF_LON
            at = token_row(quad, line % HALF_LAT, inner % 2, inner // 2)
            rows[at : at + LEVELS, :] = tokens[line, column].astype(f32)
    copies[1].wait()
    upper = lax.axis_index("lev") == 1
    for row, odd, below, inner in cell_places():
        for pair in range(PAIRS):
            for side in range(2):
                block = side * 2 + odd
                part = grad[row, pair, :, block * width : (block + 1) * width].astype(f32)
                low, high = part[:LEVELS], part[LEVELS:]
                at = token_row(int(below), inner, side, pair)
                cells[at : at + LEVELS, :] = jnp.where(upper, high, low)
                at = at + 2 * QUAD
                cells[at : at + LEVELS, :] = jnp.where(upper, low, high)
    data, grads = rows[...], cells[...]
    lat, lon, both = quadrant(data, 1), quadrant(data, 2), quadrant(data, 3)
    here, below = quadrant(grads, 0), quadrant(grads, 1)
    own[...] = quadrant(data, 0).astype(bf16)
    first[...] = jnp.concatenate((jnp.where(upper, lat, both), below), axis=0).astype(bf16)
    second[...] = jnp.where(upper, both, lat).astype(bf16)
    third[...] = jnp.concatenate((lon, here), axis=0).astype(bf16)
    kept[...] = here.astype(bf16)
    fourth[...] = quadrant(grads, 2).astype(bf16)
    fifth[...] = quadrant(grads, 3).astype(bf16)


def pack_pieces(tokens, grad):
    width = tokens.shape[-1]
    piece, double = shape((QUAD, width), bf16), shape((2 * QUAD, width), bf16)
    return pl.pallas_call(
        pack_kernel,
        out_shape=[piece, double, piece, double, piece, piece, piece],
        in_specs=[pl.BlockSpec(memory_space=pltpu.MemorySpace.HBM)] * 2,
        scratch_shapes=[
            pltpu.VMEM(tokens.shape, bf16),
            pltpu.VMEM(grad.shape, bf16),
            pltpu.VMEM((WIN, width), f32),
            pltpu.VMEM((WIN, width), f32),
            pltpu.SemaphoreType.DMA((2,)),
        ],
        compiler_params=params(),
        name="pack",
    )(*in_hbm(tokens, grad))


def bias_kernel(
    table_at, index_at, labels_at, valid_at, main, tail,
    table, index, labels, valid, split, fine, high, low, fine_high, fine_low, rest_rows, mask, mask_tail, done,
):
    copies = start_copies(
        done, (table_at.at[0, 0], table), (index_at, index), (labels_at, labels), (valid_at, valid)
    )
    row_k, column_k, level_k, _ = token_places((WIN, 1), 0)
    row_q, _, _, _ = token_places((1, WIN), 1)
    natural = (level_k * WLAT + row_k) * WLON + column_k
    columns = lax.broadcasted_iota(jnp.int32, (WIN, WIN), 1)
    rows = lax.broadcasted_iota(jnp.int32, (WIN, WIN), 0)
    permute = jnp.where(natural == columns, 1.0, 0.0).astype(bf16)
    for copy in copies:
        copy.wait()

    label_q, label_k = jnp.zeros_like(row_q), jnp.zeros_like(row_k)
    for r in range(WLAT):
        label_q = jnp.where(row_q == r, labels[r], label_q)
        label_k = jnp.where(row_k == r, labels[r], label_k)
    valid_k = jnp.zeros_like(column_k)
    start = lax.axis_index("lon") * WLON + HALF_LON
    total = valid.shape[0]
    for c in range(WLON):
        at = start + c
        at = jnp.where(at >= total, at - total, at)
        valid_k = jnp.where(column_k == c, valid[at], valid_k)
    seen = (label_k == label_q) & ((valid_k > 0) | (rows == columns))
    added = jnp.where(seen, 0.0, BLOCKED).astype(f32)
    mask[...] = added[:, :128]
    mask_tail[...] = jnp.concatenate((added[:, 128:], jnp.zeros((WIN, 128 - TAIL), f32)), axis=1)

    heads, entries = table.shape
    gathered = 8
    wide = heads - gathered
    chunks = (entries + 255) // 256
    small_chunks = (entries + 127) // 128
    for c in range(small_chunks):
        size = min(128, entries - c * 128)
        part = table[wide:, c * 128 : c * 128 + size]
        if size < 128:
            part = jnp.concatenate((part, jnp.zeros((gathered, 128 - size), f32)), axis=1)
        fine[:, c * 128 : (c + 1) * 128] = part
    for c in range(chunks):
        size = min(256, entries - c * 256)
        part = table[:wide, c * 256 : c * 256 + size]
        if size < 256:
            part = jnp.concatenate((part, jnp.zeros((wide, 256 - size), f32)), axis=1)
        coarse = part.astype(bf16).astype(f32)
        split[c * wide : (c + 1) * wide, :] = coarse
        split[(chunks + c) * wide : (chunks + c + 1) * wide, :] = part - coarse
    source = split[...].astype(bf16)
    part_rows = chunks * wide

    def place(values, out):
        moved = mxu(mxu(permute, values.astype(f32).astype(bf16), NT).astype(bf16), permute, NT)
        out[0:WIN, :] = moved[:, :128]
        rest_rows[...] = jnp.concatenate((moved[:, 128:], jnp.zeros((WIN, 128 - TAIL), f32)), axis=1)
        total = None
        for g in range(8):
            piece = rest_rows[pl.ds(g, TAIL_GROUPS, stride=8), :]
            if g:
                piece = pltpu.roll(piece, TAIL * g, 1)
            total = piece if total is None else total + piece
        out[WIN : WIN + TAIL_GROUPS, :] = total

    entry = index[...]
    place(lax.shift_right_logical(entry, 8), high)
    place(entry & 255, low)
    upper, lower = high[...], low[...]
    far = lower >= 128.0
    fine_high[...] = (2.0 * upper + jnp.where(far, 1.0, 0.0)).astype(jnp.int32)
    fine_low[...] = jnp.where(far, lower - 128.0, lower).astype(jnp.int32)
    depth = lax.broadcasted_iota(jnp.int32, (256, 128), 0).astype(f32).astype(bf16)
    one, zero = jnp.ones((), bf16), jnp.zeros((), bf16)

    def lookup(row):
        hot = []
        for j in range(2):
            lane = jnp.broadcast_to(low[pl.ds(row + j, 1), :], (16, 128)).astype(bf16)
            hot.append(jnp.where(depth == jnp.concatenate([lane] * 16, axis=0), one, zero))
        product = mxu(source, jnp.concatenate(hot, axis=1))
        out = []
        for j in range(2):
            here = slice(j * 128, (j + 1) * 128)
            chunk = jnp.broadcast_to(high[pl.ds(row + j, 1), :], (8, 128))
            coarse, rest = [None] * (wide // 8), [None] * (wide // 8)
            for c in range(chunks):
                hit = chunk == c
                for block in range(wide // 8):
                    at = c * wide + block * 8
                    a = product[at : at + 8, here]
                    b = product[part_rows + at : part_rows + at + 8, here]
                    coarse[block] = a if c == 0 else jnp.where(hit, a, coarse[block])
                    rest[block] = b if c == 0 else jnp.where(hit, b, rest[block])
            found = [a + b for a, b in zip(coarse, rest)]
            chunk = jnp.broadcast_to(fine_high[pl.ds(row + j, 1), :], (8, 128))
            lane = jnp.broadcast_to(fine_low[pl.ds(row + j, 1), :], (8, 128))
            value = None
            for c in range(small_chunks):
                a = jnp.take_along_axis(fine[:, c * 128 : (c + 1) * 128], lane, axis=1, mode="promise_in_bounds")
                value = a if c == 0 else jnp.where(chunk == c, a, value)
            found.append(value)
            out.append(found)
        return out

    for key in range(0, WIN, 2):
        for j, found in enumerate(lookup(key)):
            extra = jnp.broadcast_to(mask[key + j : key + j + 1, :], (8, 128))
            for block, value in enumerate(found):
                main[pl.ds(block * 8 * WIN + key + j, 8, stride=WIN), :] = value + extra
    for row in range(0, TAIL_GROUPS, 2):
        for j, found in enumerate(lookup(WIN + row)):
            for block, value in enumerate(found):
                for g in range(8):
                    key = (row + j) * 8 + g
                    moved = pltpu.roll(value, 128 - TAIL * g, 1) if g else value
                    extra = jnp.broadcast_to(mask_tail[key : key + 1, :], (8, 128))
                    tail[pl.ds(block * 8 * WIN + key, 8, stride=WIN), :] = moved + extra


def window_bias(table, index, labels, valid):
    heads, entries = table.shape[-2:]
    whole = (entries + 255) // 256
    index_rows = WIN + TAIL_GROUPS
    return pl.pallas_call(
        bias_kernel,
        out_shape=[shape((heads * WIN, 128), f32)] * 2,
        in_specs=[pl.BlockSpec(memory_space=pltpu.MemorySpace.HBM)] * 4,
        scratch_shapes=[
            pltpu.VMEM((heads, entries), f32),
            pltpu.VMEM(index.shape, jnp.int32),
            pltpu.SMEM(labels.shape, jnp.int32),
            pltpu.SMEM(valid.shape, jnp.int32),
            pltpu.VMEM((2 * whole * (heads - 8), 256), f32),
            pltpu.VMEM((8, (entries + 127) // 128 * 128), f32),
            pltpu.VMEM((index_rows, 128), f32),
            pltpu.VMEM((index_rows, 128), f32),
            pltpu.VMEM((index_rows, 128), jnp.int32),
            pltpu.VMEM((index_rows, 128), jnp.int32),
            pltpu.VMEM((WIN, 128), f32),
            pltpu.VMEM((WIN, 128), f32),
            pltpu.VMEM((WIN, 128), f32),
            pltpu.SemaphoreType.DMA((4,)),
        ],
        compiler_params=params(),
        cost_estimate=cost(10**10, 2 * 10**7),
        name="bias",
    )(*in_hbm(table, index, labels, valid))


def row_mean(values):
    return jnp.mean(values, axis=-1, keepdims=True)


def unit_rows(data):
    center = data - row_mean(data)
    scale = lax.rsqrt(row_mean(center * center) + epsilon)
    return center * scale, scale


def stacked(block):
    lane = lax.broadcasted_iota(jnp.int32, (1, 128), 1) // HEAD
    return jnp.concatenate(
        [jnp.where(lane == h, block, jnp.zeros((), block.dtype)) for h in range(GROUP)], axis=0
    )


def lanes_of(parts):
    lane = lax.broadcasted_iota(jnp.int32, (1, 128), 1) // HEAD
    out = parts[0]
    for h in range(1, GROUP):
        out = jnp.where(lane == h, parts[h], out)
    return out


def forward_kernel(
    own, first, second, third, packed, output, gain, main, tail,
    weights, triple, keys_t, residual, tokens,
    gathered, values_t, heads_t,
):
    width = own.shape[-1]
    upper = lax.axis_index("lev") == 1
    a, b = first[...].astype(f32)[:QUAD], second[...].astype(f32)
    lon = third[...].astype(f32)[:QUAD]
    for quad, piece in enumerate((own[...].astype(f32), jnp.where(upper, a, b), lon, jnp.where(upper, b, a))):
        gathered[quad * QUAD : (quad + 1) * QUAD, :] = piece
    data = gathered[...]
    tokens[...] = data.astype(bf16)
    unit, _ = unit_rows(data)
    normed = (unit * gain[...].reshape(1, -1)).astype(bf16)
    triple[...] = mxu(normed, packed[...]).astype(bf16)
    keys_t[...] = triple[:, width : 2 * width].astype(f32).T.astype(bf16)
    values_t[...] = triple[:, 2 * width :].astype(f32).T.astype(bf16)
    for g in range(width // 128):
        query = triple[:, g * 128 : (g + 1) * 128]
        key = triple[:, width + g * 128 : width + (g + 1) * 128]
        product = mxu(stacked(key), query, NT) * HEAD ** (-0.5)
        for h in range(GROUP):
            head = g * GROUP + h
            at = slice(head * WIN, (head + 1) * WIN)
            bias = jnp.concatenate((main[at, :], tail[at, :TAIL]), axis=1)
            scores = product[h * WIN : (h + 1) * WIN] + bias
            raised = jnp.exp(scores - jnp.max(scores, axis=0, keepdims=True))
            share = (raised * (1.0 / jnp.sum(raised, axis=0, keepdims=True))).astype(bf16)
            weights[at, :] = share
            here = slice(head * HEAD, (head + 1) * HEAD)
            heads_t[here, :] = mxu(values_t[here, :], share)
    heads = heads_t[...].T.astype(bf16)
    attended = mxu(heads, output[...]).astype(bf16)
    residual[...] = (data + attended.astype(f32)).astype(bf16)


def forward(pieces, packed, output, gain, main, tail):
    width = output.shape[0]
    return pl.pallas_call(
        forward_kernel,
        out_shape=[
            shape((HEADS * WIN, WIN), bf16),
            shape((WIN, 3 * width), bf16),
            shape((width, WIN), bf16),
            shape((WIN, width), bf16),
            shape((WIN, width), bf16),
        ],
        scratch_shapes=[
            pltpu.VMEM((WIN, width), f32),
            pltpu.VMEM((width, WIN), bf16),
            pltpu.VMEM((width, WIN), f32),
        ],
        compiler_params=params(),
        cost_estimate=cost(10**9, 2 * 10**7),
        name="forward",
    )(*pieces, packed, output, gain, main, tail)


def gain_rows(gain, out):
    width = out.shape[-1]
    for quad in range(4):
        for row in range(HALF_LAT):
            odd = 1 - (row + (quad & 1) * HALF_LAT) % 2
            for side in range(2):
                block = side * 2 + odd
                at = token_row(quad, row, side, 0)
                factor = gain[:, block * width : (block + 1) * width]
                out[at : at + CELLS, :] = jnp.broadcast_to(factor, (CELLS, width))


def cell_number(places):
    row, column, level, right = places
    band = lax.shift_right_logical(row + 1, 1)
    return (band * HALF_LON + lax.shift_right_logical(column, 1)) * LEVELS + level


def split_row(places):
    return (places[0] == 0) | (places[0] == WLAT - 1)


def sent_tokens(dims, axis):
    i = lax.broadcasted_iota(jnp.int32, dims, axis)
    last = (i >= 2 * CELLS).astype(jnp.int32)
    i = i - last * 2 * CELLS
    right = (i >= CELLS).astype(jnp.int32)
    cell = i - right * CELLS
    return (2 * right + last) * QUAD + last * (HALF_LAT - 1) * 2 * CELLS + cell


def columns_of(parts):
    lane = lax.broadcasted_iota(jnp.int32, (1, 128), 1)
    out = jnp.zeros((WIN, 128), f32)
    for i, part in enumerate(parts):
        out = jnp.where(lane == i, part, out)
    return out


def moments_kernel(residual, kept, first, third, fourth, fifth, gain, scaled, moments, sent, near, over, factors):
    width = residual.shape[-1]
    upper = lax.axis_index("lev") == 1
    own, a, b = kept[...].astype(f32), fourth[...].astype(f32), fifth[...].astype(f32)
    below, right = first[...].astype(f32)[QUAD:], third[...].astype(f32)[QUAD:]
    gain_rows(gain, factors)
    for quad, part in enumerate((
        jnp.where(upper, own, a),
        jnp.where(upper, below, b),
        jnp.where(upper, a, right),
        jnp.where(upper, b, below),
    )):
        scaled[quad * QUAD : (quad + 1) * QUAD, :] = part
    grad = scaled[...] * factors[...]
    scaled[...] = grad
    data = residual[...].astype(f32)
    down = token_places((WIN, 1), 0)
    grouping = jnp.where(cell_number(down) == cell_number(token_places((1, WIN), 1)), 1.0, 0.0).astype(f32)
    inverse = jnp.where(split_row(down), 1 / (2 * width), 1 / (4 * width)).astype(f32)
    total = jnp.sum(data, axis=-1, keepdims=True)
    middle = exact(grouping, jnp.broadcast_to(total, (WIN, 128)))[:, 0:1] * inverse
    center = data - middle
    sums = columns_of((
        jnp.sum(center * center, axis=-1, keepdims=True),
        jnp.sum(grad, axis=-1, keepdims=True),
        jnp.sum(grad * center, axis=-1, keepdims=True),
    ))
    sums = exact(grouping, sums)
    lane = lax.broadcasted_iota(jnp.int32, (1, 128), 1)
    sums = jnp.where(lane == 3, middle, sums)
    moments[...] = sums
    pick = sent_tokens((4 * CELLS, 1), 0) == lax.broadcasted_iota(jnp.int32, (4 * CELLS, WIN), 1)
    sent[...] = exact(jnp.where(pick, 1.0, 0.0).astype(f32), sums)
    scale = lax.rsqrt(sums[:, 0:1] * (1 / (4 * width)) + epsilon)
    out = jnp.where(split_row(down), data, center * scale * factors[...])
    left, right = out[: 2 * QUAD], out[2 * QUAD :]
    near[...] = jnp.where(upper, left, right).astype(bf16)
    over[...] = jnp.where(upper, right, left).astype(bf16)


def cell_moments(residual, pieces, gain):
    width = residual.shape[-1]
    return pl.pallas_call(
        moments_kernel,
        out_shape=[shape((WIN, width), f32), shape((WIN, 128), f32), shape((4 * CELLS, 128), f32)]
        + [shape((2 * QUAD, width), bf16)] * 2,
        scratch_shapes=[pltpu.VMEM((WIN, width), f32)],
        compiler_params=params(),
        cost_estimate=cost(10**8, 10**6),
        name="moments",
    )(residual, *pieces, gain)


def merge_kernel(residual, scaled, moments, before, after, grad):
    width = residual.shape[-1]
    down = token_places((WIN, 1), 0)
    shared = split_row(down)
    row = down[0]
    sender = split_tokens(sent_tokens((1, 4 * CELLS), 1))
    match = (cell_number(down) == cell_number(sender)) & shared
    there = jnp.concatenate((before[2 * CELLS :], after[: 2 * CELLS]), axis=0)
    theirs = exact(jnp.where(match, 1.0, 0.0).astype(f32), there)
    mine = moments[...]
    full = 4.0 * width
    middle = jnp.where(shared, 0.5 * (mine[:, 3:4] + theirs[:, 3:4]), mine[:, 3:4])
    gap = theirs[:, 3:4] - mine[:, 3:4]
    square = jnp.where(shared, mine[:, 0:1] + theirs[:, 0:1] + gap * gap * width, mine[:, 0:1])
    scale = lax.rsqrt(square / full + epsilon)
    grad_sum = jnp.where(shared, mine[:, 1:2] + theirs[:, 1:2], mine[:, 1:2])
    cross = jnp.where(
        shared,
        mine[:, 2:3] + (mine[:, 3:4] - middle) * mine[:, 1:2]
        + theirs[:, 2:3] + (theirs[:, 3:4] - middle) * theirs[:, 1:2],
        mine[:, 2:3],
    )
    unit = (residual[...].astype(f32) - middle) * scale
    grad[...] = (scale * (scaled[...] - grad_sum / full - unit * (cross * scale / full))).astype(bf16)


def merge_back(residual, scaled, moments, before, after):
    return pl.pallas_call(
        merge_kernel,
        out_shape=shape(residual.shape, bf16),
        compiler_params=params(),
        cost_estimate=cost(10**8, 10**6),
        name="merge",
    )(residual, scaled, moments, before, after)


def backward_kernel(half, grad, weights, triple, keys_t, output, joined, queries_t):
    width = grad.shape[-1]
    part = width // 2
    begin = half * part
    arriving_all = mxu(grad[...], output[begin : begin + part, :], NT).astype(bf16)
    for g in range(part // 128):
        here = slice(g * 128, (g + 1) * 128)
        at = begin + g * 128
        query = triple[:, at : at + 128]
        value = triple[:, 2 * width + at : 2 * width + at + 128]
        arriving = arriving_all[:, here]
        product = mxu(stacked(value), arriving, NT)
        first = at // HEAD
        shares = weights[first * WIN : (first + GROUP) * WIN, :]
        grad_value = mxu(shares, arriving)
        slopes = []
        for h in range(GROUP):
            share = shares[h * WIN : (h + 1) * WIN].astype(f32)
            change = product[h * WIN : (h + 1) * WIN]
            level = jnp.sum(share * change, axis=0, keepdims=True)
            slope = (share * (change - level) * HEAD ** (-0.5)).astype(bf16)
            head = at + h * HEAD
            queries_t[head - begin : head - begin + HEAD, :] = mxu(keys_t[head : head + HEAD, :], slope)
            slopes.append(slope)
        grad_key = mxu(jnp.concatenate(slopes, axis=0), query)
        rows = [slice(h * WIN, (h + 1) * WIN) for h in range(GROUP)]
        joined[:, part + g * 128 : part + (g + 1) * 128] = lanes_of([grad_key[r] for r in rows]).astype(bf16)
        joined[:, 2 * part + g * 128 : 2 * part + (g + 1) * 128] = lanes_of(
            [grad_value[r] for r in rows]
        ).astype(bf16)
    joined[:, :part] = queries_t[...].T.astype(bf16)


def backward(half, grad, weights, triple, keys_t, output):
    width = grad.shape[-1]
    return pl.pallas_call(
        functools.partial(backward_kernel, half),
        out_shape=shape((WIN, 3 * width // 2), bf16),
        scratch_shapes=[pltpu.VMEM((width // 2, WIN), f32)],
        compiler_params=params(),
        cost_estimate=cost(10**10, 2 * 10**7),
        name="backward",
    )(grad, weights, triple, keys_t, output)


def finish_kernel(grad, first, second, tokens, packed, gain, own, lat, lon, both):
    part = first.shape[-1] // 3
    joined = [half[:, i * part : (i + 1) * part] for i in range(3) for half in (first, second)]
    grad_inputs = mxu(jnp.concatenate(joined, axis=1), packed[...], NT).astype(bf16)
    unit, scale = unit_rows(tokens[...].astype(f32))
    scaled = grad_inputs.astype(f32) * gain[...].reshape(1, -1)
    out = grad[...].astype(f32) + scale * (scaled - row_mean(scaled) - unit * row_mean(scaled * unit))
    for quad, piece in enumerate((own, lat, lon, both)):
        piece[...] = quadrant(out, quad).astype(bf16)


def finish(grad, first, second, tokens, packed, gain):
    width = grad.shape[-1]
    return pl.pallas_call(
        finish_kernel,
        out_shape=[shape((QUAD, width), bf16)] * 4,
        compiler_params=params(),
        cost_estimate=cost(10**7, 10**6),
        name="finish",
    )(grad, first, second, tokens, packed, gain)


def relay_kernel(near, cross, out):
    out[...] = jnp.concatenate((near[...].astype(f32)[QUAD:], cross[...].astype(f32)[QUAD:]), axis=0).astype(bf16)


def relay(near, cross):
    return pl.pallas_call(
        relay_kernel,
        out_shape=shape(near.shape, bf16),
        compiler_params=params(),
        name="relay",
    )(near, cross)


def token_kernel(own, lat, lon, both, tokens):
    quads = [piece[...].astype(f32) for piece in (own, lat, lon, both)]
    for line in range(WLAT):
        for column in range(WLON):
            quad = (0 if line >= HALF_LAT else 1) + (0 if column >= HALF_LON else 2)
            inner = column % HALF_LON
            at = token_row(0, line % HALF_LAT, inner % 2, inner // 2)
            tokens[line, column] = quads[quad][at : at + LEVELS].astype(bf16)


def unpack_tokens(*pieces):
    width = pieces[0].shape[-1]
    return pl.pallas_call(
        token_kernel,
        out_shape=shape((WLAT, WLON, LEVELS, width), bf16),
        compiler_params=params(),
        name="unpack_tokens",
    )(*pieces)


def cell_kernel(near, cross, onward, gain, merged):
    width = near.shape[-1]
    upper = lax.axis_index("lev") == 1
    arrived = onward[...].astype(f32)
    same = (near[...].astype(f32)[:QUAD], arrived[:QUAD])
    other = (cross[...].astype(f32)[:QUAD], arrived[QUAD:])
    levels = (
        [jnp.where(upper, b, a) for a, b in zip(same, other)],
        [jnp.where(upper, a, b) for a, b in zip(same, other)],
    )
    blocks = {}
    for row, odd, below, inner in cell_places():
        for side in range(2):
            at = token_row(0, inner, side, 0)
            for part in range(2):
                blocks[row, side * 2 + odd, part] = levels[part][below][at : at + CELLS]
    for part in range(2):
        parts = [blocks[1, block, part] for block in range(4)]
        mean = sum(jnp.sum(x, axis=-1, keepdims=True) for x in parts) * (1 / (4 * width))
        parts = [x - mean for x in parts]
        spread = sum(jnp.sum(x * x, axis=-1, keepdims=True) for x in parts) * (1 / (4 * width))
        scale = lax.rsqrt(spread + epsilon)
        for block, x in enumerate(parts):
            blocks[1, block, part] = x * scale * gain[:, block * width : (block + 1) * width]
    for row in range(HALF_LAT):
        for pair in range(PAIRS):
            here = slice(pair * LEVELS, (pair + 1) * LEVELS)
            for block in range(4):
                merged[row, pair, :, block * width : (block + 1) * width] = jnp.concatenate(
                    (blocks[row, block, 0][here], blocks[row, block, 1][here]), axis=0
                ).astype(bf16)


def unpack_cells(near, cross, onward, gain):
    width = near.shape[-1]
    return pl.pallas_call(
        cell_kernel,
        out_shape=shape((HALF_LAT, PAIRS, 2 * LEVELS, 4 * width), bf16),
        compiler_params=params(),
        cost_estimate=cost(10**9, 10**6),
        name="unpack_cells",
    )(near, cross, onward, gain)


def routes(sizes, target):
    lons, lats, levs = sizes

    def number(i, a, k):
        return ((i % lons) * lats + a % lats) * levs + k % levs

    return [
        (number(i, a, k), number(*target(i, a, k)))
        for i in range(lons)
        for a in range(lats)
        for k in range(levs)
    ]


def send(block, sizes, target, back=False):
    pairs = routes(sizes, target)
    if back:
        pairs = [(b, a) for a, b in pairs]
    return lax.ppermute(block, ("lon", "lat", "lev"), pairs)


FIRST = lambda i, a, k: (i - (1 - k), a - 1, k)
SECOND = lambda i, a, k: (i - k, a - 1, k)
THIRD = lambda i, a, k: (i - 1, a, k)
FOURTH = lambda i, a, k: (i - (1 - k), a, 1 - k)
FIFTH = lambda i, a, k: (i - (1 - k), a - 1, 1 - k)
LAT = lambda i, a, k: (i, a - 1, k)
LON = lambda i, a, k: (i - 1, a, k)
BOTH = lambda i, a, k: (i - 1, a - 1, k)
HERE = lambda i, a, k: (i - (1 - k), a, k)


def per_device(
    sizes,
    tokens,
    packed_weight,
    output_weight,
    norm_gain,
    merge_gain,
    bias_table,
    bias_index,
    row_labels,
    column_valid,
    merged_grad,
):
    own, first, second, third, kept, fourth, fifth = pack_pieces(
        tokens.transpose(1, 2, 0, 3), merged_grad.transpose(1, 2, 0, 3)
    )
    first = send(first, sizes, FIRST)
    second = send(second, sizes, SECOND)
    third = send(third, sizes, THIRD)
    fourth = send(fourth, sizes, FOURTH)
    fifth = send(fifth, sizes, FIFTH)
    main, tail = window_bias(bias_table, bias_index, row_labels, column_valid)
    cell_gain = merge_gain.reshape(1, -1)
    weights, triple, keys_t, residual, data = forward(
        (own, first, second, third), packed_weight, output_weight, norm_gain, main, tail
    )
    scaled, moments, sent, near, cross = cell_moments(residual, (kept, first, third, fourth, fifth), cell_gain)
    before = send(sent, sizes, lambda i, a, k: (i, a + 1, k))
    after = before if sizes[1] == 2 else send(sent, sizes, lambda i, a, k: (i, a - 1, k))
    near = send(near, sizes, HERE, True)
    cross = send(cross, sizes, FOURTH, True)
    grad = merge_back(residual, scaled, moments, before, after)
    first = backward(0, grad, weights, triple, keys_t, output_weight)
    first, near, cross = lax.optimization_barrier((first, near, cross))
    onward, grad = lax.optimization_barrier((relay(near, cross), grad))
    onward = send(onward, sizes, LAT, True)
    second = backward(1, grad, weights, triple, keys_t, output_weight)
    own, lat, lon, both = finish(grad, first, second, data, packed_weight, norm_gain)
    lat = send(lat, sizes, LAT, True)
    both = send(both, sizes, BOTH, True)
    lon = send(lon, sizes, LON, True)
    merged = unpack_cells(near, cross, onward, cell_gain)
    merged, lat, both, lon = lax.optimization_barrier((merged, lat, both, lon))
    grads = unpack_tokens(own, lat, lon, both)
    return merged.transpose(2, 0, 1, 3), grads.transpose(2, 0, 1, 3)


def solution(mesh):
    sizes = tuple(mesh.shape[name] for name in ("lon", "lat", "lev"))
    placed = (
        P("lev", "lat", "lon", None),
        P(),
        P(),
        P(),
        P(),
        P("lev", "lat", None, None),
        P(),
        P("lat"),
        P(),
        P(None, "lat", ("lon", "lev"), None),
    )
    return jax.shard_map(
        functools.partial(per_device, sizes),
        mesh=mesh,
        in_specs=placed,
        out_specs=(P(None, "lat", ("lon", "lev"), None), P("lev", "lat", "lon", None)),
        check_vma=False,
    )
```

```python
import functools

import jax
import jax.numpy as jnp
from jax import lax
from jax.experimental import pallas as pl
from jax.experimental.pallas import tpu as pltpu
from jax.sharding import PartitionSpec as P

HEADS = 24
HEAD = 32
WLAT = 6
WLON = 12
HALF_LAT = WLAT // 2
HALF_LON = WLON // 2
LEVELS = 2
WIN = LEVELS * WLAT * WLON
QUAD = WIN // 4
PAIRS = HALF_LON // 2
CELLS = LEVELS * PAIRS
GROUP = 128 // HEAD
TAIL = WIN - 128
TAIL_GROUPS = WIN // 8
BLOCKED = -1e30

epsilon = 1e-05
f32 = jnp.float32
bf16 = jnp.bfloat16

NN = (((1,), (0,)), ((), ()))
NT = (((1,), (1,)), ((), ()))


def token_row(quad, row, side, pair):
    return quad * QUAD + ((row * 2 + side) * PAIRS + pair) * LEVELS


def split_tokens(t):
    def digit(rest, size, count):
        found = jnp.zeros_like(rest)
        for i in range(1, count):
            found = found + (rest >= i * size).astype(jnp.int32)
        return found, rest - found * size

    quad, rest = digit(t, QUAD, 4)
    row, rest = digit(rest, 2 * CELLS, HALF_LAT)
    side, rest = digit(rest, CELLS, 2)
    pair, level = digit(rest, LEVELS, PAIRS)
    right, below = digit(quad, 2, 2)
    row = row + HALF_LAT * below
    column = right * HALF_LON + 2 * pair + side
    return row, column, level, right


def token_places(dims, axis):
    return split_tokens(lax.broadcasted_iota(jnp.int32, dims, axis))


def mxu(a, b, dims=NN):
    return lax.dot_general(a, b, dims, preferred_element_type=f32)


def exact(a, b):
    return lax.dot_general(a, b, NN, precision=lax.Precision.HIGHEST, preferred_element_type=f32)


def params(megabytes=12):
    return pltpu.CompilerParams(vmem_limit_bytes=megabytes << 20)


def shape(dims, dtype):
    return jax.ShapeDtypeStruct(dims, dtype)


def cost(flops, nbytes):
    return pl.CostEstimate(flops=flops, bytes_accessed=nbytes, transcendentals=0)


def in_hbm(*arrays):
    return [pltpu.with_memory_space_constraint(x, pltpu.MemorySpace.HBM) for x in arrays]


def start_copies(done, *pairs):
    copies = [pltpu.make_async_copy(source, target, done.at[i]) for i, (source, target) in enumerate(pairs)]
    for copy in copies:
        copy.start()
    return copies


def quadrant(values, quad):
    return values[quad * QUAD : (quad + 1) * QUAD]


def cell_places():
    return [(0, 0, True, 0), (0, 1, True, 1), (1, 0, True, 2), (1, 1, False, 0), (2, 0, False, 1), (2, 1, False, 2)]


def pack_kernel(
    tokens_at, grad_at, table_at, index_at, own, first, second, third, kept, table, index,
    tokens, grad, rows, cells, done,
):
    width = tokens.shape[-1]
    copies = start_copies(done, (tokens_at, tokens), (grad_at, grad), (index_at, index), (table_at.at[0, 0], table))
    copies[0].wait()
    for line in range(WLAT):
        for column in range(WLON):
            quad = (0 if line >= HALF_LAT else 1) + (0 if column >= HALF_LON else 2)
            inner = column % HALF_LON
            at = token_row(quad, line % HALF_LAT, inner % 2, inner // 2)
            rows[at : at + LEVELS, :] = tokens[line, column].astype(f32)
    copies[1].wait()
    upper = lax.axis_index("lev") == 1
    for row, odd, below, inner in cell_places():
        for pair in range(PAIRS):
            for side in range(2):
                block = side * 2 + odd
                part = grad[row, pair, :, block * width : (block + 1) * width].astype(f32)
                low, high = part[:LEVELS], part[LEVELS:]
                at = token_row(int(below), inner, side, pair)
                cells[at : at + LEVELS, :] = jnp.where(upper, high, low)
                at = at + 2 * QUAD
                cells[at : at + LEVELS, :] = jnp.where(upper, low, high)
    data, grads = rows[...], cells[...]
    lat, lon, both = quadrant(data, 1), quadrant(data, 2), quadrant(data, 3)
    here, below = quadrant(grads, 0), quadrant(grads, 1)
    own[...] = quadrant(data, 0).astype(bf16)
    more = quadrant(grads, 3)
    sides = jnp.concatenate((here, quadrant(grads, 2)), axis=0)
    first[...] = jnp.concatenate((jnp.where(upper, lat, both), below, more), axis=0).astype(bf16)
    second[...] = jnp.where(upper, both, lat).astype(bf16)
    third[...] = jnp.concatenate((lon, sides), axis=0).astype(bf16)
    kept[...] = sides.astype(bf16)
    copies[2].wait()
    copies[3].wait()


def pack_pieces(tokens, grad, table, index):
    width = tokens.shape[-1]
    piece, double, triple = (shape((n * QUAD, width), bf16) for n in (1, 2, 3))
    return pl.pallas_call(
        pack_kernel,
        out_shape=[piece, triple, piece, triple, double, shape(table.shape[2:], f32), shape(index.shape, jnp.int32)],
        in_specs=[pl.BlockSpec(memory_space=pltpu.MemorySpace.HBM)] * 4,
        scratch_shapes=[
            pltpu.VMEM(tokens.shape, bf16),
            pltpu.VMEM(grad.shape, bf16),
            pltpu.VMEM((WIN, width), f32),
            pltpu.VMEM((WIN, width), f32),
            pltpu.SemaphoreType.DMA((4,)),
        ],
        compiler_params=params(),
        name="pack",
    )(*in_hbm(tokens, grad, table, index))


def bias_kernel(
    table, index, labels_at, valid_at, main, tail,
    labels, valid, split, fine, high, low, fine_high, fine_low, rest_rows, mask, mask_tail, done,
):
    copies = start_copies(done, (labels_at, labels), (valid_at, valid))
    row_k, column_k, level_k, _ = token_places((WIN, 1), 0)
    row_q, _, _, _ = token_places((1, WIN), 1)
    natural = (level_k * WLAT + row_k) * WLON + column_k
    columns = lax.broadcasted_iota(jnp.int32, (WIN, WIN), 1)
    rows = lax.broadcasted_iota(jnp.int32, (WIN, WIN), 0)
    permute = jnp.where(natural == columns, 1.0, 0.0).astype(bf16)
    heads, entries = table.shape
    gathered = 8
    wide = heads - gathered
    chunks = (entries + 255) // 256
    small_chunks = (entries + 127) // 128
    for c in range(small_chunks):
        size = min(128, entries - c * 128)
        part = table[wide:, c * 128 : c * 128 + size]
        if size < 128:
            part = jnp.concatenate((part, jnp.zeros((gathered, 128 - size), f32)), axis=1)
        fine[:, c * 128 : (c + 1) * 128] = part
    for c in range(chunks):
        size = min(256, entries - c * 256)
        part = table[:wide, c * 256 : c * 256 + size]
        if size < 256:
            part = jnp.concatenate((part, jnp.zeros((wide, 256 - size), f32)), axis=1)
        coarse = part.astype(bf16).astype(f32)
        split[c * wide : (c + 1) * wide, :] = coarse
        split[(chunks + c) * wide : (chunks + c + 1) * wide, :] = part - coarse
    source = split[...].astype(bf16)
    part_rows = chunks * wide

    def place(values, out):
        moved = mxu(mxu(permute, values.astype(f32).astype(bf16), NT).astype(bf16), permute, NT)
        out[0:WIN, :] = moved[:, :128]
        rest_rows[...] = jnp.concatenate((moved[:, 128:], jnp.zeros((WIN, 128 - TAIL), f32)), axis=1)
        total = None
        for g in range(8):
            piece = rest_rows[pl.ds(g, TAIL_GROUPS, stride=8), :]
            if g:
                piece = pltpu.roll(piece, TAIL * g, 1)
            total = piece if total is None else total + piece
        out[WIN : WIN + TAIL_GROUPS, :] = total

    entry = index[...]
    place(lax.shift_right_logical(entry, 8), high)
    place(entry & 255, low)
    upper, lower = high[...], low[...]
    far = lower >= 128.0
    fine_high[...] = (2.0 * upper + jnp.where(far, 1.0, 0.0)).astype(jnp.int32)
    fine_low[...] = jnp.where(far, lower - 128.0, lower).astype(jnp.int32)
    for copy in copies:
        copy.wait()

    label_q, label_k = jnp.zeros_like(row_q), jnp.zeros_like(row_k)
    for r in range(WLAT):
        label_q = jnp.where(row_q == r, labels[r], label_q)
        label_k = jnp.where(row_k == r, labels[r], label_k)
    valid_k = jnp.zeros_like(column_k)
    start = lax.axis_index("lon") * WLON + HALF_LON
    total = valid.shape[0]
    for c in range(WLON):
        at = start + c
        at = jnp.where(at >= total, at - total, at)
        valid_k = jnp.where(column_k == c, valid[at], valid_k)
    seen = (label_k == label_q) & ((valid_k > 0) | (rows == columns))
    added = jnp.where(seen, 0.0, BLOCKED).astype(f32)
    mask[...] = added[:, :128]
    mask_tail[...] = jnp.concatenate((added[:, 128:], jnp.zeros((WIN, 128 - TAIL), f32)), axis=1)

    depth = lax.broadcasted_iota(jnp.int32, (256, 128), 0).astype(f32).astype(bf16)
    one, zero = jnp.ones((), bf16), jnp.zeros((), bf16)

    def lookup(row):
        hot = []
        for j in range(2):
            lane = jnp.broadcast_to(low[pl.ds(row + j, 1), :], (16, 128)).astype(bf16)
            hot.append(jnp.where(depth == jnp.concatenate([lane] * 16, axis=0), one, zero))
        product = mxu(source, jnp.concatenate(hot, axis=1))
        out = []
        for j in range(2):
            here = slice(j * 128, (j + 1) * 128)
            chunk = jnp.broadcast_to(high[pl.ds(row + j, 1), :], (8, 128))
            coarse, rest = [None] * (wide // 8), [None] * (wide // 8)
            for c in range(chunks):
                hit = chunk == c
                for block in range(wide // 8):
                    at = c * wide + block * 8
                    a = product[at : at + 8, here]
                    b = product[part_rows + at : part_rows + at + 8, here]
                    coarse[block] = a if c == 0 else jnp.where(hit, a, coarse[block])
                    rest[block] = b if c == 0 else jnp.where(hit, b, rest[block])
            found = [a + b for a, b in zip(coarse, rest)]
            chunk = jnp.broadcast_to(fine_high[pl.ds(row + j, 1), :], (8, 128))
            lane = jnp.broadcast_to(fine_low[pl.ds(row + j, 1), :], (8, 128))
            value = None
            for c in range(small_chunks):
                a = jnp.take_along_axis(fine[:, c * 128 : (c + 1) * 128], lane, axis=1, mode="promise_in_bounds")
                value = a if c == 0 else jnp.where(chunk == c, a, value)
            found.append(value)
            out.append(found)
        return out

    for key in range(0, WIN, 2):
        for j, found in enumerate(lookup(key)):
            extra = jnp.broadcast_to(mask[key + j : key + j + 1, :], (8, 128))
            for block, value in enumerate(found):
                main[pl.ds(block * 8 * WIN + key + j, 8, stride=WIN), :] = value + extra
    for row in range(0, TAIL_GROUPS, 2):
        for j, found in enumerate(lookup(WIN + row)):
            for block, value in enumerate(found):
                for g in range(8):
                    key = (row + j) * 8 + g
                    moved = pltpu.roll(value, 128 - TAIL * g, 1) if g else value
                    extra = jnp.broadcast_to(mask_tail[key : key + 1, :], (8, 128))
                    tail[pl.ds(block * 8 * WIN + key, 8, stride=WIN), :] = moved + extra


def window_bias(table, index, labels, valid):
    heads, entries = table.shape
    whole = (entries + 255) // 256
    index_rows = WIN + TAIL_GROUPS
    return pl.pallas_call(
        bias_kernel,
        out_shape=[shape((heads * WIN, 128), f32)] * 2,
        in_specs=[pl.BlockSpec(memory_space=pltpu.MemorySpace.VMEM)] * 2
        + [pl.BlockSpec(memory_space=pltpu.MemorySpace.HBM)] * 2,
        scratch_shapes=[
            pltpu.SMEM(labels.shape, jnp.int32),
            pltpu.SMEM(valid.shape, jnp.int32),
            pltpu.VMEM((2 * whole * (heads - 8), 256), f32),
            pltpu.VMEM((8, (entries + 127) // 128 * 128), f32),
            pltpu.VMEM((index_rows, 128), f32),
            pltpu.VMEM((index_rows, 128), f32),
            pltpu.VMEM((index_rows, 128), jnp.int32),
            pltpu.VMEM((index_rows, 128), jnp.int32),
            pltpu.VMEM((WIN, 128), f32),
            pltpu.VMEM((WIN, 128), f32),
            pltpu.VMEM((WIN, 128), f32),
            pltpu.SemaphoreType.DMA((2,)),
        ],
        compiler_params=params(),
        cost_estimate=cost(10**10, 2 * 10**7),
        name="bias",
    )(table, index, *in_hbm(labels, valid))


def row_mean(values):
    return jnp.mean(values, axis=-1, keepdims=True)


def unit_rows(data):
    center = data - row_mean(data)
    scale = lax.rsqrt(row_mean(center * center) + epsilon)
    return center * scale, scale


def stacked(block):
    lane = lax.broadcasted_iota(jnp.int32, (1, 128), 1) // HEAD
    return jnp.concatenate(
        [jnp.where(lane == h, block, jnp.zeros((), block.dtype)) for h in range(GROUP)], axis=0
    )


def lanes_of(parts):
    lane = lax.broadcasted_iota(jnp.int32, (1, 128), 1) // HEAD
    out = parts[0]
    for h in range(1, GROUP):
        out = jnp.where(lane == h, parts[h], out)
    return out


def forward_kernel(
    own, first, second, third, packed, output, gain, main, tail,
    weights, triple, keys_t, residual, tokens,
    gathered, values_t, heads_t,
):
    width = own.shape[-1]
    upper = lax.axis_index("lev") == 1
    a, b = first[...].astype(f32)[:QUAD], second[...].astype(f32)
    lon = third[...].astype(f32)[:QUAD]
    for quad, piece in enumerate((own[...].astype(f32), jnp.where(upper, a, b), lon, jnp.where(upper, b, a))):
        gathered[quad * QUAD : (quad + 1) * QUAD, :] = piece
    data = gathered[...]
    tokens[...] = data.astype(bf16)
    unit, _ = unit_rows(data)
    normed = (unit * gain[...].reshape(1, -1)).astype(bf16)
    triple[...] = mxu(normed, packed[...]).astype(bf16)
    keys_t[...] = triple[:, width : 2 * width].astype(f32).T.astype(bf16)
    values_t[...] = triple[:, 2 * width :].astype(f32).T.astype(bf16)
    for g in range(width // 128):
        query = triple[:, g * 128 : (g + 1) * 128]
        key = triple[:, width + g * 128 : width + (g + 1) * 128]
        product = mxu(stacked(key), query, NT) * HEAD ** (-0.5)
        for h in range(GROUP):
            head = g * GROUP + h
            at = slice(head * WIN, (head + 1) * WIN)
            bias = jnp.concatenate((main[at, :], tail[at, :TAIL]), axis=1)
            scores = product[h * WIN : (h + 1) * WIN] + bias
            raised = jnp.exp(scores - jnp.max(scores, axis=0, keepdims=True))
            share = (raised * (1.0 / jnp.sum(raised, axis=0, keepdims=True))).astype(bf16)
            weights[at, :] = share
            here = slice(head * HEAD, (head + 1) * HEAD)
            heads_t[here, :] = mxu(values_t[here, :], share)
    heads = heads_t[...].T.astype(bf16)
    attended = mxu(heads, output[...]).astype(bf16)
    residual[...] = (data + attended.astype(f32)).astype(bf16)


def forward(pieces, packed, output, gain, main, tail):
    width = output.shape[0]
    return pl.pallas_call(
        forward_kernel,
        out_shape=[
            shape((HEADS * WIN, WIN), bf16),
            shape((WIN, 3 * width), bf16),
            shape((width, WIN), bf16),
            shape((WIN, width), bf16),
            shape((WIN, width), bf16),
        ],
        scratch_shapes=[
            pltpu.VMEM((WIN, width), f32),
            pltpu.VMEM((width, WIN), bf16),
            pltpu.VMEM((width, WIN), f32),
        ],
        compiler_params=params(),
        cost_estimate=cost(10**10, 2 * 10**7),
        name="forward",
    )(*pieces, packed, output, gain, main, tail)


def gain_rows(gain, out):
    width = out.shape[-1]
    for quad in range(4):
        for row in range(HALF_LAT):
            odd = 1 - (row + (quad & 1) * HALF_LAT) % 2
            for side in range(2):
                block = side * 2 + odd
                at = token_row(quad, row, side, 0)
                factor = gain[:, block * width : (block + 1) * width]
                out[at : at + CELLS, :] = jnp.broadcast_to(factor, (CELLS, width))


def cell_number(places):
    row, column, level, right = places
    band = lax.shift_right_logical(row + 1, 1)
    return (band * HALF_LON + lax.shift_right_logical(column, 1)) * LEVELS + level


def split_row(places):
    return (places[0] == 0) | (places[0] == WLAT - 1)


def sent_tokens(dims, axis):
    i = lax.broadcasted_iota(jnp.int32, dims, axis)
    last = (i >= 2 * CELLS).astype(jnp.int32)
    i = i - last * 2 * CELLS
    right = (i >= CELLS).astype(jnp.int32)
    cell = i - right * CELLS
    return (2 * right + last) * QUAD + last * (HALF_LAT - 1) * 2 * CELLS + cell


def columns_of(parts):
    lane = lax.broadcasted_iota(jnp.int32, (1, 128), 1)
    out = jnp.zeros((WIN, 128), f32)
    for i, part in enumerate(parts):
        out = jnp.where(lane == i, part, out)
    return out


def moments_kernel(residual, kept, first, third, hopped, gain, scaled, moments, sent, near, over, factors):
    width = residual.shape[-1]
    upper = lax.axis_index("lev") == 1
    own, hop = kept[...].astype(f32)[:QUAD], hopped[...].astype(f32)
    a, b = hop[:QUAD], hop[QUAD:]
    below, right = first[...].astype(f32)[QUAD : 2 * QUAD], third[...].astype(f32)[QUAD : 2 * QUAD]
    gain_rows(gain, factors)
    for quad, part in enumerate((
        jnp.where(upper, own, a),
        jnp.where(upper, below, b),
        jnp.where(upper, a, right),
        jnp.where(upper, b, below),
    )):
        scaled[quad * QUAD : (quad + 1) * QUAD, :] = part
    grad = scaled[...] * factors[...]
    scaled[...] = grad
    data = residual[...].astype(f32)
    down = token_places((WIN, 1), 0)
    grouping = jnp.where(cell_number(down) == cell_number(token_places((1, WIN), 1)), 1.0, 0.0).astype(f32)
    inverse = jnp.where(split_row(down), 1 / (2 * width), 1 / (4 * width)).astype(f32)
    total = jnp.sum(data, axis=-1, keepdims=True)
    middle = exact(grouping, jnp.broadcast_to(total, (WIN, 128)))[:, 0:1] * inverse
    center = data - middle
    sums = columns_of((
        jnp.sum(center * center, axis=-1, keepdims=True),
        jnp.sum(grad, axis=-1, keepdims=True),
        jnp.sum(grad * center, axis=-1, keepdims=True),
    ))
    sums = exact(grouping, sums)
    lane = lax.broadcasted_iota(jnp.int32, (1, 128), 1)
    sums = jnp.where(lane == 3, middle, sums)
    moments[...] = sums
    pick = sent_tokens((4 * CELLS, 1), 0) == lax.broadcasted_iota(jnp.int32, (4 * CELLS, WIN), 1)
    sent[...] = exact(jnp.where(pick, 1.0, 0.0).astype(f32), sums)
    scale = lax.rsqrt(sums[:, 0:1] * (1 / (4 * width)) + epsilon)
    out = jnp.where(split_row(down), data, center * scale * factors[...])
    left, right = out[: 2 * QUAD], out[2 * QUAD :]
    near[...] = jnp.where(upper, left, right).astype(bf16)
    over[...] = jnp.where(upper, right, left).astype(bf16)


def cell_moments(residual, pieces, gain):
    width = residual.shape[-1]
    return pl.pallas_call(
        moments_kernel,
        out_shape=[shape((WIN, width), f32), shape((WIN, 128), f32), shape((4 * CELLS, 128), f32)]
        + [shape((2 * QUAD, width), bf16)] * 2,
        scratch_shapes=[pltpu.VMEM((WIN, width), f32)],
        compiler_params=params(),
        cost_estimate=cost(10**8, 10**6),
        name="moments",
    )(residual, *pieces, gain)


def merge_kernel(residual, scaled, moments, before, after, grad):
    width = residual.shape[-1]
    down = token_places((WIN, 1), 0)
    shared = split_row(down)
    row = down[0]
    sender = split_tokens(sent_tokens((1, 4 * CELLS), 1))
    match = (cell_number(down) == cell_number(sender)) & shared
    there = jnp.concatenate((before[2 * CELLS :], after[: 2 * CELLS]), axis=0)
    theirs = exact(jnp.where(match, 1.0, 0.0).astype(f32), there)
    mine = moments[...]
    full = 4.0 * width
    middle = jnp.where(shared, 0.5 * (mine[:, 3:4] + theirs[:, 3:4]), mine[:, 3:4])
    gap = theirs[:, 3:4] - mine[:, 3:4]
    square = jnp.where(shared, mine[:, 0:1] + theirs[:, 0:1] + gap * gap * width, mine[:, 0:1])
    scale = lax.rsqrt(square / full + epsilon)
    grad_sum = jnp.where(shared, mine[:, 1:2] + theirs[:, 1:2], mine[:, 1:2])
    cross = jnp.where(
        shared,
        mine[:, 2:3] + (mine[:, 3:4] - middle) * mine[:, 1:2]
        + theirs[:, 2:3] + (theirs[:, 3:4] - middle) * theirs[:, 1:2],
        mine[:, 2:3],
    )
    unit = (residual[...].astype(f32) - middle) * scale
    grad[...] = (scale * (scaled[...] - grad_sum / full - unit * (cross * scale / full))).astype(bf16)


def merge_back(residual, scaled, moments, before, after):
    return pl.pallas_call(
        merge_kernel,
        out_shape=shape(residual.shape, bf16),
        compiler_params=params(),
        cost_estimate=cost(10**8, 10**6),
        name="merge",
    )(residual, scaled, moments, before, after)


def backward_kernel(half, grad, weights, triple, keys_t, output, joined, queries_t):
    width = grad.shape[-1]
    part = width // 2
    begin = half * part
    arriving_all = mxu(grad[...], output[begin : begin + part, :], NT).astype(bf16)
    for g in range(part // 128):
        here = slice(g * 128, (g + 1) * 128)
        at = begin + g * 128
        query = triple[:, at : at + 128]
        value = triple[:, 2 * width + at : 2 * width + at + 128]
        arriving = arriving_all[:, here]
        product = mxu(stacked(value), arriving, NT)
        first = at // HEAD
        shares = weights[first * WIN : (first + GROUP) * WIN, :]
        grad_value = mxu(shares, arriving)
        slopes = []
        for h in range(GROUP):
            share = shares[h * WIN : (h + 1) * WIN].astype(f32)
            change = product[h * WIN : (h + 1) * WIN]
            level = jnp.sum(share * change, axis=0, keepdims=True)
            slope = (share * (change - level) * HEAD ** (-0.5)).astype(bf16)
            head = at + h * HEAD
            queries_t[head - begin : head - begin + HEAD, :] = mxu(keys_t[head : head + HEAD, :], slope)
            slopes.append(slope)
        grad_key = mxu(jnp.concatenate(slopes, axis=0), query)
        rows = [slice(h * WIN, (h + 1) * WIN) for h in range(GROUP)]
        joined[:, part + g * 128 : part + (g + 1) * 128] = lanes_of([grad_key[r] for r in rows]).astype(bf16)
        joined[:, 2 * part + g * 128 : 2 * part + (g + 1) * 128] = lanes_of(
            [grad_value[r] for r in rows]
        ).astype(bf16)
    joined[:, :part] = queries_t[...].T.astype(bf16)


def backward(half, grad, weights, triple, keys_t, output):
    width = grad.shape[-1]
    return pl.pallas_call(
        functools.partial(backward_kernel, half),
        out_shape=shape((WIN, 3 * width // 2), bf16),
        scratch_shapes=[pltpu.VMEM((width // 2, WIN), f32)],
        compiler_params=params(),
        cost_estimate=cost(10**10, 2 * 10**7),
        name="backward",
    )(grad, weights, triple, keys_t, output)


def finish_kernel(grad, first, second, tokens, packed, gain, own, lat, lon, both):
    part = first.shape[-1] // 3
    joined = [half[:, i * part : (i + 1) * part] for i in range(3) for half in (first, second)]
    grad_inputs = mxu(jnp.concatenate(joined, axis=1), packed[...], NT).astype(bf16)
    unit, scale = unit_rows(tokens[...].astype(f32))
    scaled = grad_inputs.astype(f32) * gain[...].reshape(1, -1)
    out = grad[...].astype(f32) + scale * (scaled - row_mean(scaled) - unit * row_mean(scaled * unit))
    for quad, piece in enumerate((own, lat, lon, both)):
        piece[...] = quadrant(out, quad).astype(bf16)


def finish(grad, first, second, tokens, packed, gain):
    width = grad.shape[-1]
    return pl.pallas_call(
        finish_kernel,
        out_shape=[shape((QUAD, width), bf16)] * 4,
        compiler_params=params(),
        cost_estimate=cost(10**7, 10**6),
        name="finish",
    )(grad, first, second, tokens, packed, gain)


def hop_kernel(kept, first, third, out):
    upper = lax.axis_index("lev") == 1
    here = jnp.where(upper, kept[...].astype(f32)[QUAD:], third[...].astype(f32)[2 * QUAD :])
    out[...] = jnp.concatenate((here, first[...].astype(f32)[2 * QUAD :]), axis=0).astype(bf16)


def hop(kept, first, third):
    return pl.pallas_call(
        hop_kernel,
        out_shape=shape(kept.shape, bf16),
        compiler_params=params(),
        name="hop",
    )(kept, first, third)


def relay_kernel(near, cross, out):
    out[...] = jnp.concatenate((near[...].astype(f32)[QUAD:], cross[...].astype(f32)[QUAD:]), axis=0).astype(bf16)


def relay(near, cross):
    return pl.pallas_call(
        relay_kernel,
        out_shape=shape(near.shape, bf16),
        compiler_params=params(),
        name="relay",
    )(near, cross)


def token_kernel(own, lat, lon, both, tokens):
    quads = [piece[...].astype(f32) for piece in (own, lat, lon, both)]
    for line in range(WLAT):
        for column in range(WLON):
            quad = (0 if line >= HALF_LAT else 1) + (0 if column >= HALF_LON else 2)
            inner = column % HALF_LON
            at = token_row(0, line % HALF_LAT, inner % 2, inner // 2)
            tokens[line, column] = quads[quad][at : at + LEVELS].astype(bf16)


def unpack_tokens(*pieces):
    width = pieces[0].shape[-1]
    return pl.pallas_call(
        token_kernel,
        out_shape=shape((WLAT, WLON, LEVELS, width), bf16),
        compiler_params=params(),
        name="unpack_tokens",
    )(*pieces)


def cell_kernel(near, cross, onward, gain, merged):
    width = near.shape[-1]
    upper = lax.axis_index("lev") == 1
    arrived = onward[...].astype(f32)
    same = (near[...].astype(f32)[:QUAD], arrived[:QUAD])
    other = (cross[...].astype(f32)[:QUAD], arrived[QUAD:])
    levels = (
        [jnp.where(upper, b, a) for a, b in zip(same, other)],
        [jnp.where(upper, a, b) for a, b in zip(same, other)],
    )
    blocks = {}
    for row, odd, below, inner in cell_places():
        for side in range(2):
            at = token_row(0, inner, side, 0)
            for part in range(2):
                blocks[row, side * 2 + odd, part] = levels[part][below][at : at + CELLS]
    for part in range(2):
        parts = [blocks[1, block, part] for block in range(4)]
        mean = sum(jnp.sum(x, axis=-1, keepdims=True) for x in parts) * (1 / (4 * width))
        parts = [x - mean for x in parts]
        spread = sum(jnp.sum(x * x, axis=-1, keepdims=True) for x in parts) * (1 / (4 * width))
        scale = lax.rsqrt(spread + epsilon)
        for block, x in enumerate(parts):
            blocks[1, block, part] = x * scale * gain[:, block * width : (block + 1) * width]
    for row in range(HALF_LAT):
        for pair in range(PAIRS):
            here = slice(pair * LEVELS, (pair + 1) * LEVELS)
            for block in range(4):
                merged[row, pair, :, block * width : (block + 1) * width] = jnp.concatenate(
                    (blocks[row, block, 0][here], blocks[row, block, 1][here]), axis=0
                ).astype(bf16)


def unpack_cells(near, cross, onward, gain):
    width = near.shape[-1]
    return pl.pallas_call(
        cell_kernel,
        out_shape=shape((HALF_LAT, PAIRS, 2 * LEVELS, 4 * width), bf16),
        compiler_params=params(),
        cost_estimate=cost(10**9, 10**6),
        name="unpack_cells",
    )(near, cross, onward, gain)


def routes(sizes, target):
    lons, lats, levs = sizes

    def number(i, a, k):
        return ((i % lons) * lats + a % lats) * levs + k % levs

    return [
        (number(i, a, k), number(*target(i, a, k)))
        for i in range(lons)
        for a in range(lats)
        for k in range(levs)
    ]


def send(block, sizes, target, back=False):
    pairs = routes(sizes, target)
    if back:
        pairs = [(b, a) for a, b in pairs]
    return lax.ppermute(block, ("lon", "lat", "lev"), pairs)


FIRST = lambda i, a, k: (i - (1 - k), a - 1, k)
SECOND = lambda i, a, k: (i - k, a - 1, k)
THIRD = lambda i, a, k: (i - 1, a, k)
FOURTH = lambda i, a, k: (i - (1 - k), a, 1 - k)
LEV = lambda i, a, k: (i, a, 1 - k)
LAT = lambda i, a, k: (i, a - 1, k)
LON = lambda i, a, k: (i - 1, a, k)
BOTH = lambda i, a, k: (i - 1, a - 1, k)
HERE = lambda i, a, k: (i - (1 - k), a, k)


def per_device(
    sizes,
    tokens,
    packed_weight,
    output_weight,
    norm_gain,
    merge_gain,
    bias_table,
    bias_index,
    row_labels,
    column_valid,
    merged_grad,
):
    own, first, second, third, kept, table, index = pack_pieces(
        tokens.transpose(1, 2, 0, 3), merged_grad.transpose(1, 2, 0, 3), bias_table, bias_index
    )
    first = send(first, sizes, FIRST)
    second = send(second, sizes, SECOND)
    third = send(third, sizes, THIRD)
    main, tail = window_bias(table, index, row_labels, column_valid)
    cell_gain = merge_gain.reshape(1, -1)
    hopped, own = lax.optimization_barrier((hop(kept, first, third), own))
    hopped = send(hopped, sizes, LEV)
    weights, triple, keys_t, residual, data = forward(
        (own, first, second, third), packed_weight, output_weight, norm_gain, main, tail
    )
    scaled, moments, sent, near, cross = cell_moments(residual, (kept, first, third, hopped), cell_gain)
    before = send(sent, sizes, lambda i, a, k: (i, a + 1, k))
    after = before if sizes[1] == 2 else send(sent, sizes, lambda i, a, k: (i, a - 1, k))
    near = send(near, sizes, HERE, True)
    cross = send(cross, sizes, FOURTH, True)
    grad = merge_back(residual, scaled, moments, before, after)
    first = backward(0, grad, weights, triple, keys_t, output_weight)
    first, near, cross = lax.optimization_barrier((first, near, cross))
    onward, grad = lax.optimization_barrier((relay(near, cross), grad))
    onward = send(onward, sizes, LAT, True)
    second = backward(1, grad, weights, triple, keys_t, output_weight)
    own, lat, lon, both = finish(grad, first, second, data, packed_weight, norm_gain)
    lat = send(lat, sizes, LAT, True)
    both = send(both, sizes, BOTH, True)
    lon = send(lon, sizes, LON, True)
    merged = unpack_cells(near, cross, onward, cell_gain)
    merged, lat, both, lon = lax.optimization_barrier((merged, lat, both, lon))
    grads = unpack_tokens(own, lat, lon, both)
    return merged.transpose(2, 0, 1, 3), grads.transpose(2, 0, 1, 3)


def solution(mesh):
    sizes = tuple(mesh.shape[name] for name in ("lon", "lat", "lev"))
    placed = (
        P("lev", "lat", "lon", None),
        P(),
        P(),
        P(),
        P(),
        P("lev", "lat", None, None),
        P(),
        P("lat"),
        P(),
        P(None, "lat", ("lon", "lev"), None),
    )
    return jax.shard_map(
        functools.partial(per_device, sizes),
        mesh=mesh,
        in_specs=placed,
        out_specs=(P(None, "lat", ("lon", "lev"), None), P("lev", "lat", "lon", None)),
        check_vma=False,
    )
```

```python
import functools

import jax
import jax.numpy as jnp
from jax import lax
from jax.experimental import pallas as pl
from jax.experimental.pallas import tpu as pltpu
from jax.sharding import PartitionSpec as P

HEADS = 24
HEAD = 32
WLAT = 6
WLON = 12
HALF_LAT = WLAT // 2
HALF_LON = WLON // 2
LEVELS = 2
WIN = LEVELS * WLAT * WLON
QUAD = WIN // 4
PAIRS = HALF_LON // 2
CELLS = LEVELS * PAIRS
GROUP = 128 // HEAD
TAIL = WIN - 128
TAIL_GROUPS = WIN // 8
BLOCKED = -1e30

epsilon = 1e-05
f32 = jnp.float32
bf16 = jnp.bfloat16

NN = (((1,), (0,)), ((), ()))
NT = (((1,), (1,)), ((), ()))


def token_row(quad, row, side, pair):
    return quad * QUAD + ((row * 2 + side) * PAIRS + pair) * LEVELS


def split_tokens(t):
    def digit(rest, size, count):
        found = jnp.zeros_like(rest)
        for i in range(1, count):
            found = found + (rest >= i * size).astype(jnp.int32)
        return found, rest - found * size

    quad, rest = digit(t, QUAD, 4)
    row, rest = digit(rest, 2 * CELLS, HALF_LAT)
    side, rest = digit(rest, CELLS, 2)
    pair, level = digit(rest, LEVELS, PAIRS)
    right, below = digit(quad, 2, 2)
    row = row + HALF_LAT * below
    column = right * HALF_LON + 2 * pair + side
    return row, column, level, right


def token_places(dims, axis):
    return split_tokens(lax.broadcasted_iota(jnp.int32, dims, axis))


def mxu(a, b, dims=NN):
    return lax.dot_general(a, b, dims, preferred_element_type=f32)


def exact(a, b):
    return lax.dot_general(a, b, NN, precision=lax.Precision.HIGHEST, preferred_element_type=f32)


def params(megabytes=12):
    return pltpu.CompilerParams(vmem_limit_bytes=megabytes << 20)


def shape(dims, dtype):
    return jax.ShapeDtypeStruct(dims, dtype)


def cost(flops, nbytes):
    return pl.CostEstimate(flops=flops, bytes_accessed=nbytes, transcendentals=0)


def in_hbm(*arrays):
    return [pltpu.with_memory_space_constraint(x, pltpu.MemorySpace.HBM) for x in arrays]


def start_copies(done, *pairs):
    copies = [pltpu.make_async_copy(source, target, done.at[i]) for i, (source, target) in enumerate(pairs)]
    for copy in copies:
        copy.start()
    return copies


def quadrant(values, quad):
    return values[quad * QUAD : (quad + 1) * QUAD]


def cell_places():
    return [(0, 0, True, 0), (0, 1, True, 1), (1, 0, True, 2), (1, 1, False, 0), (2, 0, False, 1), (2, 1, False, 2)]


def pack_kernel(
    tokens_at, grad_at, table_at, index_at, own, first, second, third, kept, fourth, fifth, table, index,
    tokens, grad, rows, cells, done,
):
    width = tokens.shape[-1]
    copies = start_copies(done, (tokens_at, tokens), (grad_at, grad), (index_at, index), (table_at.at[0, 0], table))
    copies[0].wait()
    for line in range(WLAT):
        for column in range(WLON):
            quad = (0 if line >= HALF_LAT else 1) + (0 if column >= HALF_LON else 2)
            inner = column % HALF_LON
            at = token_row(quad, line % HALF_LAT, inner % 2, inner // 2)
            rows[at : at + LEVELS, :] = tokens[line, column].astype(f32)
    copies[1].wait()
    upper = lax.axis_index("lev") == 1
    for row, odd, below, inner in cell_places():
        for pair in range(PAIRS):
            for side in range(2):
                block = side * 2 + odd
                part = grad[row, pair, :, block * width : (block + 1) * width].astype(f32)
                low, high = part[:LEVELS], part[LEVELS:]
                at = token_row(int(below), inner, side, pair)
                cells[at : at + LEVELS, :] = jnp.where(upper, high, low)
                at = at + 2 * QUAD
                cells[at : at + LEVELS, :] = jnp.where(upper, low, high)
    data, grads = rows[...], cells[...]
    lat, lon, both = quadrant(data, 1), quadrant(data, 2), quadrant(data, 3)
    here, below = quadrant(grads, 0), quadrant(grads, 1)
    own[...] = quadrant(data, 0).astype(bf16)
    first[...] = jnp.concatenate((jnp.where(upper, lat, both), below), axis=0).astype(bf16)
    second[...] = jnp.where(upper, both, lat).astype(bf16)
    third[...] = jnp.concatenate((lon, here), axis=0).astype(bf16)
    kept[...] = here.astype(bf16)
    fourth[...] = quadrant(grads, 2).astype(bf16)
    fifth[...] = quadrant(grads, 3).astype(bf16)
    copies[2].wait()
    copies[3].wait()


def pack_pieces(tokens, grad, table, index):
    width = tokens.shape[-1]
    piece, double = shape((QUAD, width), bf16), shape((2 * QUAD, width), bf16)
    return pl.pallas_call(
        pack_kernel,
        out_shape=[piece, double, piece, double, piece, piece, piece]
        + [shape(table.shape[2:], f32), shape(index.shape, jnp.int32)],
        in_specs=[pl.BlockSpec(memory_space=pltpu.MemorySpace.HBM)] * 4,
        scratch_shapes=[
            pltpu.VMEM(tokens.shape, bf16),
            pltpu.VMEM(grad.shape, bf16),
            pltpu.VMEM((WIN, width), f32),
            pltpu.VMEM((WIN, width), f32),
            pltpu.SemaphoreType.DMA((4,)),
        ],
        compiler_params=params(),
        name="pack",
    )(*in_hbm(tokens, grad, table, index))


def bias_kernel(
    table, index, labels_at, valid_at, main, tail,
    labels, valid, split, fine, high, low, fine_high, fine_low, rest_rows, mask, mask_tail, done,
):
    copies = start_copies(done, (labels_at, labels), (valid_at, valid))
    row_k, column_k, level_k, _ = token_places((WIN, 1), 0)
    row_q, _, _, _ = token_places((1, WIN), 1)
    natural = (level_k * WLAT + row_k) * WLON + column_k
    columns = lax.broadcasted_iota(jnp.int32, (WIN, WIN), 1)
    rows = lax.broadcasted_iota(jnp.int32, (WIN, WIN), 0)
    permute = jnp.where(natural == columns, 1.0, 0.0).astype(bf16)
    heads, entries = table.shape
    chunks = (entries + 255) // 256
    small_chunks = (entries + 127) // 128
    for c in range(small_chunks):
        size = min(128, entries - c * 128)
        part = table[:, c * 128 : c * 128 + size]
        if size < 128:
            part = jnp.concatenate((part, jnp.zeros((heads, 128 - size), f32)), axis=1)
        fine[:, c * 128 : (c + 1) * 128] = part
    for c in range(chunks):
        size = min(256, entries - c * 256)
        part = table[:, c * 256 : c * 256 + size]
        if size < 256:
            part = jnp.concatenate((part, jnp.zeros((heads, 256 - size), f32)), axis=1)
        coarse = part.astype(bf16).astype(f32)
        split[c * heads : (c + 1) * heads, :] = coarse
        split[(chunks + c) * heads : (chunks + c + 1) * heads, :] = part - coarse
    source = split[...].astype(bf16)
    part_rows = chunks * heads

    def place(values, out):
        moved = mxu(mxu(permute, values.astype(f32).astype(bf16), NT).astype(bf16), permute, NT)
        out[0:WIN, :] = moved[:, :128]
        rest_rows[...] = jnp.concatenate((moved[:, 128:], jnp.zeros((WIN, 128 - TAIL), f32)), axis=1)
        total = None
        for g in range(8):
            piece = rest_rows[pl.ds(g, TAIL_GROUPS, stride=8), :]
            if g:
                piece = pltpu.roll(piece, TAIL * g, 1)
            total = piece if total is None else total + piece
        out[WIN : WIN + TAIL_GROUPS, :] = total

    entry = index[...]
    place(lax.shift_right_logical(entry, 8), high)
    place(entry & 255, low)
    upper, lower = high[...], low[...]
    far = lower >= 128.0
    fine_high[...] = (2.0 * upper + jnp.where(far, 1.0, 0.0)).astype(jnp.int32)
    fine_low[...] = jnp.where(far, lower - 128.0, lower).astype(jnp.int32)
    for copy in copies:
        copy.wait()

    label_q, label_k = jnp.zeros_like(row_q), jnp.zeros_like(row_k)
    for r in range(WLAT):
        label_q = jnp.where(row_q == r, labels[r], label_q)
        label_k = jnp.where(row_k == r, labels[r], label_k)
    valid_k = jnp.zeros_like(column_k)
    start = lax.axis_index("lon") * WLON + HALF_LON
    total = valid.shape[0]
    for c in range(WLON):
        at = start + c
        at = jnp.where(at >= total, at - total, at)
        valid_k = jnp.where(column_k == c, valid[at], valid_k)
    seen = (label_k == label_q) & ((valid_k > 0) | (rows == columns))
    added = jnp.where(seen, 0.0, BLOCKED).astype(f32)
    mask[...] = added[:, :128]
    mask_tail[...] = jnp.concatenate((added[:, 128:], jnp.zeros((WIN, 128 - TAIL), f32)), axis=1)

    depth = lax.broadcasted_iota(jnp.int32, (256, 128), 0).astype(f32).astype(bf16)
    one, zero = jnp.ones((), bf16), jnp.zeros((), bf16)

    def pick(chunk, parts, count):
        found = [None] * (heads // 8)
        for c in range(count):
            hit = chunk == c
            for block in range(heads // 8):
                a = parts(c, block)
                found[block] = a if c == 0 else jnp.where(hit, a, found[block])
        return found

    def gathered(row):
        chunk = jnp.broadcast_to(fine_high[pl.ds(row, 1), :], (8, 128))
        lane = jnp.broadcast_to(fine_low[pl.ds(row, 1), :], (8, 128))

        def part(c, block):
            values = fine[block * 8 : block * 8 + 8, c * 128 : (c + 1) * 128]
            return jnp.take_along_axis(values, lane, axis=1, mode="promise_in_bounds")

        return pick(chunk, part, small_chunks)

    def lookup(row):
        if row // 2 % 4 == 3:
            return [gathered(row), gathered(row + 1)]
        hot = []
        for j in range(2):
            lane = jnp.broadcast_to(low[pl.ds(row + j, 1), :], (16, 128)).astype(bf16)
            hot.append(jnp.where(depth == jnp.concatenate([lane] * 16, axis=0), one, zero))
        product = mxu(source, jnp.concatenate(hot, axis=1))
        out = []
        for j in range(2):
            chunk = jnp.broadcast_to(high[pl.ds(row + j, 1), :], (8, 128))
            halves = []
            for begin in (0, part_rows):

                def part(c, block):
                    at = begin + c * heads + block * 8
                    return product[at : at + 8, j * 128 : (j + 1) * 128]

                halves.append(pick(chunk, part, chunks))
            out.append([a + b for a, b in zip(*halves)])
        return out

    for key in range(0, WIN, 2):
        for j, found in enumerate(lookup(key)):
            extra = jnp.broadcast_to(mask[key + j : key + j + 1, :], (8, 128))
            for block, value in enumerate(found):
                main[pl.ds(block * 8 * WIN + key + j, 8, stride=WIN), :] = value + extra
    for row in range(0, TAIL_GROUPS, 2):
        for j, found in enumerate(lookup(WIN + row)):
            for block, value in enumerate(found):
                for g in range(8):
                    key = (row + j) * 8 + g
                    moved = pltpu.roll(value, 128 - TAIL * g, 1) if g else value
                    extra = jnp.broadcast_to(mask_tail[key : key + 1, :], (8, 128))
                    tail[pl.ds(block * 8 * WIN + key, 8, stride=WIN), :] = moved + extra


def window_bias(table, index, labels, valid):
    heads, entries = table.shape
    whole = (entries + 255) // 256
    index_rows = WIN + TAIL_GROUPS
    return pl.pallas_call(
        bias_kernel,
        out_shape=[shape((heads * WIN, 128), f32)] * 2,
        in_specs=[pl.BlockSpec(memory_space=pltpu.MemorySpace.VMEM)] * 2
        + [pl.BlockSpec(memory_space=pltpu.MemorySpace.HBM)] * 2,
        scratch_shapes=[
            pltpu.SMEM(labels.shape, jnp.int32),
            pltpu.SMEM(valid.shape, jnp.int32),
            pltpu.VMEM((2 * whole * heads, 256), f32),
            pltpu.VMEM((heads, (entries + 127) // 128 * 128), f32),
            pltpu.VMEM((index_rows, 128), f32),
            pltpu.VMEM((index_rows, 128), f32),
            pltpu.VMEM((index_rows, 128), jnp.int32),
            pltpu.VMEM((index_rows, 128), jnp.int32),
            pltpu.VMEM((WIN, 128), f32),
            pltpu.VMEM((WIN, 128), f32),
            pltpu.VMEM((WIN, 128), f32),
            pltpu.SemaphoreType.DMA((2,)),
        ],
        compiler_params=params(),
        cost_estimate=cost(10**10, 2 * 10**7),
        name="bias",
    )(table, index, *in_hbm(labels, valid))


def row_mean(values):
    return jnp.mean(values, axis=-1, keepdims=True)


def unit_rows(data):
    center = data - row_mean(data)
    scale = lax.rsqrt(row_mean(center * center) + epsilon)
    return center * scale, scale


def stacked(block):
    lane = lax.broadcasted_iota(jnp.int32, (1, 128), 1) // HEAD
    return jnp.concatenate(
        [jnp.where(lane == h, block, jnp.zeros((), block.dtype)) for h in range(GROUP)], axis=0
    )


def lanes_of(parts):
    lane = lax.broadcasted_iota(jnp.int32, (1, 128), 1) // HEAD
    out = parts[0]
    for h in range(1, GROUP):
        out = jnp.where(lane == h, parts[h], out)
    return out


def forward_kernel(
    own, first, second, third, packed, output, gain, main, tail,
    weights, triple, keys_t, residual, tokens,
    gathered, values_t, heads_t,
):
    width = own.shape[-1]
    upper = lax.axis_index("lev") == 1
    a, b = first[...].astype(f32)[:QUAD], second[...].astype(f32)
    lon = third[...].astype(f32)[:QUAD]
    for quad, piece in enumerate((own[...].astype(f32), jnp.where(upper, a, b), lon, jnp.where(upper, b, a))):
        gathered[quad * QUAD : (quad + 1) * QUAD, :] = piece
    data = gathered[...]
    tokens[...] = data.astype(bf16)
    unit, _ = unit_rows(data)
    normed = (unit * gain[...].reshape(1, -1)).astype(bf16)
    triple[...] = mxu(normed, packed[...]).astype(bf16)
    keys_t[...] = triple[:, width : 2 * width].astype(f32).T.astype(bf16)
    values_t[...] = triple[:, 2 * width :].astype(f32).T.astype(bf16)
    for g in range(width // 128):
        query = triple[:, g * 128 : (g + 1) * 128]
        key = triple[:, width + g * 128 : width + (g + 1) * 128]
        product = mxu(stacked(key), query, NT) * HEAD ** (-0.5)
        for h in range(GROUP):
            head = g * GROUP + h
            at = slice(head * WIN, (head + 1) * WIN)
            bias = jnp.concatenate((main[at, :], tail[at, :TAIL]), axis=1)
            scores = product[h * WIN : (h + 1) * WIN] + bias
            raised = jnp.exp(scores - jnp.max(scores, axis=0, keepdims=True))
            share = (raised * (1.0 / jnp.sum(raised, axis=0, keepdims=True))).astype(bf16)
            weights[at, :] = share
            here = slice(head * HEAD, (head + 1) * HEAD)
            heads_t[here, :] = mxu(values_t[here, :], share)
    heads = heads_t[...].T.astype(bf16)
    attended = mxu(heads, output[...]).astype(bf16)
    residual[...] = (data + attended.astype(f32)).astype(bf16)


def forward(pieces, packed, output, gain, main, tail):
    width = output.shape[0]
    return pl.pallas_call(
        forward_kernel,
        out_shape=[
            shape((HEADS * WIN, WIN), bf16),
            shape((WIN, 3 * width), bf16),
            shape((width, WIN), bf16),
            shape((WIN, width), bf16),
            shape((WIN, width), bf16),
        ],
        scratch_shapes=[
            pltpu.VMEM((WIN, width), f32),
            pltpu.VMEM((width, WIN), bf16),
            pltpu.VMEM((width, WIN), f32),
        ],
        compiler_params=params(),
        cost_estimate=cost(10**10, 2 * 10**7),
        name="forward",
    )(*pieces, packed, output, gain, main, tail)


def gain_rows(gain, out):
    width = out.shape[-1]
    for quad in range(4):
        for row in range(HALF_LAT):
            odd = 1 - (row + (quad & 1) * HALF_LAT) % 2
            for side in range(2):
                block = side * 2 + odd
                at = token_row(quad, row, side, 0)
                factor = gain[:, block * width : (block + 1) * width]
                out[at : at + CELLS, :] = jnp.broadcast_to(factor, (CELLS, width))


def cell_number(places):
    row, column, level, right = places
    band = lax.shift_right_logical(row + 1, 1)
    return (band * HALF_LON + lax.shift_right_logical(column, 1)) * LEVELS + level


def split_row(places):
    return (places[0] == 0) | (places[0] == WLAT - 1)


def sent_tokens(dims, axis):
    i = lax.broadcasted_iota(jnp.int32, dims, axis)
    last = (i >= 2 * CELLS).astype(jnp.int32)
    i = i - last * 2 * CELLS
    right = (i >= CELLS).astype(jnp.int32)
    cell = i - right * CELLS
    return (2 * right + last) * QUAD + last * (HALF_LAT - 1) * 2 * CELLS + cell


def columns_of(parts):
    lane = lax.broadcasted_iota(jnp.int32, (1, 128), 1)
    out = jnp.zeros((WIN, 128), f32)
    for i, part in enumerate(parts):
        out = jnp.where(lane == i, part, out)
    return out


def moments_kernel(residual, kept, first, third, fourth, fifth, gain, scaled, moments, sent, near, over, factors):
    width = residual.shape[-1]
    upper = lax.axis_index("lev") == 1
    own, a, b = kept[...].astype(f32), fourth[...].astype(f32), fifth[...].astype(f32)
    below, right = first[...].astype(f32)[QUAD:], third[...].astype(f32)[QUAD:]
    gain_rows(gain, factors)
    for quad, part in enumerate((
        jnp.where(upper, own, a),
        jnp.where(upper, below, b),
        jnp.where(upper, a, right),
        jnp.where(upper, b, below),
    )):
        scaled[quad * QUAD : (quad + 1) * QUAD, :] = part
    grad = scaled[...] * factors[...]
    scaled[...] = grad
    data = residual[...].astype(f32)
    down = token_places((WIN, 1), 0)
    grouping = jnp.where(cell_number(down) == cell_number(token_places((1, WIN), 1)), 1.0, 0.0).astype(f32)
    inverse = jnp.where(split_row(down), 1 / (2 * width), 1 / (4 * width)).astype(f32)
    total = jnp.sum(data, axis=-1, keepdims=True)
    middle = exact(grouping, jnp.broadcast_to(total, (WIN, 128)))[:, 0:1] * inverse
    center = data - middle
    sums = columns_of((
        jnp.sum(center * center, axis=-1, keepdims=True),
        jnp.sum(grad, axis=-1, keepdims=True),
        jnp.sum(grad * center, axis=-1, keepdims=True),
    ))
    sums = exact(grouping, sums)
    lane = lax.broadcasted_iota(jnp.int32, (1, 128), 1)
    sums = jnp.where(lane == 3, middle, sums)
    moments[...] = sums
    pick = sent_tokens((4 * CELLS, 1), 0) == lax.broadcasted_iota(jnp.int32, (4 * CELLS, WIN), 1)
    sent[...] = exact(jnp.where(pick, 1.0, 0.0).astype(f32), sums)
    scale = lax.rsqrt(sums[:, 0:1] * (1 / (4 * width)) + epsilon)
    out = jnp.where(split_row(down), data, center * scale * factors[...])
    left, right = out[: 2 * QUAD], out[2 * QUAD :]
    near[...] = jnp.where(upper, left, right).astype(bf16)
    over[...] = jnp.where(upper, right, left).astype(bf16)


def cell_moments(residual, pieces, gain):
    width = residual.shape[-1]
    return pl.pallas_call(
        moments_kernel,
        out_shape=[shape((WIN, width), f32), shape((WIN, 128), f32), shape((4 * CELLS, 128), f32)]
        + [shape((2 * QUAD, width), bf16)] * 2,
        scratch_shapes=[pltpu.VMEM((WIN, width), f32)],
        compiler_params=params(),
        cost_estimate=cost(10**8, 10**6),
        name="moments",
    )(residual, *pieces, gain)


def merge_kernel(residual, scaled, moments, before, after, grad):
    width = residual.shape[-1]
    down = token_places((WIN, 1), 0)
    shared = split_row(down)
    row = down[0]
    sender = split_tokens(sent_tokens((1, 4 * CELLS), 1))
    match = (cell_number(down) == cell_number(sender)) & shared
    there = jnp.concatenate((before[2 * CELLS :], after[: 2 * CELLS]), axis=0)
    theirs = exact(jnp.where(match, 1.0, 0.0).astype(f32), there)
    mine = moments[...]
    full = 4.0 * width
    middle = jnp.where(shared, 0.5 * (mine[:, 3:4] + theirs[:, 3:4]), mine[:, 3:4])
    gap = theirs[:, 3:4] - mine[:, 3:4]
    square = jnp.where(shared, mine[:, 0:1] + theirs[:, 0:1] + gap * gap * width, mine[:, 0:1])
    scale = lax.rsqrt(square / full + epsilon)
    grad_sum = jnp.where(shared, mine[:, 1:2] + theirs[:, 1:2], mine[:, 1:2])
    cross = jnp.where(
        shared,
        mine[:, 2:3] + (mine[:, 3:4] - middle) * mine[:, 1:2]
        + theirs[:, 2:3] + (theirs[:, 3:4] - middle) * theirs[:, 1:2],
        mine[:, 2:3],
    )
    unit = (residual[...].astype(f32) - middle) * scale
    grad[...] = (scale * (scaled[...] - grad_sum / full - unit * (cross * scale / full))).astype(bf16)


def merge_back(residual, scaled, moments, before, after):
    return pl.pallas_call(
        merge_kernel,
        out_shape=shape(residual.shape, bf16),
        compiler_params=params(),
        cost_estimate=cost(10**8, 10**6),
        name="merge",
    )(residual, scaled, moments, before, after)


def backward_kernel(half, grad, weights, triple, keys_t, output, joined, queries_t):
    width = grad.shape[-1]
    part = width // 2
    begin = half * part
    arriving_all = mxu(grad[...], output[begin : begin + part, :], NT).astype(bf16)
    for g in range(part // 128):
        here = slice(g * 128, (g + 1) * 128)
        at = begin + g * 128
        query = triple[:, at : at + 128]
        value = triple[:, 2 * width + at : 2 * width + at + 128]
        arriving = arriving_all[:, here]
        product = mxu(stacked(value), arriving, NT)
        first = at // HEAD
        shares = weights[first * WIN : (first + GROUP) * WIN, :]
        grad_value = mxu(shares, arriving)
        slopes = []
        for h in range(GROUP):
            share = shares[h * WIN : (h + 1) * WIN].astype(f32)
            change = product[h * WIN : (h + 1) * WIN]
            level = jnp.sum(share * change, axis=0, keepdims=True)
            slope = (share * (change - level) * HEAD ** (-0.5)).astype(bf16)
            head = at + h * HEAD
            queries_t[head - begin : head - begin + HEAD, :] = mxu(keys_t[head : head + HEAD, :], slope)
            slopes.append(slope)
        grad_key = mxu(jnp.concatenate(slopes, axis=0), query)
        rows = [slice(h * WIN, (h + 1) * WIN) for h in range(GROUP)]
        joined[:, part + g * 128 : part + (g + 1) * 128] = lanes_of([grad_key[r] for r in rows]).astype(bf16)
        joined[:, 2 * part + g * 128 : 2 * part + (g + 1) * 128] = lanes_of(
            [grad_value[r] for r in rows]
        ).astype(bf16)
    joined[:, :part] = queries_t[...].T.astype(bf16)


def backward(half, grad, weights, triple, keys_t, output):
    width = grad.shape[-1]
    return pl.pallas_call(
        functools.partial(backward_kernel, half),
        out_shape=shape((WIN, 3 * width // 2), bf16),
        scratch_shapes=[pltpu.VMEM((width // 2, WIN), f32)],
        compiler_params=params(),
        cost_estimate=cost(10**10, 2 * 10**7),
        name="backward",
    )(grad, weights, triple, keys_t, output)


def finish_kernel(quads, grad, first, second, tokens, packed, gain, *outs):
    part = first.shape[-1] // 3

    def rows(values):
        values = values.astype(f32)
        return jnp.concatenate([quadrant(values, quad) for quad in quads], axis=0)

    joined = [half[:, i * part : (i + 1) * part] for i in range(3) for half in (first, second)]
    joined = rows(jnp.concatenate(joined, axis=1)).astype(bf16)
    grad_inputs = mxu(joined, packed[...], NT).astype(bf16)
    unit, scale = unit_rows(rows(tokens[...]))
    scaled = grad_inputs.astype(f32) * gain[...].reshape(1, -1)
    out = rows(grad[...]) + scale * (scaled - row_mean(scaled) - unit * row_mean(scaled * unit))
    for i, piece in enumerate(outs):
        piece[...] = quadrant(out, i).astype(bf16)


def finish(quads, grad, first, second, tokens, packed, gain, flops):
    width = grad.shape[-1]
    return pl.pallas_call(
        functools.partial(finish_kernel, quads),
        out_shape=[shape((QUAD, width), bf16)] * 2,
        compiler_params=params(),
        cost_estimate=cost(flops, 10**6),
        name="finish",
    )(grad, first, second, tokens, packed, gain)


def relay_kernel(near, cross, out):
    out[...] = jnp.concatenate((near[...].astype(f32)[QUAD:], cross[...].astype(f32)[QUAD:]), axis=0).astype(bf16)


def relay(near, cross):
    return pl.pallas_call(
        relay_kernel,
        out_shape=shape(near.shape, bf16),
        compiler_params=params(),
        name="relay",
    )(near, cross)


def token_kernel(own, lat, lon, both, tokens):
    quads = [piece[...].astype(f32) for piece in (own, lat, lon, both)]
    for line in range(WLAT):
        for column in range(WLON):
            quad = (0 if line >= HALF_LAT else 1) + (0 if column >= HALF_LON else 2)
            inner = column % HALF_LON
            at = token_row(0, line % HALF_LAT, inner % 2, inner // 2)
            tokens[line, column] = quads[quad][at : at + LEVELS].astype(bf16)


def unpack_tokens(*pieces):
    width = pieces[0].shape[-1]
    return pl.pallas_call(
        token_kernel,
        out_shape=shape((WLAT, WLON, LEVELS, width), bf16),
        compiler_params=params(),
        name="unpack_tokens",
    )(*pieces)


def cell_kernel(near, cross, onward, gain, merged):
    width = near.shape[-1]
    upper = lax.axis_index("lev") == 1
    arrived = onward[...].astype(f32)
    same = (near[...].astype(f32)[:QUAD], arrived[:QUAD])
    other = (cross[...].astype(f32)[:QUAD], arrived[QUAD:])
    levels = (
        [jnp.where(upper, b, a) for a, b in zip(same, other)],
        [jnp.where(upper, a, b) for a, b in zip(same, other)],
    )
    blocks = {}
    for row, odd, below, inner in cell_places():
        for side in range(2):
            at = token_row(0, inner, side, 0)
            for part in range(2):
                blocks[row, side * 2 + odd, part] = levels[part][below][at : at + CELLS]
    for part in range(2):
        parts = [blocks[1, block, part] for block in range(4)]
        mean = sum(jnp.sum(x, axis=-1, keepdims=True) for x in parts) * (1 / (4 * width))
        parts = [x - mean for x in parts]
        spread = sum(jnp.sum(x * x, axis=-1, keepdims=True) for x in parts) * (1 / (4 * width))
        scale = lax.rsqrt(spread + epsilon)
        for block, x in enumerate(parts):
            blocks[1, block, part] = x * scale * gain[:, block * width : (block + 1) * width]
    for row in range(HALF_LAT):
        for pair in range(PAIRS):
            here = slice(pair * LEVELS, (pair + 1) * LEVELS)
            for block in range(4):
                merged[row, pair, :, block * width : (block + 1) * width] = jnp.concatenate(
                    (blocks[row, block, 0][here], blocks[row, block, 1][here]), axis=0
                ).astype(bf16)


def unpack_cells(near, cross, onward, gain):
    width = near.shape[-1]
    return pl.pallas_call(
        cell_kernel,
        out_shape=shape((HALF_LAT, PAIRS, 2 * LEVELS, 4 * width), bf16),
        compiler_params=params(),
        cost_estimate=cost(10**6, 10**5),
        name="unpack_cells",
    )(near, cross, onward, gain)


def routes(sizes, target):
    lons, lats, levs = sizes

    def number(i, a, k):
        return ((i % lons) * lats + a % lats) * levs + k % levs

    return [
        (number(i, a, k), number(*target(i, a, k)))
        for i in range(lons)
        for a in range(lats)
        for k in range(levs)
    ]


def send(block, sizes, target, back=False):
    pairs = routes(sizes, target)
    if back:
        pairs = [(b, a) for a, b in pairs]
    return lax.ppermute(block, ("lon", "lat", "lev"), pairs)


FIRST = lambda i, a, k: (i - (1 - k), a - 1, k)
SECOND = lambda i, a, k: (i - k, a - 1, k)
THIRD = lambda i, a, k: (i - 1, a, k)
FOURTH = lambda i, a, k: (i - (1 - k), a, 1 - k)
FIFTH = lambda i, a, k: (i - (1 - k), a - 1, 1 - k)
LAT = lambda i, a, k: (i, a - 1, k)
LON = lambda i, a, k: (i - 1, a, k)
BOTH = lambda i, a, k: (i - 1, a - 1, k)
HERE = lambda i, a, k: (i - (1 - k), a, k)


def per_device(
    sizes,
    tokens,
    packed_weight,
    output_weight,
    norm_gain,
    merge_gain,
    bias_table,
    bias_index,
    row_labels,
    column_valid,
    merged_grad,
):
    own, first, second, third, kept, fourth, fifth, table, index = pack_pieces(
        tokens.transpose(1, 2, 0, 3), merged_grad.transpose(1, 2, 0, 3), bias_table, bias_index
    )
    first = send(first, sizes, FIRST)
    second = send(second, sizes, SECOND)
    third = send(third, sizes, THIRD)
    fourth = send(fourth, sizes, FOURTH)
    fifth = send(fifth, sizes, FIFTH)
    main, tail = window_bias(table, index, row_labels, column_valid)
    cell_gain = merge_gain.reshape(1, -1)
    weights, triple, keys_t, residual, data = forward(
        (own, first, second, third), packed_weight, output_weight, norm_gain, main, tail
    )
    scaled, moments, sent, near, cross = cell_moments(
        residual, (kept, first, third, fourth, fifth), cell_gain
    )
    before = send(sent, sizes, lambda i, a, k: (i, a + 1, k))
    after = before if sizes[1] == 2 else send(sent, sizes, lambda i, a, k: (i, a - 1, k))
    near = send(near, sizes, HERE, True)
    cross = send(cross, sizes, FOURTH, True)
    grad = merge_back(residual, scaled, moments, before, after)
    first = backward(0, grad, weights, triple, keys_t, output_weight)
    first, near, cross = lax.optimization_barrier((first, near, cross))
    onward, grad = lax.optimization_barrier((relay(near, cross), grad))
    onward = send(onward, sizes, LAT, True)
    second = backward(1, grad, weights, triple, keys_t, output_weight)
    lat, both = finish((1, 3), grad, first, second, data, packed_weight, norm_gain, 10**7)
    lat, both, second = lax.optimization_barrier((lat, both, second))
    own, lon = finish((0, 2), grad, first, second, data, packed_weight, norm_gain, 10**7)
    lat = send(lat, sizes, LAT, True)
    both = send(both, sizes, BOTH, True)
    lon = send(lon, sizes, LON, True)
    merged = unpack_cells(near, cross, onward, cell_gain)
    merged, lat, both, lon = lax.optimization_barrier((merged, lat, both, lon))
    grads = unpack_tokens(own, lat, lon, both)
    return merged.transpose(2, 0, 1, 3), grads.transpose(2, 0, 1, 3)


def solution(mesh):
    sizes = tuple(mesh.shape[name] for name in ("lon", "lat", "lev"))
    placed = (
        P("lev", "lat", "lon", None),
        P(),
        P(),
        P(),
        P(),
        P("lev", "lat", None, None),
        P(),
        P("lat"),
        P(),
        P(None, "lat", ("lon", "lev"), None),
    )
    return jax.shard_map(
        functools.partial(per_device, sizes),
        mesh=mesh,
        in_specs=placed,
        out_specs=(P(None, "lat", ("lon", "lev"), None), P("lev", "lat", "lon", None)),
        check_vma=False,
    )
```

```python
import functools

import jax
import jax.numpy as jnp
from jax import lax
from jax.experimental import pallas as pl
from jax.experimental.pallas import tpu as pltpu
from jax.sharding import PartitionSpec as P

HEADS = 24
HEAD = 32
WLAT = 6
WLON = 12
HALF_LAT = WLAT // 2
HALF_LON = WLON // 2
LEVELS = 2
WIN = LEVELS * WLAT * WLON
QUAD = WIN // 4
PAIRS = HALF_LON // 2
CELLS = LEVELS * PAIRS
GROUP = 128 // HEAD
TAIL = WIN - 128
TAIL_GROUPS = WIN // 8
BLOCKED = -1e30

epsilon = 1e-05
f32 = jnp.float32
bf16 = jnp.bfloat16

NN = (((1,), (0,)), ((), ()))
NT = (((1,), (1,)), ((), ()))


def token_row(quad, row, side, pair):
    return quad * QUAD + ((row * 2 + side) * PAIRS + pair) * LEVELS


def split_tokens(t):
    def digit(rest, size, count):
        found = jnp.zeros_like(rest)
        for i in range(1, count):
            found = found + (rest >= i * size).astype(jnp.int32)
        return found, rest - found * size

    quad, rest = digit(t, QUAD, 4)
    row, rest = digit(rest, 2 * CELLS, HALF_LAT)
    side, rest = digit(rest, CELLS, 2)
    pair, level = digit(rest, LEVELS, PAIRS)
    right, below = digit(quad, 2, 2)
    row = row + HALF_LAT * below
    column = right * HALF_LON + 2 * pair + side
    return row, column, level, right


def token_places(dims, axis):
    return split_tokens(lax.broadcasted_iota(jnp.int32, dims, axis))


def mxu(a, b, dims=NN):
    return lax.dot_general(a, b, dims, preferred_element_type=f32)


def exact(a, b):
    return lax.dot_general(a, b, NN, precision=lax.Precision.HIGHEST, preferred_element_type=f32)


def params(megabytes=12):
    return pltpu.CompilerParams(vmem_limit_bytes=megabytes << 20)


def shape(dims, dtype):
    return jax.ShapeDtypeStruct(dims, dtype)


def cost(flops, nbytes):
    return pl.CostEstimate(flops=flops, bytes_accessed=nbytes, transcendentals=0)


def in_hbm(*arrays):
    return [pltpu.with_memory_space_constraint(x, pltpu.MemorySpace.HBM) for x in arrays]


def start_copies(done, *pairs):
    copies = [pltpu.make_async_copy(source, target, done.at[i]) for i, (source, target) in enumerate(pairs)]
    for copy in copies:
        copy.start()
    return copies


def quadrant(values, quad):
    return values[quad * QUAD : (quad + 1) * QUAD]


def cell_places():
    return [(0, 0, True, 0), (0, 1, True, 1), (1, 0, True, 2), (1, 1, False, 0), (2, 0, False, 1), (2, 1, False, 2)]


def pack_kernel(
    tokens_at, grad_at, table_at, index_at, own, first, second, third, kept, fourth, fifth, table, index,
    tokens, grad, rows, cells, done,
):
    width = tokens.shape[-1]
    copies = start_copies(done, (tokens_at, tokens), (grad_at, grad), (index_at, index), (table_at.at[0, 0], table))
    copies[0].wait()
    for line in range(WLAT):
        for column in range(WLON):
            quad = (0 if line >= HALF_LAT else 1) + (0 if column >= HALF_LON else 2)
            inner = column % HALF_LON
            at = token_row(quad, line % HALF_LAT, inner % 2, inner // 2)
            rows[at : at + LEVELS, :] = tokens[line, column].astype(f32)
    copies[1].wait()
    upper = lax.axis_index("lev") == 1
    for row, odd, below, inner in cell_places():
        for pair in range(PAIRS):
            for side in range(2):
                block = side * 2 + odd
                part = grad[row, pair, :, block * width : (block + 1) * width].astype(f32)
                low, high = part[:LEVELS], part[LEVELS:]
                at = token_row(int(below), inner, side, pair)
                cells[at : at + LEVELS, :] = jnp.where(upper, high, low)
                at = at + 2 * QUAD
                cells[at : at + LEVELS, :] = jnp.where(upper, low, high)
    data, grads = rows[...], cells[...]
    lat, lon, both = quadrant(data, 1), quadrant(data, 2), quadrant(data, 3)
    here, below = quadrant(grads, 0), quadrant(grads, 1)
    own[...] = quadrant(data, 0).astype(bf16)
    first[...] = jnp.concatenate((jnp.where(upper, lat, both), below), axis=0).astype(bf16)
    second[...] = jnp.where(upper, both, lat).astype(bf16)
    third[...] = jnp.concatenate((lon, here), axis=0).astype(bf16)
    kept[...] = here.astype(bf16)
    fourth[...] = quadrant(grads, 2).astype(bf16)
    fifth[...] = quadrant(grads, 3).astype(bf16)
    copies[2].wait()
    copies[3].wait()


def pack_pieces(tokens, grad, table, index):
    width = tokens.shape[-1]
    piece, double = shape((QUAD, width), bf16), shape((2 * QUAD, width), bf16)
    return pl.pallas_call(
        pack_kernel,
        out_shape=[piece, double, piece, double, piece, piece, piece]
        + [shape(table.shape[2:], f32), shape(index.shape, jnp.int32)],
        in_specs=[pl.BlockSpec(memory_space=pltpu.MemorySpace.HBM)] * 4,
        scratch_shapes=[
            pltpu.VMEM(tokens.shape, bf16),
            pltpu.VMEM(grad.shape, bf16),
            pltpu.VMEM((WIN, width), f32),
            pltpu.VMEM((WIN, width), f32),
            pltpu.SemaphoreType.DMA((4,)),
        ],
        compiler_params=params(),
        name="pack",
    )(*in_hbm(tokens, grad, table, index))


def bias_kernel(
    table, index, labels_at, valid_at, main, tail,
    labels, valid, split, fine, high, low, fine_high, fine_low, rest_rows, mask, mask_tail, done,
):
    copies = start_copies(done, (labels_at, labels), (valid_at, valid))
    row_k, column_k, level_k, _ = token_places((WIN, 1), 0)
    row_q, _, _, _ = token_places((1, WIN), 1)
    natural = (level_k * WLAT + row_k) * WLON + column_k
    columns = lax.broadcasted_iota(jnp.int32, (WIN, WIN), 1)
    rows = lax.broadcasted_iota(jnp.int32, (WIN, WIN), 0)
    permute = jnp.where(natural == columns, 1.0, 0.0).astype(bf16)
    heads, entries = table.shape
    chunks = (entries + 255) // 256
    small_chunks = (entries + 127) // 128
    for c in range(small_chunks):
        size = min(128, entries - c * 128)
        part = table[:, c * 128 : c * 128 + size]
        if size < 128:
            part = jnp.concatenate((part, jnp.zeros((heads, 128 - size), f32)), axis=1)
        fine[:, c * 128 : (c + 1) * 128] = part
    for c in range(chunks):
        size = min(256, entries - c * 256)
        part = table[:, c * 256 : c * 256 + size]
        if size < 256:
            part = jnp.concatenate((part, jnp.zeros((heads, 256 - size), f32)), axis=1)
        coarse = part.astype(bf16).astype(f32)
        split[c * heads : (c + 1) * heads, :] = coarse
        split[(chunks + c) * heads : (chunks + c + 1) * heads, :] = part - coarse
    source = split[...].astype(bf16)
    part_rows = chunks * heads

    def place(values, out):
        moved = mxu(mxu(permute, values.astype(f32).astype(bf16), NT).astype(bf16), permute, NT)
        out[0:WIN, :] = moved[:, :128]
        rest_rows[...] = jnp.concatenate((moved[:, 128:], jnp.zeros((WIN, 128 - TAIL), f32)), axis=1)
        total = None
        for g in range(8):
            piece = rest_rows[pl.ds(g, TAIL_GROUPS, stride=8), :]
            if g:
                piece = pltpu.roll(piece, TAIL * g, 1)
            total = piece if total is None else total + piece
        out[WIN : WIN + TAIL_GROUPS, :] = total

    entry = index[...]
    place(lax.shift_right_logical(entry, 8), high)
    place(entry & 255, low)
    upper, lower = high[...], low[...]
    far = lower >= 128.0
    fine_high[...] = (2.0 * upper + jnp.where(far, 1.0, 0.0)).astype(jnp.int32)
    fine_low[...] = jnp.where(far, lower - 128.0, lower).astype(jnp.int32)
    for copy in copies:
        copy.wait()

    label_q, label_k = jnp.zeros_like(row_q), jnp.zeros_like(row_k)
    for r in range(WLAT):
        label_q = jnp.where(row_q == r, labels[r], label_q)
        label_k = jnp.where(row_k == r, labels[r], label_k)
    valid_k = jnp.zeros_like(column_k)
    start = lax.axis_index("lon") * WLON + HALF_LON
    total = valid.shape[0]
    for c in range(WLON):
        at = start + c
        at = jnp.where(at >= total, at - total, at)
        valid_k = jnp.where(column_k == c, valid[at], valid_k)
    seen = (label_k == label_q) & ((valid_k > 0) | (rows == columns))
    added = jnp.where(seen, 0.0, BLOCKED).astype(f32)
    mask[...] = added[:, :128]
    mask_tail[...] = jnp.concatenate((added[:, 128:], jnp.zeros((WIN, 128 - TAIL), f32)), axis=1)

    depth = lax.broadcasted_iota(jnp.int32, (256, 128), 0).astype(f32).astype(bf16)
    one, zero = jnp.ones((), bf16), jnp.zeros((), bf16)

    def pick(chunk, parts, count):
        found = [None] * (heads // 8)
        for c in range(count):
            hit = chunk == c
            for block in range(heads // 8):
                a = parts(c, block)
                found[block] = a if c == 0 else jnp.where(hit, a, found[block])
        return found

    def gathered(row):
        chunk = jnp.broadcast_to(fine_high[pl.ds(row, 1), :], (8, 128))
        lane = jnp.broadcast_to(fine_low[pl.ds(row, 1), :], (8, 128))

        def part(c, block):
            values = fine[block * 8 : block * 8 + 8, c * 128 : (c + 1) * 128]
            return jnp.take_along_axis(values, lane, axis=1, mode="promise_in_bounds")

        return pick(chunk, part, small_chunks)

    def lookup(row):
        if row // 2 % 4 == 3:
            return [gathered(row), gathered(row + 1)]
        hot = []
        for j in range(2):
            lane = jnp.broadcast_to(low[pl.ds(row + j, 1), :], (16, 128)).astype(bf16)
            hot.append(jnp.where(depth == jnp.concatenate([lane] * 16, axis=0), one, zero))
        product = mxu(source, jnp.concatenate(hot, axis=1))
        out = []
        for j in range(2):
            chunk = jnp.broadcast_to(high[pl.ds(row + j, 1), :], (8, 128))
            halves = []
            for begin in (0, part_rows):

                def part(c, block):
                    at = begin + c * heads + block * 8
                    return product[at : at + 8, j * 128 : (j + 1) * 128]

                halves.append(pick(chunk, part, chunks))
            out.append([a + b for a, b in zip(*halves)])
        return out

    for key in range(0, WIN, 2):
        for j, found in enumerate(lookup(key)):
            extra = jnp.broadcast_to(mask[key + j : key + j + 1, :], (8, 128))
            for block, value in enumerate(found):
                main[pl.ds(block * 8 * WIN + key + j, 8, stride=WIN), :] = value + extra
    for row in range(0, TAIL_GROUPS, 2):
        for j, found in enumerate(lookup(WIN + row)):
            for block, value in enumerate(found):
                for g in range(8):
                    key = (row + j) * 8 + g
                    moved = pltpu.roll(value, 128 - TAIL * g, 1) if g else value
                    extra = jnp.broadcast_to(mask_tail[key : key + 1, :], (8, 128))
                    tail[pl.ds(block * 8 * WIN + key, 8, stride=WIN), :] = moved + extra


def window_bias(table, index, labels, valid):
    heads, entries = table.shape
    whole = (entries + 255) // 256
    index_rows = WIN + TAIL_GROUPS
    return pl.pallas_call(
        bias_kernel,
        out_shape=[shape((heads * WIN, 128), f32)] * 2,
        in_specs=[pl.BlockSpec(memory_space=pltpu.MemorySpace.VMEM)] * 2
        + [pl.BlockSpec(memory_space=pltpu.MemorySpace.HBM)] * 2,
        scratch_shapes=[
            pltpu.SMEM(labels.shape, jnp.int32),
            pltpu.SMEM(valid.shape, jnp.int32),
            pltpu.VMEM((2 * whole * heads, 256), f32),
            pltpu.VMEM((heads, (entries + 127) // 128 * 128), f32),
            pltpu.VMEM((index_rows, 128), f32),
            pltpu.VMEM((index_rows, 128), f32),
            pltpu.VMEM((index_rows, 128), jnp.int32),
            pltpu.VMEM((index_rows, 128), jnp.int32),
            pltpu.VMEM((WIN, 128), f32),
            pltpu.VMEM((WIN, 128), f32),
            pltpu.VMEM((WIN, 128), f32),
            pltpu.SemaphoreType.DMA((2,)),
        ],
        compiler_params=params(),
        cost_estimate=cost(10**10, 2 * 10**7),
        name="bias",
    )(table, index, *in_hbm(labels, valid))


def row_mean(values):
    return jnp.mean(values, axis=-1, keepdims=True)


def unit_rows(data):
    center = data - row_mean(data)
    scale = lax.rsqrt(row_mean(center * center) + epsilon)
    return center * scale, scale


def stacked(block):
    lane = lax.broadcasted_iota(jnp.int32, (1, 128), 1) // HEAD
    return jnp.concatenate(
        [jnp.where(lane == h, block, jnp.zeros((), block.dtype)) for h in range(GROUP)], axis=0
    )


def lanes_of(parts):
    lane = lax.broadcasted_iota(jnp.int32, (1, 128), 1) // HEAD
    out = parts[0]
    for h in range(1, GROUP):
        out = jnp.where(lane == h, parts[h], out)
    return out


def forward_kernel(
    own, first, second, third, packed, output, gain, main, tail,
    weights, triple, keys_t, residual, tokens,
    gathered, values_t, heads_t,
):
    width = own.shape[-1]
    upper = lax.axis_index("lev") == 1
    a, b = first[...].astype(f32)[:QUAD], second[...].astype(f32)
    lon = third[...].astype(f32)[:QUAD]
    for quad, piece in enumerate((own[...].astype(f32), jnp.where(upper, a, b), lon, jnp.where(upper, b, a))):
        gathered[quad * QUAD : (quad + 1) * QUAD, :] = piece
    data = gathered[...]
    tokens[...] = data.astype(bf16)
    unit, _ = unit_rows(data)
    normed = (unit * gain[...].reshape(1, -1)).astype(bf16)
    triple[...] = mxu(normed, packed[...]).astype(bf16)
    keys_t[...] = triple[:, width : 2 * width].astype(f32).T.astype(bf16)
    values_t[...] = triple[:, 2 * width :].astype(f32).T.astype(bf16)
    for g in range(width // 128):
        query = triple[:, g * 128 : (g + 1) * 128]
        key = triple[:, width + g * 128 : width + (g + 1) * 128]
        product = mxu(stacked(key), query, NT) * HEAD ** (-0.5)
        for h in range(GROUP):
            head = g * GROUP + h
            at = slice(head * WIN, (head + 1) * WIN)
            bias = jnp.concatenate((main[at, :], tail[at, :TAIL]), axis=1)
            scores = product[h * WIN : (h + 1) * WIN] + bias
            raised = jnp.exp(scores - jnp.max(scores, axis=0, keepdims=True))
            share = (raised * (1.0 / jnp.sum(raised, axis=0, keepdims=True))).astype(bf16)
            weights[at, :] = share
            here = slice(head * HEAD, (head + 1) * HEAD)
            heads_t[here, :] = mxu(values_t[here, :], share)
    heads = heads_t[...].T.astype(bf16)
    attended = mxu(heads, output[...]).astype(bf16)
    residual[...] = (data + attended.astype(f32)).astype(bf16)


def forward(pieces, packed, output, gain, main, tail):
    width = output.shape[0]
    return pl.pallas_call(
        forward_kernel,
        out_shape=[
            shape((HEADS * WIN, WIN), bf16),
            shape((WIN, 3 * width), bf16),
            shape((width, WIN), bf16),
            shape((WIN, width), bf16),
            shape((WIN, width), bf16),
        ],
        scratch_shapes=[
            pltpu.VMEM((WIN, width), f32),
            pltpu.VMEM((width, WIN), bf16),
            pltpu.VMEM((width, WIN), f32),
        ],
        compiler_params=params(),
        cost_estimate=cost(10**10, 2 * 10**7),
        name="forward",
    )(*pieces, packed, output, gain, main, tail)


def gain_rows(gain, out):
    width = out.shape[-1]
    for quad in range(4):
        for row in range(HALF_LAT):
            odd = 1 - (row + (quad & 1) * HALF_LAT) % 2
            for side in range(2):
                block = side * 2 + odd
                at = token_row(quad, row, side, 0)
                factor = gain[:, block * width : (block + 1) * width]
                out[at : at + CELLS, :] = jnp.broadcast_to(factor, (CELLS, width))


def cell_number(places):
    row, column, level, right = places
    band = lax.shift_right_logical(row + 1, 1)
    return (band * HALF_LON + lax.shift_right_logical(column, 1)) * LEVELS + level


def split_row(places):
    return (places[0] == 0) | (places[0] == WLAT - 1)


def sent_tokens(dims, axis):
    i = lax.broadcasted_iota(jnp.int32, dims, axis)
    last = (i >= 2 * CELLS).astype(jnp.int32)
    i = i - last * 2 * CELLS
    right = (i >= CELLS).astype(jnp.int32)
    cell = i - right * CELLS
    return (2 * right + last) * QUAD + last * (HALF_LAT - 1) * 2 * CELLS + cell


def columns_of(parts):
    lane = lax.broadcasted_iota(jnp.int32, (1, 128), 1)
    out = jnp.zeros((WIN, 128), f32)
    for i, part in enumerate(parts):
        out = jnp.where(lane == i, part, out)
    return out


def moments_kernel(residual, kept, first, third, fourth, fifth, gain, scaled, moments, sent, near, over, factors):
    width = residual.shape[-1]
    upper = lax.axis_index("lev") == 1
    own, a, b = kept[...].astype(f32), fourth[...].astype(f32), fifth[...].astype(f32)
    below, right = first[...].astype(f32)[QUAD:], third[...].astype(f32)[QUAD:]
    gain_rows(gain, factors)
    for quad, part in enumerate((
        jnp.where(upper, own, a),
        jnp.where(upper, below, b),
        jnp.where(upper, a, right),
        jnp.where(upper, b, below),
    )):
        scaled[quad * QUAD : (quad + 1) * QUAD, :] = part
    grad = scaled[...] * factors[...]
    scaled[...] = grad
    data = residual[...].astype(f32)
    down = token_places((WIN, 1), 0)
    grouping = jnp.where(cell_number(down) == cell_number(token_places((1, WIN), 1)), 1.0, 0.0).astype(f32)
    inverse = jnp.where(split_row(down), 1 / (2 * width), 1 / (4 * width)).astype(f32)
    total = jnp.sum(data, axis=-1, keepdims=True)
    middle = exact(grouping, jnp.broadcast_to(total, (WIN, 128)))[:, 0:1] * inverse
    center = data - middle
    sums = columns_of((
        jnp.sum(center * center, axis=-1, keepdims=True),
        jnp.sum(grad, axis=-1, keepdims=True),
        jnp.sum(grad * center, axis=-1, keepdims=True),
    ))
    sums = exact(grouping, sums)
    lane = lax.broadcasted_iota(jnp.int32, (1, 128), 1)
    sums = jnp.where(lane == 3, middle, sums)
    moments[...] = sums
    pick = sent_tokens((4 * CELLS, 1), 0) == lax.broadcasted_iota(jnp.int32, (4 * CELLS, WIN), 1)
    sent[...] = exact(jnp.where(pick, 1.0, 0.0).astype(f32), sums)
    scale = lax.rsqrt(sums[:, 0:1] * (1 / (4 * width)) + epsilon)
    out = jnp.where(split_row(down), data, center * scale * factors[...])
    left, right = out[: 2 * QUAD], out[2 * QUAD :]
    near[...] = jnp.where(upper, left, right).astype(bf16)
    over[...] = jnp.where(upper, right, left).astype(bf16)


def cell_moments(residual, pieces, gain):
    width = residual.shape[-1]
    return pl.pallas_call(
        moments_kernel,
        out_shape=[shape((WIN, width), f32), shape((WIN, 128), f32), shape((4 * CELLS, 128), f32)]
        + [shape((2 * QUAD, width), bf16)] * 2,
        scratch_shapes=[pltpu.VMEM((WIN, width), f32)],
        compiler_params=params(),
        cost_estimate=cost(10**8, 10**6),
        name="moments",
    )(residual, *pieces, gain)


def merge_kernel(residual, scaled, moments, before, after, grad):
    width = residual.shape[-1]
    down = token_places((WIN, 1), 0)
    shared = split_row(down)
    row = down[0]
    sender = split_tokens(sent_tokens((1, 4 * CELLS), 1))
    match = (cell_number(down) == cell_number(sender)) & shared
    there = jnp.concatenate((before[2 * CELLS :], after[: 2 * CELLS]), axis=0)
    theirs = exact(jnp.where(match, 1.0, 0.0).astype(f32), there)
    mine = moments[...]
    full = 4.0 * width
    middle = jnp.where(shared, 0.5 * (mine[:, 3:4] + theirs[:, 3:4]), mine[:, 3:4])
    gap = theirs[:, 3:4] - mine[:, 3:4]
    square = jnp.where(shared, mine[:, 0:1] + theirs[:, 0:1] + gap * gap * width, mine[:, 0:1])
    scale = lax.rsqrt(square / full + epsilon)
    grad_sum = jnp.where(shared, mine[:, 1:2] + theirs[:, 1:2], mine[:, 1:2])
    cross = jnp.where(
        shared,
        mine[:, 2:3] + (mine[:, 3:4] - middle) * mine[:, 1:2]
        + theirs[:, 2:3] + (theirs[:, 3:4] - middle) * theirs[:, 1:2],
        mine[:, 2:3],
    )
    unit = (residual[...].astype(f32) - middle) * scale
    grad[...] = (scale * (scaled[...] - grad_sum / full - unit * (cross * scale / full))).astype(bf16)


def merge_back(residual, scaled, moments, before, after):
    return pl.pallas_call(
        merge_kernel,
        out_shape=shape(residual.shape, bf16),
        compiler_params=params(),
        cost_estimate=cost(10**8, 10**6),
        name="merge",
    )(residual, scaled, moments, before, after)


def backward_kernel(grad, weights, triple, keys_t, output, joined, queries_t):
    width = grad.shape[-1]
    upstream = grad[...]
    grad_heads = mxu(upstream, output[...], NT).astype(bf16)
    for g in range(width // 128):
        here = slice(g * 128, (g + 1) * 128)
        query = triple[:, g * 128 : (g + 1) * 128]
        value = triple[:, 2 * width + g * 128 : 2 * width + (g + 1) * 128]
        arriving = grad_heads[:, here]
        product = mxu(stacked(value), arriving, NT)
        shares = weights[g * GROUP * WIN : (g + 1) * GROUP * WIN, :]
        grad_value = mxu(shares, arriving)
        slopes = []
        for h in range(GROUP):
            head = g * GROUP + h
            share = shares[h * WIN : (h + 1) * WIN].astype(f32)
            change = product[h * WIN : (h + 1) * WIN]
            level = jnp.sum(share * change, axis=0, keepdims=True)
            slope = (share * (change - level) * HEAD ** (-0.5)).astype(bf16)
            at = slice(head * HEAD, (head + 1) * HEAD)
            queries_t[at, :] = mxu(keys_t[at, :], slope)
            slopes.append(slope)
        grad_key = mxu(jnp.concatenate(slopes, axis=0), query)
        split = [slice(h * WIN, (h + 1) * WIN) for h in range(GROUP)]
        joined[:, width + g * 128 : width + (g + 1) * 128] = lanes_of([grad_key[s] for s in split]).astype(bf16)
        joined[:, 2 * width + g * 128 : 2 * width + (g + 1) * 128] = lanes_of(
            [grad_value[s] for s in split]
        ).astype(bf16)
    joined[:, :width] = queries_t[...].T.astype(bf16)


def backward(grad, weights, triple, keys_t, output):
    width = grad.shape[-1]
    return pl.pallas_call(
        backward_kernel,
        out_shape=shape((WIN, 3 * width), bf16),
        scratch_shapes=[pltpu.VMEM((width, WIN), f32)],
        compiler_params=params(),
        cost_estimate=cost(10**10, 2 * 10**7),
        name="backward",
    )(grad, weights, triple, keys_t, output)


def finish_kernel(grad, joined, tokens, packed, gain, own, lat, lon, both):
    grad_inputs = mxu(joined[...], packed[...], NT).astype(bf16)
    unit, scale = unit_rows(tokens[...].astype(f32))
    scaled = grad_inputs.astype(f32) * gain[...].reshape(1, -1)
    out = grad[...].astype(f32) + scale * (scaled - row_mean(scaled) - unit * row_mean(scaled * unit))
    for quad, piece in enumerate((own, lat, lon, both)):
        piece[...] = quadrant(out, quad).astype(bf16)


def finish(grad, joined, tokens, packed, gain):
    width = grad.shape[-1]
    return pl.pallas_call(
        finish_kernel,
        out_shape=[shape((QUAD, width), bf16)] * 4,
        compiler_params=params(),
        cost_estimate=cost(10**10, 2 * 10**6),
        name="finish",
    )(grad, joined, tokens, packed, gain)


def relay_kernel(near, cross, out):
    out[...] = jnp.concatenate((near[...].astype(f32)[QUAD:], cross[...].astype(f32)[QUAD:]), axis=0).astype(bf16)


def relay(near, cross):
    return pl.pallas_call(
        relay_kernel,
        out_shape=shape(near.shape, bf16),
        compiler_params=params(),
        name="relay",
    )(near, cross)


def token_kernel(own, lat, lon, both, tokens):
    quads = [piece[...].astype(f32) for piece in (own, lat, lon, both)]
    for line in range(WLAT):
        for column in range(WLON):
            quad = (0 if line >= HALF_LAT else 1) + (0 if column >= HALF_LON else 2)
            inner = column % HALF_LON
            at = token_row(0, line % HALF_LAT, inner % 2, inner // 2)
            tokens[line, column] = quads[quad][at : at + LEVELS].astype(bf16)


def unpack_tokens(*pieces):
    width = pieces[0].shape[-1]
    return pl.pallas_call(
        token_kernel,
        out_shape=shape((WLAT, WLON, LEVELS, width), bf16),
        compiler_params=params(),
        name="unpack_tokens",
    )(*pieces)


def cell_kernel(near, cross, onward, gain, merged):
    width = near.shape[-1]
    upper = lax.axis_index("lev") == 1
    arrived = onward[...].astype(f32)
    same = (near[...].astype(f32)[:QUAD], arrived[:QUAD])
    other = (cross[...].astype(f32)[:QUAD], arrived[QUAD:])
    levels = (
        [jnp.where(upper, b, a) for a, b in zip(same, other)],
        [jnp.where(upper, a, b) for a, b in zip(same, other)],
    )
    blocks = {}
    for row, odd, below, inner in cell_places():
        for side in range(2):
            at = token_row(0, inner, side, 0)
            for part in range(2):
                blocks[row, side * 2 + odd, part] = levels[part][below][at : at + CELLS]
    for part in range(2):
        parts = [blocks[1, block, part] for block in range(4)]
        mean = sum(jnp.sum(x, axis=-1, keepdims=True) for x in parts) * (1 / (4 * width))
        parts = [x - mean for x in parts]
        spread = sum(jnp.sum(x * x, axis=-1, keepdims=True) for x in parts) * (1 / (4 * width))
        scale = lax.rsqrt(spread + epsilon)
        for block, x in enumerate(parts):
            blocks[1, block, part] = x * scale * gain[:, block * width : (block + 1) * width]
    for row in range(HALF_LAT):
        for pair in range(PAIRS):
            here = slice(pair * LEVELS, (pair + 1) * LEVELS)
            for block in range(4):
                merged[row, pair, :, block * width : (block + 1) * width] = jnp.concatenate(
                    (blocks[row, block, 0][here], blocks[row, block, 1][here]), axis=0
                ).astype(bf16)


def unpack_cells(near, cross, onward, gain):
    width = near.shape[-1]
    return pl.pallas_call(
        cell_kernel,
        out_shape=shape((HALF_LAT, PAIRS, 2 * LEVELS, 4 * width), bf16),
        compiler_params=params(),
        cost_estimate=cost(10**6, 10**5),
        name="unpack_cells",
    )(near, cross, onward, gain)


def routes(sizes, target):
    lons, lats, levs = sizes

    def number(i, a, k):
        return ((i % lons) * lats + a % lats) * levs + k % levs

    return [
        (number(i, a, k), number(*target(i, a, k)))
        for i in range(lons)
        for a in range(lats)
        for k in range(levs)
    ]


def send(block, sizes, target, back=False):
    pairs = routes(sizes, target)
    if back:
        pairs = [(b, a) for a, b in pairs]
    return lax.ppermute(block, ("lon", "lat", "lev"), pairs)


FIRST = lambda i, a, k: (i - (1 - k), a - 1, k)
SECOND = lambda i, a, k: (i - k, a - 1, k)
THIRD = lambda i, a, k: (i - 1, a, k)
FOURTH = lambda i, a, k: (i - (1 - k), a, 1 - k)
FIFTH = lambda i, a, k: (i - (1 - k), a - 1, 1 - k)
LAT = lambda i, a, k: (i, a - 1, k)
LON = lambda i, a, k: (i - 1, a, k)
BOTH = lambda i, a, k: (i - 1, a - 1, k)
HERE = lambda i, a, k: (i - (1 - k), a, k)


def per_device(
    sizes,
    tokens,
    packed_weight,
    output_weight,
    norm_gain,
    merge_gain,
    bias_table,
    bias_index,
    row_labels,
    column_valid,
    merged_grad,
):
    own, first, second, third, kept, fourth, fifth, table, index = pack_pieces(
        tokens.transpose(1, 2, 0, 3), merged_grad.transpose(1, 2, 0, 3), bias_table, bias_index
    )
    first = send(first, sizes, FIRST)
    second = send(second, sizes, SECOND)
    third = send(third, sizes, THIRD)
    main, tail = window_bias(table, index, row_labels, column_valid)
    main, fourth, fifth = lax.optimization_barrier((main, fourth, fifth))
    fifth = send(fifth, sizes, FIFTH)
    fourth = send(fourth, sizes, FOURTH)
    cell_gain = merge_gain.reshape(1, -1)
    weights, triple, keys_t, residual, data = forward(
        (own, first, second, third), packed_weight, output_weight, norm_gain, main, tail
    )
    scaled, moments, sent, near, cross = cell_moments(
        residual, (kept, first, third, fourth, fifth), cell_gain
    )
    before = send(sent, sizes, lambda i, a, k: (i, a + 1, k))
    after = before if sizes[1] == 2 else send(sent, sizes, lambda i, a, k: (i, a - 1, k))
    near = send(near, sizes, HERE, True)
    cross = send(cross, sizes, FOURTH, True)
    grad = merge_back(residual, scaled, moments, before, after)
    joined = backward(grad, weights, triple, keys_t, output_weight)
    joined, near, cross = lax.optimization_barrier((joined, near, cross))
    onward, joined = lax.optimization_barrier((relay(near, cross), joined))
    onward = send(onward, sizes, LAT, True)
    own, lat, lon, both = finish(grad, joined, data, packed_weight, norm_gain)
    lat = send(lat, sizes, LAT, True)
    both = send(both, sizes, BOTH, True)
    lon = send(lon, sizes, LON, True)
    merged = unpack_cells(near, cross, onward, cell_gain)
    merged, lat, both, lon = lax.optimization_barrier((merged, lat, both, lon))
    grads = unpack_tokens(own, lat, lon, both)
    return merged.transpose(2, 0, 1, 3), grads.transpose(2, 0, 1, 3)


def solution(mesh):
    sizes = tuple(mesh.shape[name] for name in ("lon", "lat", "lev"))
    placed = (
        P("lev", "lat", "lon", None),
        P(),
        P(),
        P(),
        P(),
        P("lev", "lat", None, None),
        P(),
        P("lat"),
        P(),
        P(None, "lat", ("lon", "lev"), None),
    )
    return jax.shard_map(
        functools.partial(per_device, sizes),
        mesh=mesh,
        in_specs=placed,
        out_specs=(P(None, "lat", ("lon", "lev"), None), P("lev", "lat", "lon", None)),
        check_vma=False,
    )
```

```python
import functools

import jax
import jax.numpy as jnp
from jax import lax
from jax.experimental import pallas as pl
from jax.experimental.pallas import tpu as pltpu
from jax.sharding import PartitionSpec as P

HEADS = 24
HEAD = 32
WLAT = 6
WLON = 12
HALF_LAT = WLAT // 2
HALF_LON = WLON // 2
LEVELS = 2
WIN = LEVELS * WLAT * WLON
QUAD = WIN // 4
PAIRS = HALF_LON // 2
CELLS = LEVELS * PAIRS
GROUP = 128 // HEAD
TAIL = WIN - 128
TAIL_GROUPS = WIN // 8
BLOCKED = -1e30

epsilon = 1e-05
f32 = jnp.float32
bf16 = jnp.bfloat16

NN = (((1,), (0,)), ((), ()))
NT = (((1,), (1,)), ((), ()))


def token_row(quad, row, side, pair):
    return quad * QUAD + ((row * 2 + side) * PAIRS + pair) * LEVELS


def split_tokens(t):
    def digit(rest, size, count):
        found = jnp.zeros_like(rest)
        for i in range(1, count):
            found = found + (rest >= i * size).astype(jnp.int32)
        return found, rest - found * size

    quad, rest = digit(t, QUAD, 4)
    row, rest = digit(rest, 2 * CELLS, HALF_LAT)
    side, rest = digit(rest, CELLS, 2)
    pair, level = digit(rest, LEVELS, PAIRS)
    right, below = digit(quad, 2, 2)
    row = row + HALF_LAT * below
    column = right * HALF_LON + 2 * pair + side
    return row, column, level, right


def token_places(dims, axis):
    return split_tokens(lax.broadcasted_iota(jnp.int32, dims, axis))


def mxu(a, b, dims=NN):
    return lax.dot_general(a, b, dims, preferred_element_type=f32)


def exact(a, b):
    return lax.dot_general(a, b, NN, precision=lax.Precision.HIGHEST, preferred_element_type=f32)


def params(megabytes=12):
    return pltpu.CompilerParams(vmem_limit_bytes=megabytes << 20)


def shape(dims, dtype):
    return jax.ShapeDtypeStruct(dims, dtype)


def cost(flops, nbytes):
    return pl.CostEstimate(flops=flops, bytes_accessed=nbytes, transcendentals=0)


def in_hbm(*arrays):
    return [pltpu.with_memory_space_constraint(x, pltpu.MemorySpace.HBM) for x in arrays]


def start_copies(done, *pairs):
    copies = [pltpu.make_async_copy(source, target, done.at[i]) for i, (source, target) in enumerate(pairs)]
    for copy in copies:
        copy.start()
    return copies


def quadrant(values, quad):
    return values[quad * QUAD : (quad + 1) * QUAD]


def cell_places():
    return [(0, 0, True, 0), (0, 1, True, 1), (1, 0, True, 2), (1, 1, False, 0), (2, 0, False, 1), (2, 1, False, 2)]


def pack_kernel(
    tokens_at, grad_at, table_at, index_at, own, first, second, third, kept, fourth, fifth, table, index,
    tokens, grad, rows, cells, done,
):
    width = tokens.shape[-1]
    copies = start_copies(done, (tokens_at, tokens), (grad_at, grad), (index_at, index), (table_at.at[0, 0], table))
    copies[0].wait()
    for line in range(WLAT):
        for column in range(WLON):
            quad = (0 if line >= HALF_LAT else 1) + (0 if column >= HALF_LON else 2)
            inner = column % HALF_LON
            at = token_row(quad, line % HALF_LAT, inner % 2, inner // 2)
            rows[at : at + LEVELS, :] = tokens[line, column].astype(f32)
    copies[1].wait()
    upper = lax.axis_index("lev") == 1
    for row, odd, below, inner in cell_places():
        for pair in range(PAIRS):
            for side in range(2):
                block = side * 2 + odd
                part = grad[row, pair, :, block * width : (block + 1) * width].astype(f32)
                low, high = part[:LEVELS], part[LEVELS:]
                at = token_row(int(below), inner, side, pair)
                cells[at : at + LEVELS, :] = jnp.where(upper, high, low)
                at = at + 2 * QUAD
                cells[at : at + LEVELS, :] = jnp.where(upper, low, high)
    data, grads = rows[...], cells[...]
    lat, lon, both = quadrant(data, 1), quadrant(data, 2), quadrant(data, 3)
    here, below = quadrant(grads, 0), quadrant(grads, 1)
    own[...] = quadrant(data, 0).astype(bf16)
    first[...] = jnp.concatenate((jnp.where(upper, lat, both), below), axis=0).astype(bf16)
    second[...] = jnp.where(upper, both, lat).astype(bf16)
    third[...] = jnp.concatenate((lon, here), axis=0).astype(bf16)
    kept[...] = here.astype(bf16)
    fourth[...] = quadrant(grads, 2).astype(bf16)
    fifth[...] = quadrant(grads, 3).astype(bf16)
    copies[2].wait()
    copies[3].wait()


def pack_pieces(tokens, grad, table, index):
    width = tokens.shape[-1]
    piece, double = shape((QUAD, width), bf16), shape((2 * QUAD, width), bf16)
    return pl.pallas_call(
        pack_kernel,
        out_shape=[piece, double, piece, double, piece, piece, piece]
        + [shape(table.shape[2:], f32), shape(index.shape, jnp.int32)],
        in_specs=[pl.BlockSpec(memory_space=pltpu.MemorySpace.HBM)] * 4,
        scratch_shapes=[
            pltpu.VMEM(tokens.shape, bf16),
            pltpu.VMEM(grad.shape, bf16),
            pltpu.VMEM((WIN, width), f32),
            pltpu.VMEM((WIN, width), f32),
            pltpu.SemaphoreType.DMA((4,)),
        ],
        compiler_params=params(),
        name="pack",
    )(*in_hbm(tokens, grad, table, index))


def bias_kernel(
    table, index, labels_at, valid_at, main, tail,
    labels, valid, split, fine, high, low, fine_high, fine_low, rest_rows, mask, mask_tail, done,
):
    copies = start_copies(done, (labels_at, labels), (valid_at, valid))
    row_k, column_k, level_k, _ = token_places((WIN, 1), 0)
    row_q, _, _, _ = token_places((1, WIN), 1)
    natural = (level_k * WLAT + row_k) * WLON + column_k
    columns = lax.broadcasted_iota(jnp.int32, (WIN, WIN), 1)
    rows = lax.broadcasted_iota(jnp.int32, (WIN, WIN), 0)
    permute = jnp.where(natural == columns, 1.0, 0.0).astype(bf16)
    heads, entries = table.shape
    chunks = (entries + 255) // 256
    small_chunks = (entries + 127) // 128
    for c in range(small_chunks):
        size = min(128, entries - c * 128)
        part = table[:, c * 128 : c * 128 + size]
        if size < 128:
            part = jnp.concatenate((part, jnp.zeros((heads, 128 - size), f32)), axis=1)
        fine[:, c * 128 : (c + 1) * 128] = part
    for c in range(chunks):
        size = min(256, entries - c * 256)
        part = table[:, c * 256 : c * 256 + size]
        if size < 256:
            part = jnp.concatenate((part, jnp.zeros((heads, 256 - size), f32)), axis=1)
        coarse = part.astype(bf16).astype(f32)
        split[c * heads : (c + 1) * heads, :] = coarse
        split[(chunks + c) * heads : (chunks + c + 1) * heads, :] = part - coarse
    source = split[...].astype(bf16)
    part_rows = chunks * heads

    def place(values, out):
        moved = mxu(mxu(permute, values.astype(f32).astype(bf16), NT).astype(bf16), permute, NT)
        out[0:WIN, :] = moved[:, :128]
        rest_rows[...] = jnp.concatenate((moved[:, 128:], jnp.zeros((WIN, 128 - TAIL), f32)), axis=1)
        total = None
        for g in range(8):
            piece = rest_rows[pl.ds(g, TAIL_GROUPS, stride=8), :]
            if g:
                piece = pltpu.roll(piece, TAIL * g, 1)
            total = piece if total is None else total + piece
        out[WIN : WIN + TAIL_GROUPS, :] = total

    entry = index[...]
    place(lax.shift_right_logical(entry, 8), high)
    place(entry & 255, low)
    upper, lower = high[...], low[...]
    far = lower >= 128.0
    fine_high[...] = (2.0 * upper + jnp.where(far, 1.0, 0.0)).astype(jnp.int32)
    fine_low[...] = jnp.where(far, lower - 128.0, lower).astype(jnp.int32)
    for copy in copies:
        copy.wait()

    label_q, label_k = jnp.zeros_like(row_q), jnp.zeros_like(row_k)
    for r in range(WLAT):
        label_q = jnp.where(row_q == r, labels[r], label_q)
        label_k = jnp.where(row_k == r, labels[r], label_k)
    valid_k = jnp.zeros_like(column_k)
    start = lax.axis_index("lon") * WLON + HALF_LON
    total = valid.shape[0]
    for c in range(WLON):
        at = start + c
        at = jnp.where(at >= total, at - total, at)
        valid_k = jnp.where(column_k == c, valid[at], valid_k)
    seen = (label_k == label_q) & ((valid_k > 0) | (rows == columns))
    added = jnp.where(seen, 0.0, BLOCKED).astype(f32)
    mask[...] = added[:, :128]
    mask_tail[...] = jnp.concatenate((added[:, 128:], jnp.zeros((WIN, 128 - TAIL), f32)), axis=1)

    depth = lax.broadcasted_iota(jnp.int32, (256, 128), 0).astype(f32).astype(bf16)
    one, zero = jnp.ones((), bf16), jnp.zeros((), bf16)

    def pick(chunk, parts, count):
        found = [None] * (heads // 8)
        for c in range(count):
            hit = chunk == c
            for block in range(heads // 8):
                a = parts(c, block)
                found[block] = a if c == 0 else jnp.where(hit, a, found[block])
        return found

    def gathered(row):
        chunk = jnp.broadcast_to(fine_high[pl.ds(row, 1), :], (8, 128))
        lane = jnp.broadcast_to(fine_low[pl.ds(row, 1), :], (8, 128))

        def part(c, block):
            values = fine[block * 8 : block * 8 + 8, c * 128 : (c + 1) * 128]
            return jnp.take_along_axis(values, lane, axis=1, mode="promise_in_bounds")

        return pick(chunk, part, small_chunks)

    def lookup(row):
        if row // 2 % 4 == 3:
            return [gathered(row), gathered(row + 1)]
        hot = []
        for j in range(2):
            lane = jnp.broadcast_to(low[pl.ds(row + j, 1), :], (16, 128)).astype(bf16)
            hot.append(jnp.where(depth == jnp.concatenate([lane] * 16, axis=0), one, zero))
        product = mxu(source, jnp.concatenate(hot, axis=1))
        out = []
        for j in range(2):
            chunk = jnp.broadcast_to(high[pl.ds(row + j, 1), :], (8, 128))
            halves = []
            for begin in (0, part_rows):

                def part(c, block):
                    at = begin + c * heads + block * 8
                    return product[at : at + 8, j * 128 : (j + 1) * 128]

                halves.append(pick(chunk, part, chunks))
            out.append([a + b for a, b in zip(*halves)])
        return out

    for key in range(0, WIN, 2):
        for j, found in enumerate(lookup(key)):
            extra = jnp.broadcast_to(mask[key + j : key + j + 1, :], (8, 128))
            for block, value in enumerate(found):
                main[pl.ds(block * 8 * WIN + key + j, 8, stride=WIN), :] = value + extra
    for row in range(0, TAIL_GROUPS, 2):
        for j, found in enumerate(lookup(WIN + row)):
            for block, value in enumerate(found):
                for g in range(8):
                    key = (row + j) * 8 + g
                    moved = pltpu.roll(value, 128 - TAIL * g, 1) if g else value
                    extra = jnp.broadcast_to(mask_tail[key : key + 1, :], (8, 128))
                    tail[pl.ds(block * 8 * WIN + key, 8, stride=WIN), :] = moved + extra


def window_bias(table, index, labels, valid):
    heads, entries = table.shape
    whole = (entries + 255) // 256
    index_rows = WIN + TAIL_GROUPS
    return pl.pallas_call(
        bias_kernel,
        out_shape=[shape((heads * WIN, 128), f32)] * 2,
        in_specs=[pl.BlockSpec(memory_space=pltpu.MemorySpace.VMEM)] * 2
        + [pl.BlockSpec(memory_space=pltpu.MemorySpace.HBM)] * 2,
        scratch_shapes=[
            pltpu.SMEM(labels.shape, jnp.int32),
            pltpu.SMEM(valid.shape, jnp.int32),
            pltpu.VMEM((2 * whole * heads, 256), f32),
            pltpu.VMEM((heads, (entries + 127) // 128 * 128), f32),
            pltpu.VMEM((index_rows, 128), f32),
            pltpu.VMEM((index_rows, 128), f32),
            pltpu.VMEM((index_rows, 128), jnp.int32),
            pltpu.VMEM((index_rows, 128), jnp.int32),
            pltpu.VMEM((WIN, 128), f32),
            pltpu.VMEM((WIN, 128), f32),
            pltpu.VMEM((WIN, 128), f32),
            pltpu.SemaphoreType.DMA((2,)),
        ],
        compiler_params=params(),
        cost_estimate=cost(10**10, 2 * 10**7),
        name="bias",
    )(table, index, *in_hbm(labels, valid))


def row_mean(values):
    return jnp.mean(values, axis=-1, keepdims=True)


def unit_rows(data):
    center = data - row_mean(data)
    scale = lax.rsqrt(row_mean(center * center) + epsilon)
    return center * scale, scale


def stacked(block):
    lane = lax.broadcasted_iota(jnp.int32, (1, 128), 1) // HEAD
    return jnp.concatenate(
        [jnp.where(lane == h, block, jnp.zeros((), block.dtype)) for h in range(GROUP)], axis=0
    )


def lanes_of(parts):
    lane = lax.broadcasted_iota(jnp.int32, (1, 128), 1) // HEAD
    out = parts[0]
    for h in range(1, GROUP):
        out = jnp.where(lane == h, parts[h], out)
    return out


def forward_kernel(
    own, first, second, third, packed, output, gain, main, tail,
    weights, triple, keys_t, residual, tokens,
    gathered, values_t, heads_t,
):
    width = own.shape[-1]
    upper = lax.axis_index("lev") == 1
    a, b = first[...].astype(f32)[:QUAD], second[...].astype(f32)
    lon = third[...].astype(f32)[:QUAD]
    for quad, piece in enumerate((own[...].astype(f32), jnp.where(upper, a, b), lon, jnp.where(upper, b, a))):
        gathered[quad * QUAD : (quad + 1) * QUAD, :] = piece
    data = gathered[...]
    tokens[...] = data.astype(bf16)
    unit, _ = unit_rows(data)
    normed = (unit * gain[...].reshape(1, -1)).astype(bf16)
    triple[...] = mxu(normed, packed[...]).astype(bf16)
    keys_t[...] = triple[:, width : 2 * width].astype(f32).T.astype(bf16)
    values_t[...] = triple[:, 2 * width :].astype(f32).T.astype(bf16)
    for g in range(width // 128):
        query = triple[:, g * 128 : (g + 1) * 128]
        key = triple[:, width + g * 128 : width + (g + 1) * 128]
        product = mxu(stacked(key), query, NT) * HEAD ** (-0.5)
        for h in range(GROUP):
            head = g * GROUP + h
            at = slice(head * WIN, (head + 1) * WIN)
            bias = jnp.concatenate((main[at, :], tail[at, :TAIL]), axis=1)
            scores = product[h * WIN : (h + 1) * WIN] + bias
            raised = jnp.exp(scores - jnp.max(scores, axis=0, keepdims=True))
            share = (raised * (1.0 / jnp.sum(raised, axis=0, keepdims=True))).astype(bf16)
            weights[at, :] = share
            here = slice(head * HEAD, (head + 1) * HEAD)
            heads_t[here, :] = mxu(values_t[here, :], share)
    heads = heads_t[...].T.astype(bf16)
    attended = mxu(heads, output[...]).astype(bf16)
    residual[...] = (data + attended.astype(f32)).astype(bf16)


def forward(pieces, packed, output, gain, main, tail):
    width = output.shape[0]
    return pl.pallas_call(
        forward_kernel,
        out_shape=[
            shape((HEADS * WIN, WIN), bf16),
            shape((WIN, 3 * width), bf16),
            shape((width, WIN), bf16),
            shape((WIN, width), bf16),
            shape((WIN, width), bf16),
        ],
        scratch_shapes=[
            pltpu.VMEM((WIN, width), f32),
            pltpu.VMEM((width, WIN), bf16),
            pltpu.VMEM((width, WIN), f32),
        ],
        compiler_params=params(),
        cost_estimate=cost(10**10, 2 * 10**7),
        name="forward",
    )(*pieces, packed, output, gain, main, tail)


def gain_rows(gain, out):
    width = out.shape[-1]
    for quad in range(4):
        for row in range(HALF_LAT):
            odd = 1 - (row + (quad & 1) * HALF_LAT) % 2
            for side in range(2):
                block = side * 2 + odd
                at = token_row(quad, row, side, 0)
                factor = gain[:, block * width : (block + 1) * width]
                out[at : at + CELLS, :] = jnp.broadcast_to(factor, (CELLS, width))


def cell_number(places):
    row, column, level, right = places
    band = lax.shift_right_logical(row + 1, 1)
    return (band * HALF_LON + lax.shift_right_logical(column, 1)) * LEVELS + level


def split_row(places):
    return (places[0] == 0) | (places[0] == WLAT - 1)


def sent_tokens(dims, axis):
    i = lax.broadcasted_iota(jnp.int32, dims, axis)
    last = (i >= 2 * CELLS).astype(jnp.int32)
    i = i - last * 2 * CELLS
    right = (i >= CELLS).astype(jnp.int32)
    cell = i - right * CELLS
    return (2 * right + last) * QUAD + last * (HALF_LAT - 1) * 2 * CELLS + cell


def columns_of(parts):
    lane = lax.broadcasted_iota(jnp.int32, (1, 128), 1)
    out = jnp.zeros((WIN, 128), f32)
    for i, part in enumerate(parts):
        out = jnp.where(lane == i, part, out)
    return out


def moments_kernel(residual, kept, first, third, fourth, fifth, gain, scaled, moments, sent, same_here, same_next, other_here, other_next, factors):
    width = residual.shape[-1]
    upper = lax.axis_index("lev") == 1
    own, a, b = kept[...].astype(f32), fourth[...].astype(f32), fifth[...].astype(f32)
    below, right = first[...].astype(f32)[QUAD:], third[...].astype(f32)[QUAD:]
    gain_rows(gain, factors)
    for quad, part in enumerate((
        jnp.where(upper, own, a),
        jnp.where(upper, below, b),
        jnp.where(upper, a, right),
        jnp.where(upper, b, below),
    )):
        scaled[quad * QUAD : (quad + 1) * QUAD, :] = part
    grad = scaled[...] * factors[...]
    scaled[...] = grad
    data = residual[...].astype(f32)
    down = token_places((WIN, 1), 0)
    grouping = jnp.where(cell_number(down) == cell_number(token_places((1, WIN), 1)), 1.0, 0.0).astype(f32)
    inverse = jnp.where(split_row(down), 1 / (2 * width), 1 / (4 * width)).astype(f32)
    total = jnp.sum(data, axis=-1, keepdims=True)
    middle = exact(grouping, jnp.broadcast_to(total, (WIN, 128)))[:, 0:1] * inverse
    center = data - middle
    sums = columns_of((
        jnp.sum(center * center, axis=-1, keepdims=True),
        jnp.sum(grad, axis=-1, keepdims=True),
        jnp.sum(grad * center, axis=-1, keepdims=True),
    ))
    sums = exact(grouping, sums)
    lane = lax.broadcasted_iota(jnp.int32, (1, 128), 1)
    sums = jnp.where(lane == 3, middle, sums)
    moments[...] = sums
    pick = sent_tokens((4 * CELLS, 1), 0) == lax.broadcasted_iota(jnp.int32, (4 * CELLS, WIN), 1)
    sent[...] = exact(jnp.where(pick, 1.0, 0.0).astype(f32), sums)
    scale = lax.rsqrt(sums[:, 0:1] * (1 / (4 * width)) + epsilon)
    out = jnp.where(split_row(down), data, center * scale * factors[...])
    parts = [quadrant(out, quad) for quad in range(4)]
    same_here[...] = jnp.where(upper, parts[0], parts[2]).astype(bf16)
    same_next[...] = jnp.where(upper, parts[1], parts[3]).astype(bf16)
    other_here[...] = jnp.where(upper, parts[2], parts[0]).astype(bf16)
    other_next[...] = jnp.where(upper, parts[3], parts[1]).astype(bf16)


def cell_moments(residual, pieces, gain):
    width = residual.shape[-1]
    return pl.pallas_call(
        moments_kernel,
        out_shape=[shape((WIN, width), f32), shape((WIN, 128), f32), shape((4 * CELLS, 128), f32)]
        + [shape((QUAD, width), bf16)] * 4,
        scratch_shapes=[pltpu.VMEM((WIN, width), f32)],
        compiler_params=params(),
        cost_estimate=cost(10**8, 10**6),
        name="moments",
    )(residual, *pieces, gain)


def merge_kernel(residual, scaled, moments, before, after, grad):
    width = residual.shape[-1]
    down = token_places((WIN, 1), 0)
    shared = split_row(down)
    row = down[0]
    sender = split_tokens(sent_tokens((1, 4 * CELLS), 1))
    match = (cell_number(down) == cell_number(sender)) & shared
    there = jnp.concatenate((before[2 * CELLS :], after[: 2 * CELLS]), axis=0)
    theirs = exact(jnp.where(match, 1.0, 0.0).astype(f32), there)
    mine = moments[...]
    full = 4.0 * width
    middle = jnp.where(shared, 0.5 * (mine[:, 3:4] + theirs[:, 3:4]), mine[:, 3:4])
    gap = theirs[:, 3:4] - mine[:, 3:4]
    square = jnp.where(shared, mine[:, 0:1] + theirs[:, 0:1] + gap * gap * width, mine[:, 0:1])
    scale = lax.rsqrt(square / full + epsilon)
    grad_sum = jnp.where(shared, mine[:, 1:2] + theirs[:, 1:2], mine[:, 1:2])
    cross = jnp.where(
        shared,
        mine[:, 2:3] + (mine[:, 3:4] - middle) * mine[:, 1:2]
        + theirs[:, 2:3] + (theirs[:, 3:4] - middle) * theirs[:, 1:2],
        mine[:, 2:3],
    )
    unit = (residual[...].astype(f32) - middle) * scale
    grad[...] = (scale * (scaled[...] - grad_sum / full - unit * (cross * scale / full))).astype(bf16)


def merge_back(residual, scaled, moments, before, after):
    return pl.pallas_call(
        merge_kernel,
        out_shape=shape(residual.shape, bf16),
        compiler_params=params(),
        cost_estimate=cost(10**8, 10**6),
        name="merge",
    )(residual, scaled, moments, before, after)


def backward_kernel(grad, weights, triple, keys_t, output, joined, queries_t):
    width = grad.shape[-1]
    upstream = grad[...]
    grad_heads = mxu(upstream, output[...], NT).astype(bf16)
    for g in range(width // 128):
        here = slice(g * 128, (g + 1) * 128)
        query = triple[:, g * 128 : (g + 1) * 128]
        value = triple[:, 2 * width + g * 128 : 2 * width + (g + 1) * 128]
        arriving = grad_heads[:, here]
        product = mxu(stacked(value), arriving, NT)
        shares = weights[g * GROUP * WIN : (g + 1) * GROUP * WIN, :]
        grad_value = mxu(shares, arriving)
        slopes = []
        for h in range(GROUP):
            head = g * GROUP + h
            share = shares[h * WIN : (h + 1) * WIN].astype(f32)
            change = product[h * WIN : (h + 1) * WIN]
            level = jnp.sum(share * change, axis=0, keepdims=True)
            slope = (share * (change - level) * HEAD ** (-0.5)).astype(bf16)
            at = slice(head * HEAD, (head + 1) * HEAD)
            queries_t[at, :] = mxu(keys_t[at, :], slope)
            slopes.append(slope)
        grad_key = mxu(jnp.concatenate(slopes, axis=0), query)
        split = [slice(h * WIN, (h + 1) * WIN) for h in range(GROUP)]
        joined[:, width + g * 128 : width + (g + 1) * 128] = lanes_of([grad_key[s] for s in split]).astype(bf16)
        joined[:, 2 * width + g * 128 : 2 * width + (g + 1) * 128] = lanes_of(
            [grad_value[s] for s in split]
        ).astype(bf16)
    joined[:, :width] = queries_t[...].T.astype(bf16)


def backward(grad, weights, triple, keys_t, output):
    width = grad.shape[-1]
    return pl.pallas_call(
        backward_kernel,
        out_shape=shape((WIN, 3 * width), bf16),
        scratch_shapes=[pltpu.VMEM((width, WIN), f32)],
        compiler_params=params(),
        cost_estimate=cost(10**10, 2 * 10**7),
        name="backward",
    )(grad, weights, triple, keys_t, output)


def finish_kernel(grad, joined, tokens, packed, gain, own, lat, lon, both):
    grad_inputs = mxu(joined[...], packed[...], NT).astype(bf16)
    unit, scale = unit_rows(tokens[...].astype(f32))
    scaled = grad_inputs.astype(f32) * gain[...].reshape(1, -1)
    out = grad[...].astype(f32) + scale * (scaled - row_mean(scaled) - unit * row_mean(scaled * unit))
    for quad, piece in enumerate((own, lat, lon, both)):
        piece[...] = quadrant(out, quad).astype(bf16)


def finish(grad, joined, tokens, packed, gain):
    width = grad.shape[-1]
    return pl.pallas_call(
        finish_kernel,
        out_shape=[shape((QUAD, width), bf16)] * 4,
        compiler_params=params(),
        cost_estimate=cost(10**10, 2 * 10**6),
        name="finish",
    )(grad, joined, tokens, packed, gain)


def token_kernel(own, lat, lon, both, tokens):
    quads = [piece[...].astype(f32) for piece in (own, lat, lon, both)]
    for line in range(WLAT):
        for column in range(WLON):
            quad = (0 if line >= HALF_LAT else 1) + (0 if column >= HALF_LON else 2)
            inner = column % HALF_LON
            at = token_row(0, line % HALF_LAT, inner % 2, inner // 2)
            tokens[line, column] = quads[quad][at : at + LEVELS].astype(bf16)


def unpack_tokens(*pieces):
    width = pieces[0].shape[-1]
    return pl.pallas_call(
        token_kernel,
        out_shape=shape((WLAT, WLON, LEVELS, width), bf16),
        compiler_params=params(),
        name="unpack_tokens",
    )(*pieces)


def cell_kernel(same_here, same_next, other_here, other_next, gain, merged):
    width = same_here.shape[-1]
    upper = lax.axis_index("lev") == 1
    same = (same_here[...].astype(f32), same_next[...].astype(f32))
    other = (other_here[...].astype(f32), other_next[...].astype(f32))
    levels = (
        [jnp.where(upper, b, a) for a, b in zip(same, other)],
        [jnp.where(upper, a, b) for a, b in zip(same, other)],
    )
    blocks = {}
    for row, odd, below, inner in cell_places():
        for side in range(2):
            at = token_row(0, inner, side, 0)
            for part in range(2):
                blocks[row, side * 2 + odd, part] = levels[part][below][at : at + CELLS]
    for part in range(2):
        parts = [blocks[1, block, part] for block in range(4)]
        mean = sum(jnp.sum(x, axis=-1, keepdims=True) for x in parts) * (1 / (4 * width))
        parts = [x - mean for x in parts]
        spread = sum(jnp.sum(x * x, axis=-1, keepdims=True) for x in parts) * (1 / (4 * width))
        scale = lax.rsqrt(spread + epsilon)
        for block, x in enumerate(parts):
            blocks[1, block, part] = x * scale * gain[:, block * width : (block + 1) * width]
    for row in range(HALF_LAT):
        for pair in range(PAIRS):
            here = slice(pair * LEVELS, (pair + 1) * LEVELS)
            for block in range(4):
                merged[row, pair, :, block * width : (block + 1) * width] = jnp.concatenate(
                    (blocks[row, block, 0][here], blocks[row, block, 1][here]), axis=0
                ).astype(bf16)


def unpack_cells(pieces, gain):
    width = pieces[0].shape[-1]
    return pl.pallas_call(
        cell_kernel,
        out_shape=shape((HALF_LAT, PAIRS, 2 * LEVELS, 4 * width), bf16),
        compiler_params=params(),
        cost_estimate=cost(10**9, 10**6),
        name="unpack_cells",
    )(*pieces, gain)


def routes(sizes, target):
    lons, lats, levs = sizes

    def number(i, a, k):
        return ((i % lons) * lats + a % lats) * levs + k % levs

    return [
        (number(i, a, k), number(*target(i, a, k)))
        for i in range(lons)
        for a in range(lats)
        for k in range(levs)
    ]


def send(block, sizes, target, back=False):
    pairs = routes(sizes, target)
    if back:
        pairs = [(b, a) for a, b in pairs]
    return lax.ppermute(block, ("lon", "lat", "lev"), pairs)


FIRST = lambda i, a, k: (i - (1 - k), a - 1, k)
SECOND = lambda i, a, k: (i - k, a - 1, k)
THIRD = lambda i, a, k: (i - 1, a, k)
FOURTH = lambda i, a, k: (i - (1 - k), a, 1 - k)
FIFTH = lambda i, a, k: (i - (1 - k), a - 1, 1 - k)
LAT = lambda i, a, k: (i, a - 1, k)
LON = lambda i, a, k: (i - 1, a, k)
BOTH = lambda i, a, k: (i - 1, a - 1, k)
HERE = lambda i, a, k: (i - (1 - k), a, k)


def per_device(
    sizes,
    tokens,
    packed_weight,
    output_weight,
    norm_gain,
    merge_gain,
    bias_table,
    bias_index,
    row_labels,
    column_valid,
    merged_grad,
):
    own, first, second, third, kept, fourth, fifth, table, index = pack_pieces(
        tokens.transpose(1, 2, 0, 3), merged_grad.transpose(1, 2, 0, 3), bias_table, bias_index
    )
    first = send(first, sizes, FIRST)
    second = send(second, sizes, SECOND)
    third = send(third, sizes, THIRD)
    fourth = send(fourth, sizes, FOURTH)
    fifth = send(fifth, sizes, FIFTH)
    main, tail = window_bias(table, index, row_labels, column_valid)
    cell_gain = merge_gain.reshape(1, -1)
    weights, triple, keys_t, residual, data = forward(
        (own, first, second, third), packed_weight, output_weight, norm_gain, main, tail
    )
    scaled, moments, sent, *merged = cell_moments(
        residual, (kept, first, third, fourth, fifth), cell_gain
    )
    before = send(sent, sizes, lambda i, a, k: (i, a + 1, k))
    after = before if sizes[1] == 2 else send(sent, sizes, lambda i, a, k: (i, a - 1, k))
    merged = [send(x, sizes, target, True) for x, target in zip(merged, (HERE, FIRST, FOURTH, FIFTH))]
    grad = merge_back(residual, scaled, moments, before, after)
    joined = backward(grad, weights, triple, keys_t, output_weight)
    own, lat, lon, both = finish(grad, joined, data, packed_weight, norm_gain)
    lat, lon, both, *merged = lax.optimization_barrier((lat, lon, both, *merged))
    lat = send(lat, sizes, LAT, True)
    both = send(both, sizes, BOTH, True)
    lon = send(lon, sizes, LON, True)
    merged = unpack_cells(merged, cell_gain)
    merged, lat, both, lon = lax.optimization_barrier((merged, lat, both, lon))
    grads = unpack_tokens(own, lat, lon, both)
    return merged.transpose(2, 0, 1, 3), grads.transpose(2, 0, 1, 3)


def solution(mesh):
    sizes = tuple(mesh.shape[name] for name in ("lon", "lat", "lev"))
    placed = (
        P("lev", "lat", "lon", None),
        P(),
        P(),
        P(),
        P(),
        P("lev", "lat", None, None),
        P(),
        P("lat"),
        P(),
        P(None, "lat", ("lon", "lev"), None),
    )
    return jax.shard_map(
        functools.partial(per_device, sizes),
        mesh=mesh,
        in_specs=placed,
        out_specs=(P(None, "lat", ("lon", "lev"), None), P("lev", "lat", "lon", None)),
        check_vma=False,
    )
```

```python
import functools

import jax
import jax.numpy as jnp
from jax import lax
from jax.experimental import pallas as pl
from jax.experimental.pallas import tpu as pltpu
from jax.sharding import PartitionSpec as P

HEADS = 24
HEAD = 32
WLAT = 6
WLON = 12
HALF_LAT = WLAT // 2
HALF_LON = WLON // 2
LEVELS = 2
WIN = LEVELS * WLAT * WLON
QUAD = WIN // 4
PAIRS = HALF_LON // 2
CELLS = LEVELS * PAIRS
GROUP = 128 // HEAD
TAIL = WIN - 128
TAIL_GROUPS = WIN // 8
BLOCKED = -1e30

epsilon = 1e-05
f32 = jnp.float32
bf16 = jnp.bfloat16

NN = (((1,), (0,)), ((), ()))
NT = (((1,), (1,)), ((), ()))


def token_row(quad, row, side, pair):
    return quad * QUAD + ((row * 2 + side) * PAIRS + pair) * LEVELS


def split_tokens(t):
    def digit(rest, size, count):
        found = jnp.zeros_like(rest)
        for i in range(1, count):
            found = found + (rest >= i * size).astype(jnp.int32)
        return found, rest - found * size

    quad, rest = digit(t, QUAD, 4)
    row, rest = digit(rest, 2 * CELLS, HALF_LAT)
    side, rest = digit(rest, CELLS, 2)
    pair, level = digit(rest, LEVELS, PAIRS)
    right, below = digit(quad, 2, 2)
    row = row + HALF_LAT * below
    column = right * HALF_LON + 2 * pair + side
    return row, column, level, right


def token_places(dims, axis):
    return split_tokens(lax.broadcasted_iota(jnp.int32, dims, axis))


def mxu(a, b, dims=NN):
    return lax.dot_general(a, b, dims, preferred_element_type=f32)


def exact(a, b):
    return lax.dot_general(a, b, NN, precision=lax.Precision.HIGHEST, preferred_element_type=f32)


def params(megabytes=12):
    return pltpu.CompilerParams(vmem_limit_bytes=megabytes << 20)


def shape(dims, dtype):
    return jax.ShapeDtypeStruct(dims, dtype)


def cost(flops, nbytes):
    return pl.CostEstimate(flops=flops, bytes_accessed=nbytes, transcendentals=0)


def in_hbm(*arrays):
    return [pltpu.with_memory_space_constraint(x, pltpu.MemorySpace.HBM) for x in arrays]


def start_copies(done, *pairs):
    copies = [pltpu.make_async_copy(source, target, done.at[i]) for i, (source, target) in enumerate(pairs)]
    for copy in copies:
        copy.start()
    return copies


def quadrant(values, quad):
    return values[quad * QUAD : (quad + 1) * QUAD]


def cell_places():
    return [(0, 0, True, 0), (0, 1, True, 1), (1, 0, True, 2), (1, 1, False, 0), (2, 0, False, 1), (2, 1, False, 2)]


def pack_kernel(
    tokens_at, grad_at, table_at, index_at, own, first, second, third, kept, fourth, fifth, table, index,
    tokens, grad, rows, cells, done,
):
    width = tokens.shape[-1]
    copies = start_copies(done, (tokens_at, tokens), (grad_at, grad), (index_at, index), (table_at.at[0, 0], table))
    copies[0].wait()
    for line in range(WLAT):
        for column in range(WLON):
            quad = (0 if line >= HALF_LAT else 1) + (0 if column >= HALF_LON else 2)
            inner = column % HALF_LON
            at = token_row(quad, line % HALF_LAT, inner % 2, inner // 2)
            rows[at : at + LEVELS, :] = tokens[line, column].astype(f32)
    copies[1].wait()
    upper = lax.axis_index("lev") == 1
    for row, odd, below, inner in cell_places():
        for pair in range(PAIRS):
            for side in range(2):
                block = side * 2 + odd
                part = grad[row, pair, :, block * width : (block + 1) * width].astype(f32)
                low, high = part[:LEVELS], part[LEVELS:]
                at = token_row(int(below), inner, side, pair)
                cells[at : at + LEVELS, :] = jnp.where(upper, high, low)
                at = at + 2 * QUAD
                cells[at : at + LEVELS, :] = jnp.where(upper, low, high)
    data, grads = rows[...], cells[...]
    lat, lon, both = quadrant(data, 1), quadrant(data, 2), quadrant(data, 3)
    here, below = quadrant(grads, 0), quadrant(grads, 1)
    own[...] = quadrant(data, 0).astype(bf16)
    first[...] = jnp.concatenate((jnp.where(upper, lat, both), below), axis=0).astype(bf16)
    second[...] = jnp.where(upper, both, lat).astype(bf16)
    third[...] = jnp.concatenate((lon, here), axis=0).astype(bf16)
    kept[...] = here.astype(bf16)
    fourth[...] = quadrant(grads, 2).astype(bf16)
    fifth[...] = quadrant(grads, 3).astype(bf16)
    copies[2].wait()
    copies[3].wait()


def pack_pieces(tokens, grad, table, index):
    width = tokens.shape[-1]
    piece, double = shape((QUAD, width), bf16), shape((2 * QUAD, width), bf16)
    return pl.pallas_call(
        pack_kernel,
        out_shape=[piece, double, piece, double, piece, piece, piece]
        + [shape(table.shape[2:], f32), shape(index.shape, jnp.int32)],
        in_specs=[pl.BlockSpec(memory_space=pltpu.MemorySpace.HBM)] * 4,
        scratch_shapes=[
            pltpu.VMEM(tokens.shape, bf16),
            pltpu.VMEM(grad.shape, bf16),
            pltpu.VMEM((WIN, width), f32),
            pltpu.VMEM((WIN, width), f32),
            pltpu.SemaphoreType.DMA((4,)),
        ],
        compiler_params=params(),
        name="pack",
    )(*in_hbm(tokens, grad, table, index))


def index_kernel(
    index, labels_at, valid_at, high, low, fine_high, fine_low, mask, mask_tail, labels, valid, rest_rows, done
):
    copies = start_copies(done, (labels_at, labels), (valid_at, valid))
    row_k, column_k, level_k, _ = token_places((WIN, 1), 0)
    row_q, _, _, _ = token_places((1, WIN), 1)
    natural = (level_k * WLAT + row_k) * WLON + column_k
    columns = lax.broadcasted_iota(jnp.int32, (WIN, WIN), 1)
    rows = lax.broadcasted_iota(jnp.int32, (WIN, WIN), 0)
    permute = jnp.where(natural == columns, 1.0, 0.0).astype(bf16)
    def place(values, out):
        moved = mxu(mxu(permute, values.astype(f32).astype(bf16), NT).astype(bf16), permute, NT)
        out[0:WIN, :] = moved[:, :128]
        rest_rows[...] = jnp.concatenate((moved[:, 128:], jnp.zeros((WIN, 128 - TAIL), f32)), axis=1)
        total = None
        for g in range(8):
            piece = rest_rows[pl.ds(g, TAIL_GROUPS, stride=8), :]
            if g:
                piece = pltpu.roll(piece, TAIL * g, 1)
            total = piece if total is None else total + piece
        out[WIN : WIN + TAIL_GROUPS, :] = total

    entry = index[...]
    place(lax.shift_right_logical(entry, 8), high)
    place(entry & 255, low)
    upper, lower = high[...], low[...]
    far = lower >= 128.0
    fine_high[...] = (2.0 * upper + jnp.where(far, 1.0, 0.0)).astype(jnp.int32)
    fine_low[...] = jnp.where(far, lower - 128.0, lower).astype(jnp.int32)
    for copy in copies:
        copy.wait()

    label_q, label_k = jnp.zeros_like(row_q), jnp.zeros_like(row_k)
    for r in range(WLAT):
        label_q = jnp.where(row_q == r, labels[r], label_q)
        label_k = jnp.where(row_k == r, labels[r], label_k)
    valid_k = jnp.zeros_like(column_k)
    start = lax.axis_index("lon") * WLON + HALF_LON
    total = valid.shape[0]
    for c in range(WLON):
        at = start + c
        at = jnp.where(at >= total, at - total, at)
        valid_k = jnp.where(column_k == c, valid[at], valid_k)
    seen = (label_k == label_q) & ((valid_k > 0) | (rows == columns))
    added = jnp.where(seen, 0.0, BLOCKED).astype(f32)
    mask[...] = added[:, :128]
    mask_tail[...] = jnp.concatenate((added[:, 128:], jnp.zeros((WIN, 128 - TAIL), f32)), axis=1)


def window_index(index, labels, valid):
    rows = (WIN + TAIL_GROUPS, 128)
    return pl.pallas_call(
        index_kernel,
        out_shape=[shape(rows, f32)] * 2 + [shape(rows, jnp.int32)] * 2 + [shape((WIN, 128), f32)] * 2,
        in_specs=[pl.BlockSpec(memory_space=pltpu.MemorySpace.VMEM)]
        + [pl.BlockSpec(memory_space=pltpu.MemorySpace.HBM)] * 2,
        scratch_shapes=[
            pltpu.SMEM(labels.shape, jnp.int32),
            pltpu.SMEM(valid.shape, jnp.int32),
            pltpu.VMEM((WIN, 128), f32),
            pltpu.SemaphoreType.DMA((2,)),
        ],
        compiler_params=params(),
        cost_estimate=cost(10**8, 10**6),
        name="index",
    )(index, *in_hbm(labels, valid))


def bias_kernel(table, high, low, fine_high, fine_low, mask, mask_tail, main, tail, split, fine):
    heads, entries = table.shape
    chunks = (entries + 255) // 256
    small_chunks = (entries + 127) // 128
    for c in range(small_chunks):
        size = min(128, entries - c * 128)
        part = table[:, c * 128 : c * 128 + size]
        if size < 128:
            part = jnp.concatenate((part, jnp.zeros((heads, 128 - size), f32)), axis=1)
        fine[:, c * 128 : (c + 1) * 128] = part
    for c in range(chunks):
        size = min(256, entries - c * 256)
        part = table[:, c * 256 : c * 256 + size]
        if size < 256:
            part = jnp.concatenate((part, jnp.zeros((heads, 256 - size), f32)), axis=1)
        coarse = part.astype(bf16).astype(f32)
        split[c * heads : (c + 1) * heads, :] = coarse
        split[(chunks + c) * heads : (chunks + c + 1) * heads, :] = part - coarse
    source = split[...].astype(bf16)
    part_rows = chunks * heads

    depth = lax.broadcasted_iota(jnp.int32, (256, 128), 0).astype(f32).astype(bf16)
    one, zero = jnp.ones((), bf16), jnp.zeros((), bf16)

    def pick(chunk, parts, count):
        found = [None] * (heads // 8)
        for c in range(count):
            hit = chunk == c
            for block in range(heads // 8):
                a = parts(c, block)
                found[block] = a if c == 0 else jnp.where(hit, a, found[block])
        return found

    def gathered(row):
        chunk = jnp.broadcast_to(fine_high[pl.ds(row, 1), :], (8, 128))
        lane = jnp.broadcast_to(fine_low[pl.ds(row, 1), :], (8, 128))

        def part(c, block):
            values = fine[block * 8 : block * 8 + 8, c * 128 : (c + 1) * 128]
            return jnp.take_along_axis(values, lane, axis=1, mode="promise_in_bounds")

        return pick(chunk, part, small_chunks)

    def lookup(row):
        if row // 2 % 4 == 3:
            return [gathered(row), gathered(row + 1)]
        hot = []
        for j in range(2):
            lane = jnp.broadcast_to(low[pl.ds(row + j, 1), :], (16, 128)).astype(bf16)
            hot.append(jnp.where(depth == jnp.concatenate([lane] * 16, axis=0), one, zero))
        product = mxu(source, jnp.concatenate(hot, axis=1))
        out = []
        for j in range(2):
            chunk = jnp.broadcast_to(high[pl.ds(row + j, 1), :], (8, 128))
            halves = []
            for begin in (0, part_rows):

                def part(c, block):
                    at = begin + c * heads + block * 8
                    return product[at : at + 8, j * 128 : (j + 1) * 128]

                halves.append(pick(chunk, part, chunks))
            out.append([a + b for a, b in zip(*halves)])
        return out

    for key in range(0, WIN, 2):
        for j, found in enumerate(lookup(key)):
            extra = jnp.broadcast_to(mask[key + j : key + j + 1, :], (8, 128))
            for block, value in enumerate(found):
                main[pl.ds(block * 8 * WIN + key + j, 8, stride=WIN), :] = value + extra
    for row in range(0, TAIL_GROUPS, 2):
        for j, found in enumerate(lookup(WIN + row)):
            for block, value in enumerate(found):
                for g in range(8):
                    key = (row + j) * 8 + g
                    moved = pltpu.roll(value, 128 - TAIL * g, 1) if g else value
                    extra = jnp.broadcast_to(mask_tail[key : key + 1, :], (8, 128))
                    tail[pl.ds(block * 8 * WIN + key, 8, stride=WIN), :] = moved + extra


def window_bias(table, places):
    heads, entries = table.shape
    whole = (entries + 255) // 256
    return pl.pallas_call(
        bias_kernel,
        out_shape=[shape((heads * WIN, 128), f32)] * 2,
        scratch_shapes=[
            pltpu.VMEM((2 * whole * heads, 256), f32),
            pltpu.VMEM((heads, (entries + 127) // 128 * 128), f32),
        ],
        compiler_params=params(),
        cost_estimate=cost(10**10, 2 * 10**7),
        name="bias",
    )(table, *places)


def row_mean(values):
    return jnp.mean(values, axis=-1, keepdims=True)


def unit_rows(data):
    center = data - row_mean(data)
    scale = lax.rsqrt(row_mean(center * center) + epsilon)
    return center * scale, scale


def stacked(block):
    lane = lax.broadcasted_iota(jnp.int32, (1, 128), 1) // HEAD
    return jnp.concatenate(
        [jnp.where(lane == h, block, jnp.zeros((), block.dtype)) for h in range(GROUP)], axis=0
    )


def lanes_of(parts):
    lane = lax.broadcasted_iota(jnp.int32, (1, 128), 1) // HEAD
    out = parts[0]
    for h in range(1, GROUP):
        out = jnp.where(lane == h, parts[h], out)
    return out


def forward_kernel(
    own, first, second, third, packed, output, gain, main, tail,
    weights, triple, keys_t, residual, tokens,
    gathered, values_t, heads_t,
):
    width = own.shape[-1]
    upper = lax.axis_index("lev") == 1
    a, b = first[...].astype(f32)[:QUAD], second[...].astype(f32)
    lon = third[...].astype(f32)[:QUAD]
    for quad, piece in enumerate((own[...].astype(f32), jnp.where(upper, a, b), lon, jnp.where(upper, b, a))):
        gathered[quad * QUAD : (quad + 1) * QUAD, :] = piece
    data = gathered[...]
    tokens[...] = data.astype(bf16)
    unit, _ = unit_rows(data)
    normed = (unit * gain[...].reshape(1, -1)).astype(bf16)
    triple[...] = mxu(normed, packed[...]).astype(bf16)
    keys_t[...] = triple[:, width : 2 * width].astype(f32).T.astype(bf16)
    values_t[...] = triple[:, 2 * width :].astype(f32).T.astype(bf16)
    for g in range(width // 128):
        query = triple[:, g * 128 : (g + 1) * 128]
        key = triple[:, width + g * 128 : width + (g + 1) * 128]
        product = mxu(stacked(key), query, NT) * HEAD ** (-0.5)
        for h in range(GROUP):
            head = g * GROUP + h
            at = slice(head * WIN, (head + 1) * WIN)
            bias = jnp.concatenate((main[at, :], tail[at, :TAIL]), axis=1)
            scores = product[h * WIN : (h + 1) * WIN] + bias
            raised = jnp.exp(scores - jnp.max(scores, axis=0, keepdims=True))
            share = (raised * (1.0 / jnp.sum(raised, axis=0, keepdims=True))).astype(bf16)
            weights[at, :] = share
            here = slice(head * HEAD, (head + 1) * HEAD)
            heads_t[here, :] = mxu(values_t[here, :], share)
    heads = heads_t[...].T.astype(bf16)
    attended = mxu(heads, output[...]).astype(bf16)
    residual[...] = (data + attended.astype(f32)).astype(bf16)


def forward(pieces, packed, output, gain, main, tail):
    width = output.shape[0]
    return pl.pallas_call(
        forward_kernel,
        out_shape=[
            shape((HEADS * WIN, WIN), bf16),
            shape((WIN, 3 * width), bf16),
            shape((width, WIN), bf16),
            shape((WIN, width), bf16),
            shape((WIN, width), bf16),
        ],
        scratch_shapes=[
            pltpu.VMEM((WIN, width), f32),
            pltpu.VMEM((width, WIN), bf16),
            pltpu.VMEM((width, WIN), f32),
        ],
        compiler_params=params(),
        cost_estimate=cost(10**10, 2 * 10**7),
        name="forward",
    )(*pieces, packed, output, gain, main, tail)


def gain_rows(gain, out):
    width = out.shape[-1]
    for quad in range(4):
        for row in range(HALF_LAT):
            odd = 1 - (row + (quad & 1) * HALF_LAT) % 2
            for side in range(2):
                block = side * 2 + odd
                at = token_row(quad, row, side, 0)
                factor = gain[:, block * width : (block + 1) * width]
                out[at : at + CELLS, :] = jnp.broadcast_to(factor, (CELLS, width))


def cell_number(places):
    row, column, level, right = places
    band = lax.shift_right_logical(row + 1, 1)
    return (band * HALF_LON + lax.shift_right_logical(column, 1)) * LEVELS + level


def split_row(places):
    return (places[0] == 0) | (places[0] == WLAT - 1)


def sent_tokens(dims, axis):
    i = lax.broadcasted_iota(jnp.int32, dims, axis)
    last = (i >= 2 * CELLS).astype(jnp.int32)
    i = i - last * 2 * CELLS
    right = (i >= CELLS).astype(jnp.int32)
    cell = i - right * CELLS
    return (2 * right + last) * QUAD + last * (HALF_LAT - 1) * 2 * CELLS + cell


def columns_of(parts):
    lane = lax.broadcasted_iota(jnp.int32, (1, 128), 1)
    out = jnp.zeros((WIN, 128), f32)
    for i, part in enumerate(parts):
        out = jnp.where(lane == i, part, out)
    return out


def moments_kernel(residual, kept, first, third, fourth, fifth, gain, scaled, moments, sent, same_here, same_next, other_here, other_next, factors):
    width = residual.shape[-1]
    upper = lax.axis_index("lev") == 1
    own, a, b = kept[...].astype(f32), fourth[...].astype(f32), fifth[...].astype(f32)
    below, right = first[...].astype(f32)[QUAD:], third[...].astype(f32)[QUAD:]
    gain_rows(gain, factors)
    for quad, part in enumerate((
        jnp.where(upper, own, a),
        jnp.where(upper, below, b),
        jnp.where(upper, a, right),
        jnp.where(upper, b, below),
    )):
        scaled[quad * QUAD : (quad + 1) * QUAD, :] = part
    grad = scaled[...] * factors[...]
    scaled[...] = grad
    data = residual[...].astype(f32)
    down = token_places((WIN, 1), 0)
    grouping = jnp.where(cell_number(down) == cell_number(token_places((1, WIN), 1)), 1.0, 0.0).astype(f32)
    inverse = jnp.where(split_row(down), 1 / (2 * width), 1 / (4 * width)).astype(f32)
    total = jnp.sum(data, axis=-1, keepdims=True)
    middle = exact(grouping, jnp.broadcast_to(total, (WIN, 128)))[:, 0:1] * inverse
    center = data - middle
    sums = columns_of((
        jnp.sum(center * center, axis=-1, keepdims=True),
        jnp.sum(grad, axis=-1, keepdims=True),
        jnp.sum(grad * center, axis=-1, keepdims=True),
    ))
    sums = exact(grouping, sums)
    lane = lax.broadcasted_iota(jnp.int32, (1, 128), 1)
    sums = jnp.where(lane == 3, middle, sums)
    moments[...] = sums
    pick = sent_tokens((4 * CELLS, 1), 0) == lax.broadcasted_iota(jnp.int32, (4 * CELLS, WIN), 1)
    sent[...] = exact(jnp.where(pick, 1.0, 0.0).astype(f32), sums)
    scale = lax.rsqrt(sums[:, 0:1] * (1 / (4 * width)) + epsilon)
    out = jnp.where(split_row(down), data, center * scale * factors[...])
    parts = [quadrant(out, quad) for quad in range(4)]
    same_here[...] = jnp.where(upper, parts[0], parts[2]).astype(bf16)
    same_next[...] = jnp.where(upper, parts[1], parts[3]).astype(bf16)
    other_here[...] = jnp.where(upper, parts[2], parts[0]).astype(bf16)
    other_next[...] = jnp.where(upper, parts[3], parts[1]).astype(bf16)


def cell_moments(residual, pieces, gain):
    width = residual.shape[-1]
    return pl.pallas_call(
        moments_kernel,
        out_shape=[shape((WIN, width), f32), shape((WIN, 128), f32), shape((4 * CELLS, 128), f32)]
        + [shape((QUAD, width), bf16)] * 4,
        scratch_shapes=[pltpu.VMEM((WIN, width), f32)],
        compiler_params=params(),
        cost_estimate=cost(10**8, 10**6),
        name="moments",
    )(residual, *pieces, gain)


def merge_kernel(residual, scaled, moments, before, after, grad):
    width = residual.shape[-1]
    down = token_places((WIN, 1), 0)
    shared = split_row(down)
    row = down[0]
    sender = split_tokens(sent_tokens((1, 4 * CELLS), 1))
    match = (cell_number(down) == cell_number(sender)) & shared
    there = jnp.concatenate((before[2 * CELLS :], after[: 2 * CELLS]), axis=0)
    theirs = exact(jnp.where(match, 1.0, 0.0).astype(f32), there)
    mine = moments[...]
    full = 4.0 * width
    middle = jnp.where(shared, 0.5 * (mine[:, 3:4] + theirs[:, 3:4]), mine[:, 3:4])
    gap = theirs[:, 3:4] - mine[:, 3:4]
    square = jnp.where(shared, mine[:, 0:1] + theirs[:, 0:1] + gap * gap * width, mine[:, 0:1])
    scale = lax.rsqrt(square / full + epsilon)
    grad_sum = jnp.where(shared, mine[:, 1:2] + theirs[:, 1:2], mine[:, 1:2])
    cross = jnp.where(
        shared,
        mine[:, 2:3] + (mine[:, 3:4] - middle) * mine[:, 1:2]
        + theirs[:, 2:3] + (theirs[:, 3:4] - middle) * theirs[:, 1:2],
        mine[:, 2:3],
    )
    unit = (residual[...].astype(f32) - middle) * scale
    grad[...] = (scale * (scaled[...] - grad_sum / full - unit * (cross * scale / full))).astype(bf16)


def merge_back(residual, scaled, moments, before, after):
    return pl.pallas_call(
        merge_kernel,
        out_shape=shape(residual.shape, bf16),
        compiler_params=params(),
        cost_estimate=cost(10**8, 10**6),
        name="merge",
    )(residual, scaled, moments, before, after)


def backward_kernel(grad, weights, triple, keys_t, output, joined, queries_t):
    width = grad.shape[-1]
    upstream = grad[...]
    grad_heads = mxu(upstream, output[...], NT).astype(bf16)
    for g in range(width // 128):
        here = slice(g * 128, (g + 1) * 128)
        query = triple[:, g * 128 : (g + 1) * 128]
        value = triple[:, 2 * width + g * 128 : 2 * width + (g + 1) * 128]
        arriving = grad_heads[:, here]
        product = mxu(stacked(value), arriving, NT)
        shares = weights[g * GROUP * WIN : (g + 1) * GROUP * WIN, :]
        grad_value = mxu(shares, arriving)
        slopes = []
        for h in range(GROUP):
            head = g * GROUP + h
            share = shares[h * WIN : (h + 1) * WIN].astype(f32)
            change = product[h * WIN : (h + 1) * WIN]
            level = jnp.sum(share * change, axis=0, keepdims=True)
            slope = (share * (change - level) * HEAD ** (-0.5)).astype(bf16)
            at = slice(head * HEAD, (head + 1) * HEAD)
            queries_t[at, :] = mxu(keys_t[at, :], slope)
            slopes.append(slope)
        grad_key = mxu(jnp.concatenate(slopes, axis=0), query)
        split = [slice(h * WIN, (h + 1) * WIN) for h in range(GROUP)]
        joined[:, width + g * 128 : width + (g + 1) * 128] = lanes_of([grad_key[s] for s in split]).astype(bf16)
        joined[:, 2 * width + g * 128 : 2 * width + (g + 1) * 128] = lanes_of(
            [grad_value[s] for s in split]
        ).astype(bf16)
    joined[:, :width] = queries_t[...].T.astype(bf16)


def backward(grad, weights, triple, keys_t, output):
    width = grad.shape[-1]
    return pl.pallas_call(
        backward_kernel,
        out_shape=shape((WIN, 3 * width), bf16),
        scratch_shapes=[pltpu.VMEM((width, WIN), f32)],
        compiler_params=params(),
        cost_estimate=cost(10**10, 2 * 10**7),
        name="backward",
    )(grad, weights, triple, keys_t, output)


def finish_kernel(grad, joined, tokens, packed, gain, own, lat, lon, both):
    grad_inputs = mxu(joined[...], packed[...], NT).astype(bf16)
    unit, scale = unit_rows(tokens[...].astype(f32))
    scaled = grad_inputs.astype(f32) * gain[...].reshape(1, -1)
    out = grad[...].astype(f32) + scale * (scaled - row_mean(scaled) - unit * row_mean(scaled * unit))
    for quad, piece in enumerate((own, lat, lon, both)):
        piece[...] = quadrant(out, quad).astype(bf16)


def finish(grad, joined, tokens, packed, gain):
    width = grad.shape[-1]
    return pl.pallas_call(
        finish_kernel,
        out_shape=[shape((QUAD, width), bf16)] * 4,
        compiler_params=params(),
        cost_estimate=cost(10**10, 2 * 10**6),
        name="finish",
    )(grad, joined, tokens, packed, gain)


def token_kernel(own, lat, lon, both, tokens):
    quads = [piece[...].astype(f32) for piece in (own, lat, lon, both)]
    for line in range(WLAT):
        for column in range(WLON):
            quad = (0 if line >= HALF_LAT else 1) + (0 if column >= HALF_LON else 2)
            inner = column % HALF_LON
            at = token_row(0, line % HALF_LAT, inner % 2, inner // 2)
            tokens[line, column] = quads[quad][at : at + LEVELS].astype(bf16)


def unpack_tokens(*pieces):
    width = pieces[0].shape[-1]
    return pl.pallas_call(
        token_kernel,
        out_shape=shape((WLAT, WLON, LEVELS, width), bf16),
        compiler_params=params(),
        name="unpack_tokens",
    )(*pieces)


def cell_kernel(same_here, same_next, other_here, other_next, gain, merged):
    width = same_here.shape[-1]
    upper = lax.axis_index("lev") == 1
    same = (same_here[...].astype(f32), same_next[...].astype(f32))
    other = (other_here[...].astype(f32), other_next[...].astype(f32))
    levels = (
        [jnp.where(upper, b, a) for a, b in zip(same, other)],
        [jnp.where(upper, a, b) for a, b in zip(same, other)],
    )
    blocks = {}
    for row, odd, below, inner in cell_places():
        for side in range(2):
            at = token_row(0, inner, side, 0)
            for part in range(2):
                blocks[row, side * 2 + odd, part] = levels[part][below][at : at + CELLS]
    for part in range(2):
        parts = [blocks[1, block, part] for block in range(4)]
        mean = sum(jnp.sum(x, axis=-1, keepdims=True) for x in parts) * (1 / (4 * width))
        parts = [x - mean for x in parts]
        spread = sum(jnp.sum(x * x, axis=-1, keepdims=True) for x in parts) * (1 / (4 * width))
        scale = lax.rsqrt(spread + epsilon)
        for block, x in enumerate(parts):
            blocks[1, block, part] = x * scale * gain[:, block * width : (block + 1) * width]
    for row in range(HALF_LAT):
        for pair in range(PAIRS):
            here = slice(pair * LEVELS, (pair + 1) * LEVELS)
            for block in range(4):
                merged[row, pair, :, block * width : (block + 1) * width] = jnp.concatenate(
                    (blocks[row, block, 0][here], blocks[row, block, 1][here]), axis=0
                ).astype(bf16)


def unpack_cells(pieces, gain):
    width = pieces[0].shape[-1]
    return pl.pallas_call(
        cell_kernel,
        out_shape=shape((HALF_LAT, PAIRS, 2 * LEVELS, 4 * width), bf16),
        compiler_params=params(),
        cost_estimate=cost(10**9, 10**6),
        name="unpack_cells",
    )(*pieces, gain)


def routes(sizes, target):
    lons, lats, levs = sizes

    def number(i, a, k):
        return ((i % lons) * lats + a % lats) * levs + k % levs

    return [
        (number(i, a, k), number(*target(i, a, k)))
        for i in range(lons)
        for a in range(lats)
        for k in range(levs)
    ]


def send(block, sizes, target, back=False):
    pairs = routes(sizes, target)
    if back:
        pairs = [(b, a) for a, b in pairs]
    return lax.ppermute(block, ("lon", "lat", "lev"), pairs)


FIRST = lambda i, a, k: (i - (1 - k), a - 1, k)
SECOND = lambda i, a, k: (i - k, a - 1, k)
THIRD = lambda i, a, k: (i - 1, a, k)
FOURTH = lambda i, a, k: (i - (1 - k), a, 1 - k)
FIFTH = lambda i, a, k: (i - (1 - k), a - 1, 1 - k)
LAT = lambda i, a, k: (i, a - 1, k)
LON = lambda i, a, k: (i - 1, a, k)
BOTH = lambda i, a, k: (i - 1, a - 1, k)
HERE = lambda i, a, k: (i - (1 - k), a, k)


def per_device(
    sizes,
    tokens,
    packed_weight,
    output_weight,
    norm_gain,
    merge_gain,
    bias_table,
    bias_index,
    row_labels,
    column_valid,
    merged_grad,
):
    own, first, second, third, kept, fourth, fifth, table, index = pack_pieces(
        tokens.transpose(1, 2, 0, 3), merged_grad.transpose(1, 2, 0, 3), bias_table, bias_index
    )
    first = send(first, sizes, FIRST)
    second = send(second, sizes, SECOND)
    third = send(third, sizes, THIRD)
    places = window_index(index, row_labels, column_valid)
    fourth, fifth, *places = lax.optimization_barrier((fourth, fifth, *places))
    fourth = send(fourth, sizes, FOURTH)
    fifth = send(fifth, sizes, FIFTH)
    main, tail = window_bias(table, places)
    cell_gain = merge_gain.reshape(1, -1)
    weights, triple, keys_t, residual, data = forward(
        (own, first, second, third), packed_weight, output_weight, norm_gain, main, tail
    )
    scaled, moments, sent, *merged = cell_moments(
        residual, (kept, first, third, fourth, fifth), cell_gain
    )
    before = send(sent, sizes, lambda i, a, k: (i, a + 1, k))
    after = before if sizes[1] == 2 else send(sent, sizes, lambda i, a, k: (i, a - 1, k))
    same_here, same_next, other_here, other_next = merged
    other_next = send(other_next, sizes, FIFTH, True)
    same_next = send(same_next, sizes, FIRST, True)
    other_here = send(other_here, sizes, FOURTH, True)
    same_here = send(same_here, sizes, HERE, True)
    grad = merge_back(residual, scaled, moments, before, after)
    joined = backward(grad, weights, triple, keys_t, output_weight)
    own, lat, lon, both = finish(grad, joined, data, packed_weight, norm_gain)
    other_next, same_next, lat, both, lon = lax.optimization_barrier((other_next, same_next, lat, both, lon))
    lat = send(lat, sizes, LAT, True)
    both = send(both, sizes, BOTH, True)
    lon = send(lon, sizes, LON, True)
    merged = unpack_cells((same_here, same_next, other_here, other_next), cell_gain)
    merged, lat, both, lon = lax.optimization_barrier((merged, lat, both, lon))
    grads = unpack_tokens(own, lat, lon, both)
    return merged.transpose(2, 0, 1, 3), grads.transpose(2, 0, 1, 3)


def solution(mesh):
    sizes = tuple(mesh.shape[name] for name in ("lon", "lat", "lev"))
    placed = (
        P("lev", "lat", "lon", None),
        P(),
        P(),
        P(),
        P(),
        P("lev", "lat", None, None),
        P(),
        P("lat"),
        P(),
        P(None, "lat", ("lon", "lev"), None),
    )
    return jax.shard_map(
        functools.partial(per_device, sizes),
        mesh=mesh,
        in_specs=placed,
        out_specs=(P(None, "lat", ("lon", "lev"), None), P("lev", "lat", "lon", None)),
        check_vma=False,
    )
```

```python
import functools

import jax
import jax.numpy as jnp
from jax import lax
from jax.experimental import pallas as pl
from jax.experimental.pallas import tpu as pltpu
from jax.sharding import PartitionSpec as P

HEADS = 24
HEAD = 32
WLAT = 6
WLON = 12
HALF_LAT = WLAT // 2
HALF_LON = WLON // 2
LEVELS = 2
WIN = LEVELS * WLAT * WLON
QUAD = WIN // 4
PAIRS = HALF_LON // 2
CELLS = LEVELS * PAIRS
GROUP = 128 // HEAD
TAIL = WIN - 128
TAIL_GROUPS = WIN // 8
BLOCKED = -1e30

epsilon = 1e-05
f32 = jnp.float32
bf16 = jnp.bfloat16

NN = (((1,), (0,)), ((), ()))
NT = (((1,), (1,)), ((), ()))


def token_row(quad, row, side, pair):
    return quad * QUAD + ((row * 2 + side) * PAIRS + pair) * LEVELS


def split_tokens(t):
    def digit(rest, size, count):
        found = jnp.zeros_like(rest)
        for i in range(1, count):
            found = found + (rest >= i * size).astype(jnp.int32)
        return found, rest - found * size

    quad, rest = digit(t, QUAD, 4)
    row, rest = digit(rest, 2 * CELLS, HALF_LAT)
    side, rest = digit(rest, CELLS, 2)
    pair, level = digit(rest, LEVELS, PAIRS)
    right, below = digit(quad, 2, 2)
    row = row + HALF_LAT * below
    column = right * HALF_LON + 2 * pair + side
    return row, column, level, right


def token_places(dims, axis):
    return split_tokens(lax.broadcasted_iota(jnp.int32, dims, axis))


def mxu(a, b, dims=NN):
    return lax.dot_general(a, b, dims, preferred_element_type=f32)


def exact(a, b):
    return lax.dot_general(a, b, NN, precision=lax.Precision.HIGHEST, preferred_element_type=f32)


def params(megabytes=12):
    return pltpu.CompilerParams(vmem_limit_bytes=megabytes << 20)


def shape(dims, dtype):
    return jax.ShapeDtypeStruct(dims, dtype)


def cost(flops, nbytes):
    return pl.CostEstimate(flops=flops, bytes_accessed=nbytes, transcendentals=0)


def in_hbm(*arrays):
    return [pltpu.with_memory_space_constraint(x, pltpu.MemorySpace.HBM) for x in arrays]


def start_copies(done, *pairs):
    copies = [pltpu.make_async_copy(source, target, done.at[i]) for i, (source, target) in enumerate(pairs)]
    for copy in copies:
        copy.start()
    return copies


def quadrant(values, quad):
    return values[quad * QUAD : (quad + 1) * QUAD]


def cell_places():
    return [(0, 0, True, 0), (0, 1, True, 1), (1, 0, True, 2), (1, 1, False, 0), (2, 0, False, 1), (2, 1, False, 2)]


def pack_kernel(
    tokens_at, grad_at, table_at, index_at, own, first, second, third, kept, fourth, fifth, table, index,
    tokens, grad, rows, cells, done,
):
    width = tokens.shape[-1]
    copies = start_copies(done, (tokens_at, tokens), (grad_at, grad), (index_at, index), (table_at.at[0, 0], table))
    copies[0].wait()
    for line in range(WLAT):
        for column in range(WLON):
            quad = (0 if line >= HALF_LAT else 1) + (0 if column >= HALF_LON else 2)
            inner = column % HALF_LON
            at = token_row(quad, line % HALF_LAT, inner % 2, inner // 2)
            rows[at : at + LEVELS, :] = tokens[line, column].astype(f32)
    copies[1].wait()
    upper = lax.axis_index("lev") == 1
    for row, odd, below, inner in cell_places():
        for pair in range(PAIRS):
            for side in range(2):
                block = side * 2 + odd
                part = grad[row, pair, :, block * width : (block + 1) * width].astype(f32)
                low, high = part[:LEVELS], part[LEVELS:]
                at = token_row(int(below), inner, side, pair)
                cells[at : at + LEVELS, :] = jnp.where(upper, high, low)
                at = at + 2 * QUAD
                cells[at : at + LEVELS, :] = jnp.where(upper, low, high)
    data, grads = rows[...], cells[...]
    lat, lon, both = quadrant(data, 1), quadrant(data, 2), quadrant(data, 3)
    here, below = quadrant(grads, 0), quadrant(grads, 1)
    own[...] = quadrant(data, 0).astype(bf16)
    first[...] = jnp.concatenate((jnp.where(upper, lat, both), below), axis=0).astype(bf16)
    second[...] = jnp.where(upper, both, lat).astype(bf16)
    third[...] = jnp.concatenate((lon, here), axis=0).astype(bf16)
    kept[...] = here.astype(bf16)
    fourth[...] = quadrant(grads, 2).astype(bf16)
    fifth[...] = quadrant(grads, 3).astype(bf16)
    copies[2].wait()
    copies[3].wait()


def pack_pieces(tokens, grad, table, index):
    width = tokens.shape[-1]
    piece, double = shape((QUAD, width), bf16), shape((2 * QUAD, width), bf16)
    return pl.pallas_call(
        pack_kernel,
        out_shape=[piece, double, piece, double, piece, piece, piece]
        + [shape(table.shape[2:], f32), shape(index.shape, jnp.int32)],
        in_specs=[pl.BlockSpec(memory_space=pltpu.MemorySpace.HBM)] * 4,
        scratch_shapes=[
            pltpu.VMEM(tokens.shape, bf16),
            pltpu.VMEM(grad.shape, bf16),
            pltpu.VMEM((WIN, width), f32),
            pltpu.VMEM((WIN, width), f32),
            pltpu.SemaphoreType.DMA((4,)),
        ],
        compiler_params=params(),
        name="pack",
    )(*in_hbm(tokens, grad, table, index))


def index_kernel(
    index, labels_at, valid_at, high, low, fine_high, fine_low, mask, mask_tail, labels, valid, rest_rows, done
):
    copies = start_copies(done, (labels_at, labels), (valid_at, valid))
    row_k, column_k, level_k, _ = token_places((WIN, 1), 0)
    row_q, _, _, _ = token_places((1, WIN), 1)
    natural = (level_k * WLAT + row_k) * WLON + column_k
    columns = lax.broadcasted_iota(jnp.int32, (WIN, WIN), 1)
    rows = lax.broadcasted_iota(jnp.int32, (WIN, WIN), 0)
    permute = jnp.where(natural == columns, 1.0, 0.0).astype(bf16)
    def place(values, out):
        moved = mxu(mxu(permute, values.astype(f32).astype(bf16), NT).astype(bf16), permute, NT)
        out[0:WIN, :] = moved[:, :128]
        rest_rows[...] = jnp.concatenate((moved[:, 128:], jnp.zeros((WIN, 128 - TAIL), f32)), axis=1)
        total = None
        for g in range(8):
            piece = rest_rows[pl.ds(g, TAIL_GROUPS, stride=8), :]
            if g:
                piece = pltpu.roll(piece, TAIL * g, 1)
            total = piece if total is None else total + piece
        out[WIN : WIN + TAIL_GROUPS, :] = total

    entry = index[...]
    place(lax.shift_right_logical(entry, 8), high)
    place(entry & 255, low)
    upper, lower = high[...], low[...]
    far = lower >= 128.0
    fine_high[...] = (2.0 * upper + jnp.where(far, 1.0, 0.0)).astype(jnp.int32)
    fine_low[...] = jnp.where(far, lower - 128.0, lower).astype(jnp.int32)
    for copy in copies:
        copy.wait()

    label_q, label_k = jnp.zeros_like(row_q), jnp.zeros_like(row_k)
    for r in range(WLAT):
        label_q = jnp.where(row_q == r, labels[r], label_q)
        label_k = jnp.where(row_k == r, labels[r], label_k)
    valid_k = jnp.zeros_like(column_k)
    start = lax.axis_index("lon") * WLON + HALF_LON
    total = valid.shape[0]
    for c in range(WLON):
        at = start + c
        at = jnp.where(at >= total, at - total, at)
        valid_k = jnp.where(column_k == c, valid[at], valid_k)
    seen = (label_k == label_q) & ((valid_k > 0) | (rows == columns))
    added = jnp.where(seen, 0.0, BLOCKED).astype(f32)
    mask[...] = added[:, :128]
    mask_tail[...] = jnp.concatenate((added[:, 128:], jnp.zeros((WIN, 128 - TAIL), f32)), axis=1)


def window_index(index, labels, valid):
    rows = (WIN + TAIL_GROUPS, 128)
    return pl.pallas_call(
        index_kernel,
        out_shape=[shape(rows, f32)] * 2 + [shape(rows, jnp.int32)] * 2 + [shape((WIN, 128), f32)] * 2,
        in_specs=[pl.BlockSpec(memory_space=pltpu.MemorySpace.VMEM)]
        + [pl.BlockSpec(memory_space=pltpu.MemorySpace.HBM)] * 2,
        scratch_shapes=[
            pltpu.SMEM(labels.shape, jnp.int32),
            pltpu.SMEM(valid.shape, jnp.int32),
            pltpu.VMEM((WIN, 128), f32),
            pltpu.SemaphoreType.DMA((2,)),
        ],
        compiler_params=params(),
        cost_estimate=cost(10**8, 10**6),
        name="index",
    )(index, *in_hbm(labels, valid))


def bias_kernel(table, high, low, fine_high, fine_low, mask, mask_tail, main, tail, split, fine):
    heads, entries = table.shape
    chunks = (entries + 255) // 256
    small_chunks = (entries + 127) // 128
    for c in range(small_chunks):
        size = min(128, entries - c * 128)
        part = table[:, c * 128 : c * 128 + size]
        if size < 128:
            part = jnp.concatenate((part, jnp.zeros((heads, 128 - size), f32)), axis=1)
        fine[:, c * 128 : (c + 1) * 128] = part
    for c in range(chunks):
        size = min(256, entries - c * 256)
        part = table[:, c * 256 : c * 256 + size]
        if size < 256:
            part = jnp.concatenate((part, jnp.zeros((heads, 256 - size), f32)), axis=1)
        coarse = part.astype(bf16).astype(f32)
        split[c * heads : (c + 1) * heads, :] = coarse
        split[(chunks + c) * heads : (chunks + c + 1) * heads, :] = part - coarse
    source = split[...].astype(bf16)
    part_rows = chunks * heads

    depth = lax.broadcasted_iota(jnp.int32, (256, 128), 0).astype(f32).astype(bf16)
    one, zero = jnp.ones((), bf16), jnp.zeros((), bf16)

    def pick(chunk, parts, count):
        found = [None] * (heads // 8)
        for c in range(count):
            hit = chunk == c
            for block in range(heads // 8):
                a = parts(c, block)
                found[block] = a if c == 0 else jnp.where(hit, a, found[block])
        return found

    def gathered(row):
        chunk = jnp.broadcast_to(fine_high[pl.ds(row, 1), :], (8, 128))
        lane = jnp.broadcast_to(fine_low[pl.ds(row, 1), :], (8, 128))

        def part(c, block):
            values = fine[block * 8 : block * 8 + 8, c * 128 : (c + 1) * 128]
            return jnp.take_along_axis(values, lane, axis=1, mode="promise_in_bounds")

        return pick(chunk, part, small_chunks)

    def lookup(row):
        if row // 2 % 4 == 3:
            return [gathered(row), gathered(row + 1)]
        hot = []
        for j in range(2):
            lane = jnp.broadcast_to(low[pl.ds(row + j, 1), :], (16, 128)).astype(bf16)
            hot.append(jnp.where(depth == jnp.concatenate([lane] * 16, axis=0), one, zero))
        product = mxu(source, jnp.concatenate(hot, axis=1))
        out = []
        for j in range(2):
            chunk = jnp.broadcast_to(high[pl.ds(row + j, 1), :], (8, 128))
            halves = []
            for begin in (0, part_rows):

                def part(c, block):
                    at = begin + c * heads + block * 8
                    return product[at : at + 8, j * 128 : (j + 1) * 128]

                halves.append(pick(chunk, part, chunks))
            out.append([a + b for a, b in zip(*halves)])
        return out

    for key in range(0, WIN, 2):
        for j, found in enumerate(lookup(key)):
            extra = jnp.broadcast_to(mask[key + j : key + j + 1, :], (8, 128))
            for block, value in enumerate(found):
                main[pl.ds(block * 8 * WIN + key + j, 8, stride=WIN), :] = value + extra
    for row in range(0, TAIL_GROUPS, 2):
        for j, found in enumerate(lookup(WIN + row)):
            for block, value in enumerate(found):
                for g in range(8):
                    key = (row + j) * 8 + g
                    moved = pltpu.roll(value, 128 - TAIL * g, 1) if g else value
                    extra = jnp.broadcast_to(mask_tail[key : key + 1, :], (8, 128))
                    tail[pl.ds(block * 8 * WIN + key, 8, stride=WIN), :] = moved + extra


def window_bias(table, places):
    heads, entries = table.shape
    whole = (entries + 255) // 256
    return pl.pallas_call(
        bias_kernel,
        out_shape=[shape((heads * WIN, 128), f32)] * 2,
        scratch_shapes=[
            pltpu.VMEM((2 * whole * heads, 256), f32),
            pltpu.VMEM((heads, (entries + 127) // 128 * 128), f32),
        ],
        compiler_params=params(),
        cost_estimate=cost(10**10, 2 * 10**7),
        name="bias",
    )(table, *places)


def row_mean(values):
    return jnp.mean(values, axis=-1, keepdims=True)


def unit_rows(data):
    center = data - row_mean(data)
    scale = lax.rsqrt(row_mean(center * center) + epsilon)
    return center * scale, scale


def stacked(block):
    lane = lax.broadcasted_iota(jnp.int32, (1, 128), 1) // HEAD
    return jnp.concatenate(
        [jnp.where(lane == h, block, jnp.zeros((), block.dtype)) for h in range(GROUP)], axis=0
    )


def lanes_of(parts):
    lane = lax.broadcasted_iota(jnp.int32, (1, 128), 1) // HEAD
    out = parts[0]
    for h in range(1, GROUP):
        out = jnp.where(lane == h, parts[h], out)
    return out


def forward_kernel(
    own, first, second, third, packed, output, gain, main, tail,
    weights, triple, keys_t, residual, tokens,
    gathered, values_t, heads_t,
):
    width = own.shape[-1]
    upper = lax.axis_index("lev") == 1
    a, b = first[...].astype(f32)[:QUAD], second[...].astype(f32)
    lon = third[...].astype(f32)[:QUAD]
    for quad, piece in enumerate((own[...].astype(f32), jnp.where(upper, a, b), lon, jnp.where(upper, b, a))):
        gathered[quad * QUAD : (quad + 1) * QUAD, :] = piece
    data = gathered[...]
    tokens[...] = data.astype(bf16)
    unit, _ = unit_rows(data)
    normed = (unit * gain[...].reshape(1, -1)).astype(bf16)
    triple[...] = mxu(normed, packed[...]).astype(bf16)
    keys_t[...] = triple[:, width : 2 * width].astype(f32).T.astype(bf16)
    values_t[...] = triple[:, 2 * width :].astype(f32).T.astype(bf16)
    for g in range(width // 128):
        query = triple[:, g * 128 : (g + 1) * 128]
        key = triple[:, width + g * 128 : width + (g + 1) * 128]
        product = mxu(stacked(key), query, NT) * HEAD ** (-0.5)
        for h in range(GROUP):
            head = g * GROUP + h
            at = slice(head * WIN, (head + 1) * WIN)
            bias = jnp.concatenate((main[at, :], tail[at, :TAIL]), axis=1)
            scores = product[h * WIN : (h + 1) * WIN] + bias
            raised = jnp.exp(scores - jnp.max(scores, axis=0, keepdims=True))
            share = (raised * (1.0 / jnp.sum(raised, axis=0, keepdims=True))).astype(bf16)
            weights[at, :] = share
            here = slice(head * HEAD, (head + 1) * HEAD)
            heads_t[here, :] = mxu(values_t[here, :], share)
    heads = heads_t[...].T.astype(bf16)
    attended = mxu(heads, output[...]).astype(bf16)
    residual[...] = (data + attended.astype(f32)).astype(bf16)


def forward(pieces, packed, output, gain, main, tail):
    width = output.shape[0]
    return pl.pallas_call(
        forward_kernel,
        out_shape=[
            shape((HEADS * WIN, WIN), bf16),
            shape((WIN, 3 * width), bf16),
            shape((width, WIN), bf16),
            shape((WIN, width), bf16),
            shape((WIN, width), bf16),
        ],
        scratch_shapes=[
            pltpu.VMEM((WIN, width), f32),
            pltpu.VMEM((width, WIN), bf16),
            pltpu.VMEM((width, WIN), f32),
        ],
        compiler_params=params(),
        cost_estimate=cost(10**10, 2 * 10**7),
        name="forward",
    )(*pieces, packed, output, gain, main, tail)


def gain_rows(gain, out):
    width = out.shape[-1]
    for quad in range(4):
        for row in range(HALF_LAT):
            odd = 1 - (row + (quad & 1) * HALF_LAT) % 2
            for side in range(2):
                block = side * 2 + odd
                at = token_row(quad, row, side, 0)
                factor = gain[:, block * width : (block + 1) * width]
                out[at : at + CELLS, :] = jnp.broadcast_to(factor, (CELLS, width))


def cell_number(places):
    row, column, level, right = places
    band = lax.shift_right_logical(row + 1, 1)
    return (band * HALF_LON + lax.shift_right_logical(column, 1)) * LEVELS + level


def split_row(places):
    return (places[0] == 0) | (places[0] == WLAT - 1)


def columns_of(parts):
    lane = lax.broadcasted_iota(jnp.int32, (1, 128), 1)
    out = jnp.zeros((WIN, 128), f32)
    for i, part in enumerate(parts):
        out = jnp.where(lane == i, part, out)
    return out


def moments_kernel(residual, kept, first, third, fourth, fifth, gain, scaled, moments, sent, same_here, same_next, other_here, other_next, factors):
    width = residual.shape[-1]
    upper = lax.axis_index("lev") == 1
    own, a, b = kept[...].astype(f32), fourth[...].astype(f32), fifth[...].astype(f32)
    below, right = first[...].astype(f32)[QUAD:], third[...].astype(f32)[QUAD:]
    gain_rows(gain, factors)
    for quad, part in enumerate((
        jnp.where(upper, own, a),
        jnp.where(upper, below, b),
        jnp.where(upper, a, right),
        jnp.where(upper, b, below),
    )):
        scaled[quad * QUAD : (quad + 1) * QUAD, :] = part
    grad = scaled[...] * factors[...]
    scaled[...] = grad
    data = residual[...].astype(f32)
    down = token_places((WIN, 1), 0)
    grouping = jnp.where(cell_number(down) == cell_number(token_places((1, WIN), 1)), 1.0, 0.0).astype(f32)
    inverse = jnp.where(split_row(down), 1 / (2 * width), 1 / (4 * width)).astype(f32)
    total = jnp.sum(data, axis=-1, keepdims=True)
    middle = exact(grouping, jnp.broadcast_to(total, (WIN, 128)))[:, 0:1] * inverse
    center = data - middle
    sums = columns_of((
        jnp.sum(center * center, axis=-1, keepdims=True),
        jnp.sum(grad, axis=-1, keepdims=True),
        jnp.sum(grad * center, axis=-1, keepdims=True),
    ))
    sums = exact(grouping, sums)
    lane = lax.broadcasted_iota(jnp.int32, (1, 128), 1)
    sums = jnp.where(lane == 3, middle, sums)
    moments[...] = sums
    starts = [token_row(quad, row, 0, 0) for quad, row in ((0, 0), (2, 0), (1, HALF_LAT - 1), (3, HALF_LAT - 1))]
    sent[...] = jnp.concatenate([sums[at : at + CELLS] for at in starts], axis=0)
    scale = lax.rsqrt(sums[:, 0:1] * (1 / (4 * width)) + epsilon)
    out = jnp.where(split_row(down), data, center * scale * factors[...])
    parts = [quadrant(out, quad) for quad in range(4)]
    same_here[...] = jnp.where(upper, parts[0], parts[2]).astype(bf16)
    same_next[...] = jnp.where(upper, parts[1], parts[3]).astype(bf16)
    other_here[...] = jnp.where(upper, parts[2], parts[0]).astype(bf16)
    other_next[...] = jnp.where(upper, parts[3], parts[1]).astype(bf16)


def cell_moments(residual, pieces, gain):
    width = residual.shape[-1]
    return pl.pallas_call(
        moments_kernel,
        out_shape=[shape((WIN, width), f32), shape((WIN, 128), f32), shape((4 * CELLS, 128), f32)]
        + [shape((QUAD, width), bf16)] * 4,
        scratch_shapes=[pltpu.VMEM((WIN, width), f32)],
        compiler_params=params(),
        cost_estimate=cost(10**8, 10**6),
        name="moments",
    )(residual, *pieces, gain)


def merge_kernel(residual, scaled, moments, before, after, grad):
    width = residual.shape[-1]
    down = token_places((WIN, 1), 0)
    shared = split_row(down)
    there = jnp.concatenate((before[2 * CELLS :], after[: 2 * CELLS]), axis=0)
    none = jnp.zeros((QUAD - 2 * CELLS, there.shape[1]), f32)
    parts = [there[i * CELLS : (i + 1) * CELLS] for i in range(4)]
    theirs = jnp.concatenate(
        (parts[0], parts[0], none, none, parts[2], parts[2], parts[1], parts[1], none, none, parts[3], parts[3]), axis=0
    )
    mine = moments[...]
    full = 4.0 * width
    middle = jnp.where(shared, 0.5 * (mine[:, 3:4] + theirs[:, 3:4]), mine[:, 3:4])
    gap = theirs[:, 3:4] - mine[:, 3:4]
    square = jnp.where(shared, mine[:, 0:1] + theirs[:, 0:1] + gap * gap * width, mine[:, 0:1])
    scale = lax.rsqrt(square / full + epsilon)
    grad_sum = jnp.where(shared, mine[:, 1:2] + theirs[:, 1:2], mine[:, 1:2])
    cross = jnp.where(
        shared,
        mine[:, 2:3] + (mine[:, 3:4] - middle) * mine[:, 1:2]
        + theirs[:, 2:3] + (theirs[:, 3:4] - middle) * theirs[:, 1:2],
        mine[:, 2:3],
    )
    unit = (residual[...].astype(f32) - middle) * scale
    grad[...] = (scale * (scaled[...] - grad_sum / full - unit * (cross * scale / full))).astype(bf16)


def merge_back(residual, scaled, moments, before, after):
    return pl.pallas_call(
        merge_kernel,
        out_shape=shape(residual.shape, bf16),
        compiler_params=params(),
        cost_estimate=cost(10**8, 10**6),
        name="merge",
    )(residual, scaled, moments, before, after)


def backward_kernel(grad, weights, triple, keys_t, output, joined, queries_t):
    width = grad.shape[-1]
    upstream = grad[...]
    grad_heads = mxu(upstream, output[...], NT).astype(bf16)
    for g in range(width // 128):
        here = slice(g * 128, (g + 1) * 128)
        query = triple[:, g * 128 : (g + 1) * 128]
        value = triple[:, 2 * width + g * 128 : 2 * width + (g + 1) * 128]
        arriving = grad_heads[:, here]
        product = mxu(stacked(value), arriving, NT)
        shares = weights[g * GROUP * WIN : (g + 1) * GROUP * WIN, :]
        grad_value = mxu(shares, arriving)
        slopes = []
        for h in range(GROUP):
            head = g * GROUP + h
            share = shares[h * WIN : (h + 1) * WIN].astype(f32)
            change = product[h * WIN : (h + 1) * WIN]
            level = jnp.sum(share * change, axis=0, keepdims=True)
            slope = (share * (change - level) * HEAD ** (-0.5)).astype(bf16)
            at = slice(head * HEAD, (head + 1) * HEAD)
            queries_t[at, :] = mxu(keys_t[at, :], slope)
            slopes.append(slope)
        grad_key = mxu(jnp.concatenate(slopes, axis=0), query)
        split = [slice(h * WIN, (h + 1) * WIN) for h in range(GROUP)]
        joined[:, width + g * 128 : width + (g + 1) * 128] = lanes_of([grad_key[s] for s in split]).astype(bf16)
        joined[:, 2 * width + g * 128 : 2 * width + (g + 1) * 128] = lanes_of(
            [grad_value[s] for s in split]
        ).astype(bf16)
    joined[:, :width] = queries_t[...].T.astype(bf16)


def backward(grad, weights, triple, keys_t, output):
    width = grad.shape[-1]
    return pl.pallas_call(
        backward_kernel,
        out_shape=shape((WIN, 3 * width), bf16),
        scratch_shapes=[pltpu.VMEM((width, WIN), f32)],
        compiler_params=params(),
        cost_estimate=cost(10**10, 2 * 10**7),
        name="backward",
    )(grad, weights, triple, keys_t, output)


def finish_kernel(grad, joined, tokens, packed, gain, own, lat, lon, both):
    grad_inputs = mxu(joined[...], packed[...], NT).astype(bf16)
    unit, scale = unit_rows(tokens[...].astype(f32))
    scaled = grad_inputs.astype(f32) * gain[...].reshape(1, -1)
    out = grad[...].astype(f32) + scale * (scaled - row_mean(scaled) - unit * row_mean(scaled * unit))
    for quad, piece in enumerate((own, lat, lon, both)):
        piece[...] = quadrant(out, quad).astype(bf16)


def finish(grad, joined, tokens, packed, gain):
    width = grad.shape[-1]
    return pl.pallas_call(
        finish_kernel,
        out_shape=[shape((QUAD, width), bf16)] * 4,
        compiler_params=params(),
        cost_estimate=cost(10**10, 2 * 10**6),
        name="finish",
    )(grad, joined, tokens, packed, gain)


def token_kernel(own, lat, lon, both, tokens):
    quads = [piece[...].astype(f32) for piece in (own, lat, lon, both)]
    for line in range(WLAT):
        for column in range(WLON):
            quad = (0 if line >= HALF_LAT else 1) + (0 if column >= HALF_LON else 2)
            inner = column % HALF_LON
            at = token_row(0, line % HALF_LAT, inner % 2, inner // 2)
            tokens[line, column] = quads[quad][at : at + LEVELS].astype(bf16)


def unpack_tokens(*pieces):
    width = pieces[0].shape[-1]
    return pl.pallas_call(
        token_kernel,
        out_shape=shape((WLAT, WLON, LEVELS, width), bf16),
        compiler_params=params(),
        name="unpack_tokens",
    )(*pieces)


def cell_kernel(same_here, same_next, other_here, other_next, gain, merged):
    width = same_here.shape[-1]
    upper = lax.axis_index("lev") == 1
    same = (same_here[...].astype(f32), same_next[...].astype(f32))
    other = (other_here[...].astype(f32), other_next[...].astype(f32))
    levels = (
        [jnp.where(upper, b, a) for a, b in zip(same, other)],
        [jnp.where(upper, a, b) for a, b in zip(same, other)],
    )
    blocks = {}
    for row, odd, below, inner in cell_places():
        for side in range(2):
            at = token_row(0, inner, side, 0)
            for part in range(2):
                blocks[row, side * 2 + odd, part] = levels[part][below][at : at + CELLS]
    for part in range(2):
        parts = [blocks[1, block, part] for block in range(4)]
        mean = sum(jnp.sum(x, axis=-1, keepdims=True) for x in parts) * (1 / (4 * width))
        parts = [x - mean for x in parts]
        spread = sum(jnp.sum(x * x, axis=-1, keepdims=True) for x in parts) * (1 / (4 * width))
        scale = lax.rsqrt(spread + epsilon)
        for block, x in enumerate(parts):
            blocks[1, block, part] = x * scale * gain[:, block * width : (block + 1) * width]
    for row in range(HALF_LAT):
        for pair in range(PAIRS):
            here = slice(pair * LEVELS, (pair + 1) * LEVELS)
            for block in range(4):
                merged[row, pair, :, block * width : (block + 1) * width] = jnp.concatenate(
                    (blocks[row, block, 0][here], blocks[row, block, 1][here]), axis=0
                ).astype(bf16)


def unpack_cells(pieces, gain):
    width = pieces[0].shape[-1]
    return pl.pallas_call(
        cell_kernel,
        out_shape=shape((HALF_LAT, PAIRS, 2 * LEVELS, 4 * width), bf16),
        compiler_params=params(),
        cost_estimate=cost(10**9, 10**6),
        name="unpack_cells",
    )(*pieces, gain)


def routes(sizes, target):
    lons, lats, levs = sizes

    def number(i, a, k):
        return ((i % lons) * lats + a % lats) * levs + k % levs

    return [
        (number(i, a, k), number(*target(i, a, k)))
        for i in range(lons)
        for a in range(lats)
        for k in range(levs)
    ]


def send(block, sizes, target, back=False):
    pairs = routes(sizes, target)
    if back:
        pairs = [(b, a) for a, b in pairs]
    return lax.ppermute(block, ("lon", "lat", "lev"), pairs)


FIRST = lambda i, a, k: (i - (1 - k), a - 1, k)
SECOND = lambda i, a, k: (i - k, a - 1, k)
THIRD = lambda i, a, k: (i - 1, a, k)
FOURTH = lambda i, a, k: (i - (1 - k), a, 1 - k)
FIFTH = lambda i, a, k: (i - (1 - k), a - 1, 1 - k)
LAT = lambda i, a, k: (i, a - 1, k)
LON = lambda i, a, k: (i - 1, a, k)
BOTH = lambda i, a, k: (i - 1, a - 1, k)
HERE = lambda i, a, k: (i - (1 - k), a, k)


def per_device(
    sizes,
    tokens,
    packed_weight,
    output_weight,
    norm_gain,
    merge_gain,
    bias_table,
    bias_index,
    row_labels,
    column_valid,
    merged_grad,
):
    own, first, second, third, kept, fourth, fifth, table, index = pack_pieces(
        tokens.transpose(1, 2, 0, 3), merged_grad.transpose(1, 2, 0, 3), bias_table, bias_index
    )
    first = send(first, sizes, FIRST)
    second = send(second, sizes, SECOND)
    third = send(third, sizes, THIRD)
    places = window_index(index, row_labels, column_valid)
    fourth, fifth, *places = lax.optimization_barrier((fourth, fifth, *places))
    fourth = send(fourth, sizes, FOURTH)
    fifth = send(fifth, sizes, FIFTH)
    main, tail = window_bias(table, places)
    cell_gain = merge_gain.reshape(1, -1)
    weights, triple, keys_t, residual, data = forward(
        (own, first, second, third), packed_weight, output_weight, norm_gain, main, tail
    )
    scaled, moments, sent, *merged = cell_moments(
        residual, (kept, first, third, fourth, fifth), cell_gain
    )
    before = send(sent, sizes, lambda i, a, k: (i, a + 1, k))
    after = before if sizes[1] == 2 else send(sent, sizes, lambda i, a, k: (i, a - 1, k))
    same_here, same_next, other_here, other_next = merged
    other_next = send(other_next, sizes, FIFTH, True)
    same_next = send(same_next, sizes, FIRST, True)
    other_here = send(other_here, sizes, FOURTH, True)
    same_here = send(same_here, sizes, HERE, True)
    grad = merge_back(residual, scaled, moments, before, after)
    joined = backward(grad, weights, triple, keys_t, output_weight)
    own, lat, lon, both = finish(grad, joined, data, packed_weight, norm_gain)
    other_next, same_next, lat, both, lon = lax.optimization_barrier((other_next, same_next, lat, both, lon))
    lat = send(lat, sizes, LAT, True)
    both = send(both, sizes, BOTH, True)
    lon = send(lon, sizes, LON, True)
    merged = unpack_cells((same_here, same_next, other_here, other_next), cell_gain)
    merged, lat, both, lon = lax.optimization_barrier((merged, lat, both, lon))
    grads = unpack_tokens(own, lat, lon, both)
    return merged.transpose(2, 0, 1, 3), grads.transpose(2, 0, 1, 3)


def solution(mesh):
    sizes = tuple(mesh.shape[name] for name in ("lon", "lat", "lev"))
    placed = (
        P("lev", "lat", "lon", None),
        P(),
        P(),
        P(),
        P(),
        P("lev", "lat", None, None),
        P(),
        P("lat"),
        P(),
        P(None, "lat", ("lon", "lev"), None),
    )
    return jax.shard_map(
        functools.partial(per_device, sizes),
        mesh=mesh,
        in_specs=placed,
        out_specs=(P(None, "lat", ("lon", "lev"), None), P("lev", "lat", "lon", None)),
        check_vma=False,
    )
```
